256 devices in a mesh: blk: 16 (over z, y_lo), img: 16 (over x, y_hi, core).
Axes of the slice: x: 4, y: 4 (y_hi: 2, y_lo: 2; y = y_hi * 2 + y_lo), z: 8, core: 2. Of those that a mesh axis runs over, the one named last changes fastest.
Arguments:
- hidden: bfloat16 [16, 2048, 1536], P('img', 'blk'), may hold values from -6 to 6
- text_hidden: bfloat16 [16, 154, 1536], P('img'), may hold values from -6 to 6
- latent: float32 [16, 64, 2048], P('img', 'blk'), may hold values from -6 to 6
- image_mod: float32 [16, 6, 1536], P('img'), may hold values from -10 to 10
- text_mod: float32 [16, 2, 1536], P('img'), may hold values from -3 to 3
- final_mod: float32 [16, 2, 1536], P('img'), may hold values from -3 to 3
- counts: int32 [16], P('img'), may hold values from 512 to 2048, as said below
- step_index: int32 [16], P('img'), may hold values from 0 to 7
- qkv_weight: bfloat16 [1536, 2304], P(None, 'img'), may hold values from -0.21875 to 0.21875
- text_weight: bfloat16 [1536, 1536], replicated, may hold values from -0.21875 to 0.21875
- out_weight: bfloat16 [768, 1536], replicated, may hold values from -0.21875 to 0.21875
- mlp_in_weight: bfloat16 [1536, 3072], P(None, 'img'), may hold values from -0.15625 to 0.15625
- mlp_out_weight: bfloat16 [3072, 1536], P(None, 'img'), may hold values from -0.109375 to 0.109375
- final_weight: bfloat16 [1536, 64], replicated, may hold values from -0.15625 to 0.15625
- conv_weight: bfloat16 [144, 512], replicated, may hold values from -0.5 to 0.5
- conv_bias: float32 [512], replicated, may hold values from -3 to 3
Outputs:
- velocity: float32 [16, 64, 2048], P('img', 'blk')
- next_latent: float32 [16, 64, 2048], P('img', 'blk')
- features: bfloat16 [16, 64, 128, 512], P('img', 'blk')
The draws below stay inside these ranges and needn't reach their ends.
Inputs may be any that keep to these rules, and one draw needn't show every extreme that they name: `counts`: each count is a multiple of 128; in every draw one image has all 2048 patches.
All inputs are finite; a program needn't handle non-finite values.
Results may differ from the reference program's by a relative error of at most 0.015.
The reference program's roundings to bfloat16 on the way count: a program that leaves them out, or rounds other values in their place, can miss the bound.
Values may be sent and summed in bfloat16 or wider, within the bound.
No kernel may reach another device: no remote copies, remote signals or barrier semaphores. Data moves between devices by JAX's collectives and lax.ppermute only.
A program may use at most 128 MiB of HBM per device.

```python
import math
import jax
import jax.numpy as jnp
from jax import lax

D = 1536
HEAD = 64
CH = 16
COUT = 512
HEADS = 12
FFW = 3072
TEXT = 154
W_P = 64
STEPS = 8
TOK_DEV = 128
BLOCKS = 16
PATCHES = 2048
IMAGES = 16
LROWS = 64
LWIDE = 2048


def draw_image_mod(key, part):
    shift_key = jax.random.fold_in(key, 0)
    scale_key = jax.random.fold_in(key, 1)
    gate_key = jax.random.fold_in(key, 2)
    shift_two = jax.random.fold_in(key, 4)
    scale_two = jax.random.fold_in(key, 5)
    gate_two = jax.random.fold_in(key, 6)
    row_shape = (IMAGES, 1, D)
    shifts = 0.5 * jnp.clip(jax.random.normal(shift_key, row_shape, jnp.float32), -4.0, 4.0)
    scales = 0.3 * jnp.clip(jax.random.normal(scale_key, row_shape, jnp.float32), -4.0, 4.0)
    gates = jnp.clip(jax.random.normal(gate_key, row_shape, jnp.float32), -4.0, 4.0)
    shifts_mlp = 0.5 * jnp.clip(jax.random.normal(shift_two, row_shape, jnp.float32), -4.0, 4.0)
    scales_mlp = 0.3 * jnp.clip(jax.random.normal(scale_two, row_shape, jnp.float32), -4.0, 4.0)
    gates_mlp = jnp.clip(jax.random.normal(gate_two, row_shape, jnp.float32), -4.0, 4.0)
    return jnp.concatenate([shifts, scales, gates, shifts_mlp, scales_mlp, gates_mlp], axis=1).astype(jnp.float32)


def draw_counts(key, part):
    size_key, full_key = jax.random.split(key)
    fewest = max(1, BLOCKS // 4)
    blocks = jax.random.randint(size_key, (IMAGES,), fewest, BLOCKS + 1)
    chosen = jax.random.randint(full_key, (), 0, IMAGES)
    blocks = jnp.where(jnp.arange(IMAGES) == chosen, BLOCKS, blocks)
    return (blocks * TOK_DEV).astype(jnp.int32)


def place_ends(result, stream_key, least, top_value):
    index_at = [jax.random.randint(jax.random.fold_in(stream_key, axis), (), 0, length) for axis, length in enumerate(result.shape)]
    main_axis = result.shape.index(max(result.shape))
    beside = index_at[:main_axis] + [(index_at[main_axis] + 1) % result.shape[main_axis]] + index_at[main_axis + 1:]
    return result.at[tuple(index_at)].set(least).at[tuple(beside)].set(top_value)


def shard_levels(rng, extent, shards, least, high):
    factor_of = 1.0
    for dim, parts in shards:
        heights = jax.random.uniform(jax.random.fold_in(jax.random.fold_in(rng, 6), dim), (parts,), jnp.float32, least / len(shards), high / len(shards))
        factor_of = factor_of * jnp.repeat(jnp.exp(heights), extent[dim] // parts).reshape((-1,) + (1,) * (len(extent) - 1 - dim))
    return factor_of


def gaussian(own_key, extent, width, bound, shards=(), kind=jnp.bfloat16):
    level = shard_levels(own_key, extent, shards, -0.22, 0.18) if shards else 1.0
    array = jax.random.normal(own_key, extent, jnp.float32) * width * level
    return jnp.minimum(jnp.maximum(array, -bound), bound).astype(kind)


def setup_inputs(seed: int = 0) -> dict:
    key_list = jax.random.split(jax.random.key(seed), 17)
    return {
        "hidden": gaussian(key_list[0], (IMAGES, PATCHES, D), 1.0, 6.0, ((0, 16), (1, 16))),
        "text_hidden": gaussian(key_list[1], (IMAGES, TEXT, D), 1.0, 6.0, ((0, 16),)),
        "latent": gaussian(key_list[2], (IMAGES, LROWS, LWIDE), 1.0, 6.0, ((0, 16), (1, 16)), jnp.float32),
        "image_mod": draw_image_mod(jax.random.fold_in(key_list[16], 71), 0),
        "text_mod": gaussian(key_list[4], (IMAGES, 2, D), 0.3, 3.0, ((0, 16),), jnp.float32),
        "final_mod": gaussian(key_list[5], (IMAGES, 2, D), 0.3, 3.0, ((0, 16),), jnp.float32),
        "counts": draw_counts(jax.random.fold_in(key_list[16], 71), 0),
        "step_index": place_ends(jax.random.randint(key_list[7], (IMAGES,), 0, STEPS), jax.random.fold_in(key_list[7], 1), 0, STEPS - 1).astype(jnp.int32),
        "qkv_weight": gaussian(key_list[8], (D, 3 * HEADS * HEAD), (D // 2) ** -0.5, 0.21875, ((1, 16),)),
        "text_weight": gaussian(key_list[9], (D, 2 * HEADS * HEAD), (D // 2) ** -0.5, 0.21875),
        "out_weight": gaussian(key_list[10], (HEADS * HEAD, D), (HEADS * HEAD) ** -0.5, 0.21875),
        "mlp_in_weight": gaussian(key_list[11], (D, FFW), D ** -0.5, 0.15625, ((1, 16),)),
        "mlp_out_weight": gaussian(key_list[12], (FFW, D), FFW ** -0.5, 0.109375, ((1, 16),)),
        "final_weight": gaussian(key_list[13], (D, 4 * CH), D ** -0.5, 0.15625),
        "conv_weight": gaussian(key_list[14], (9 * CH, COUT), (9 * CH) ** -0.5, 0.5),
        "conv_bias": gaussian(key_list[15], (COUT,), 0.5, 3.0, (), jnp.float32),
    }


norm_eps = 1e-06
sigma_shift = 3.0
vae_scale = 1.5305
vae_offset = 0.0609
masked_score = -1e+30

def modulate(inputs, shift_row, scale_row):
    values = inputs.astype(jnp.float32)
    center = lax.optimization_barrier(jnp.mean(values, axis=-1, keepdims=True))
    spread = lax.optimization_barrier(jnp.mean(jnp.square(values - center), axis=-1, keepdims=True))
    normed = (values - center) * lax.rsqrt(spread + norm_eps)
    return (normed * (1.0 + scale_row) + shift_row).astype(jnp.bfloat16)

def plan(step_value):
    remain = 1.0 - step_value / STEPS
    return sigma_shift * remain / (1.0 + (sigma_shift - 1.0) * remain)

def reference(hidden, text_hidden, latent, image_mod, text_mod, final_mod, counts, step_index, qkv_weight, text_weight, out_weight, mlp_in_weight, mlp_out_weight, final_weight, conv_weight, conv_bias):
    width_attn = HEADS * HEAD
    query_rows = math.gcd(PATCHES, 512)

    def one_image(packed):
        image_states, text_states, lat_in, image_terms, text_terms, final_terms, patch_count, step_now = packed
        image_in = modulate(image_states, image_terms[0], image_terms[1])
        qkv_all = jnp.dot(image_in, qkv_weight, preferred_element_type=jnp.float32).astype(jnp.bfloat16)
        text_in = modulate(text_states, text_terms[0], text_terms[1])
        text_kv = jnp.dot(text_in, text_weight, preferred_element_type=jnp.float32).astype(jnp.bfloat16)
        key_rows = jnp.concatenate([text_kv[:, :width_attn], qkv_all[:, width_attn:2 * width_attn]], axis=0)
        value_rows = jnp.concatenate([text_kv[:, width_attn:], qkv_all[:, 2 * width_attn:]], axis=0)
        key_heads = key_rows.astype(jnp.float32).reshape(-1, HEADS, HEAD)
        value_heads = value_rows.astype(jnp.float32).reshape(-1, HEADS, HEAD)
        key_valid = jnp.concatenate([jnp.ones((TEXT,), dtype=bool), jnp.arange(PATCHES) < patch_count])
        query_blocks = qkv_all[:, :width_attn].astype(jnp.float32).reshape(PATCHES // query_rows, query_rows, HEADS, HEAD)

        def attend(query_block):
            scores = jnp.einsum('qhd,khd->hqk', query_block, key_heads, precision=lax.Precision.HIGHEST) * 0.125
            scores = jnp.where(key_valid[None, None, :], scores, masked_score)
            row_max = lax.optimization_barrier(jnp.max(scores, axis=-1, keepdims=True))
            numer = jnp.exp(scores - row_max)
            total = lax.optimization_barrier(jnp.sum(numer, axis=-1))
            rounded = lax.optimization_barrier(numer.astype(jnp.bfloat16)).astype(jnp.float32)
            mixed = jnp.einsum('hqk,khd->hqd', rounded, value_heads, precision=lax.Precision.HIGHEST) / total[:, :, None]
            return mixed.transpose(1, 0, 2).reshape(query_rows, width_attn).astype(jnp.bfloat16)
        attended = lax.map(attend, query_blocks).reshape(PATCHES, width_attn)
        projected = jnp.dot(attended, out_weight, preferred_element_type=jnp.float32)
        updated = image_states.astype(jnp.float32) + image_terms[2] * projected
        mlp_in = modulate(updated, image_terms[3], image_terms[4])
        mlp_hidden = jax.nn.gelu(jnp.dot(mlp_in, mlp_in_weight, preferred_element_type=jnp.float32), approximate=True).astype(jnp.bfloat16)
        mlp_out = jnp.dot(mlp_hidden, mlp_out_weight, preferred_element_type=jnp.float32)
        refined = updated + image_terms[5] * mlp_out
        final_in = modulate(refined, final_terms[0], final_terms[1])
        predicted = jnp.dot(final_in, final_weight, preferred_element_type=jnp.float32)
        vel_lat = predicted.reshape(PATCHES // W_P, W_P, 2, 2, CH).transpose(0, 2, 1, 3, 4).reshape(LROWS, LWIDE)
        live_rows = (jnp.arange(LROWS) < 2 * (patch_count // W_P))[:, None]
        velocity = jnp.where(live_rows, vel_lat, 0.0)
        step_value = step_now.astype(jnp.float32)
        sigma_gap = plan(step_value + 1.0) - plan(step_value)
        next_lat = jnp.where(live_rows, lat_in + sigma_gap * vel_lat, 0.0)
        scaled = jnp.where(live_rows, next_lat / vae_scale + vae_offset, 0.0).astype(jnp.bfloat16)
        padded_grid = jnp.pad(scaled.reshape(LROWS, 2 * W_P, CH), ((1, 1), (1, 1), (0, 0)))
        columns = jnp.concatenate([padded_grid[row_off:row_off + LROWS, col_off:col_off + 2 * W_P, :] for row_off in range(3) for col_off in range(3)], axis=-1).reshape(LROWS * 2 * W_P, 9 * CH)
        feature = jnp.dot(columns, conv_weight, preferred_element_type=jnp.float32) + conv_bias
        feature = jnp.where(live_rows[:, :, None], feature.reshape(LROWS, 2 * W_P, COUT), 0.0).astype(jnp.bfloat16)
        return (velocity, next_lat, feature)
    return lax.map(one_image, (hidden, text_hidden, latent, image_mod, text_mod, final_mod, counts, step_index))
```

```python
import jax
import jax.numpy as jnp
from jax import lax
from jax.experimental import pallas as pl
from jax.experimental.pallas import tpu as pltpu
from jax.sharding import PartitionSpec as P

HEAD = 64
CH = 16
HEADS = 12
W_P = 64
STEPS = 8

norm_eps = 1e-06
sigma_shift = 3.0
vae_scale = 1.5305
vae_offset = 0.0609
masked_score = -1e30

F32 = jnp.float32
BF16 = jnp.bfloat16


def modulate(inputs, shift_row, scale_row):
    values = inputs.astype(F32)
    center = jnp.mean(values, axis=-1, keepdims=True)
    spread = jnp.mean(jnp.square(values - center), axis=-1, keepdims=True)
    normed = (values - center) * lax.rsqrt(spread + norm_eps)
    return (normed * (1.0 + scale_row) + shift_row).astype(BF16)


def plan(step_value):
    remain = 1.0 - step_value / STEPS
    return sigma_shift * remain / (1.0 + (sigma_shift - 1.0) * remain)


def swap(x, axis, bits):
    return lax.ppermute(x, axis, [(i, i ^ bits) for i in range(lax.axis_size(axis))])


def vmem_specs(count):
    return [pl.BlockSpec(memory_space=pltpu.VMEM)] * count


OFFSETS = ((0, 0), (-1, 0), (1, 0), (0, 1), (2, 0), (-1, 1), (1, 1), (2, 1))


def ring(x, axis, step):
    size = lax.axis_size(axis)
    return lax.ppermute(x, axis, [(i, (i + step) % size) for i in range(size)])


def ring_first(x):
    return ring(x, "img", 4), ring(x, "img", -4), swap(x, "img", 2)


def ring_second(left, right, across):
    half = left.shape[0] // 2
    return (
        ring(left[:half], "img", 4),
        ring(right[half:], "img", -4),
        ring(across, "img", 4),
        ring(across, "img", -4),
    )


def ring_third(low, high):
    far = jnp.concatenate([low, high], axis=0)
    return far, swap(far, "img", 2)


def place_of(chip, k):
    dx, dy = OFFSETS[k]
    column = jnp.bitwise_and(chip // 2 + dx + 4, 3)
    return 2 * column + jnp.bitwise_xor(jnp.bitwise_and(chip, 1), dy)


def qkv_body(chip_ref, own_x, peer_x, *refs):
    weights, (own_out, peer_out) = refs[:-2], refs[-2:]
    rows = own_x.shape[0]
    both = jnp.concatenate([own_x[...], peer_x[...]], axis=0)
    for k, weight in enumerate(weights):
        part = lax.dot_general(
            weight[...], both, (((1,), (1,)), ((), ())), preferred_element_type=F32
        ).astype(BF16)
        place = place_of(chip_ref[0], k)
        own_out[place] = part[:, :rows]
        peer_out[place] = part[:, rows:]


def project_qkv(chip, own_x, peer_x, weights):
    cols, rows = weights[0].shape[0], own_x.shape[0]
    shape = jax.ShapeDtypeStruct((len(weights), cols, rows), BF16)
    flops = 4 * len(weights) * cols * rows * own_x.shape[1]
    return pl.pallas_call(
        qkv_body,
        out_shape=(shape, shape),
        in_specs=[pl.BlockSpec(memory_space=pltpu.SMEM)] + vmem_specs(2 + len(weights)),
        out_specs=tuple(vmem_specs(2)),
        compiler_params=pltpu.CompilerParams(vmem_limit_bytes=32 << 20),
        cost_estimate=pl.CostEstimate(flops=flops, bytes_accessed=5 << 20, transcendentals=0),
        name="project_qkv",
    )(chip, own_x, peer_x, *weights)


def attend_body(count_ref, parts, text, out, keys, values, queries):
    blocks, _, rows = parts.shape
    text_blocks = text.shape[1] // rows
    text_len = 154
    tile = 2 * rows
    lane = lax.broadcasted_iota(jnp.int32, (8, rows), 1)
    row = lax.broadcasted_iota(jnp.int32, (8, rows), 0)
    top = row == 0
    zeros = jnp.zeros((HEAD - 8, rows), F32)

    def place_keys(index, key_part, limit):
        bias = jnp.where(jnp.logical_and(top, lane >= limit), masked_score, 0.0)
        full = jnp.concatenate([key_part.astype(F32), bias, zeros], axis=0)
        keys[pl.ds(index * rows, rows), :] = full.T.astype(BF16)

    ones = jnp.concatenate([jnp.where(top, 1.0, 0.0).astype(F32), zeros], axis=0)
    for b in range(blocks):
        part = parts[b]
        place_keys(b, part[HEAD : 2 * HEAD], count_ref[0] - b * rows)
        values[:, b * rows : (b + 1) * rows] = part[2 * HEAD :]
        scaled = part[:HEAD].astype(F32) * 0.125
        queries[:, b * rows : (b + 1) * rows] = jnp.concatenate([scaled, ones], axis=0).astype(BF16)
    for t in range(text_blocks):
        cols = slice(t * rows, (t + 1) * rows)
        place_keys(blocks + t, text[:HEAD, cols], text_len - t * rows)
        values[:, (blocks + t) * rows : (blocks + t + 1) * rows] = text[HEAD:, cols]

    def step(t, carry):
        first = pl.multiple_of(t * tile, tile)
        scores = jnp.dot(keys[...], queries[:, pl.ds(first, tile)], preferred_element_type=F32)
        top_score = jnp.max(scores, axis=0, keepdims=True)
        numer = jnp.exp(scores - top_score)
        total = jnp.sum(numer, axis=0, keepdims=True)
        mixed = jnp.dot(values[...], numer.astype(BF16), preferred_element_type=F32) / total
        mixed = mixed.astype(BF16)
        out[2 * t] = mixed[:, :rows]
        out[2 * t + 1] = mixed[:, rows:]
        return carry

    lax.fori_loop(0, blocks // 2, step, 0)


def attend(count, parts, text):
    blocks, _, rows = parts.shape
    keys = blocks * rows + text.shape[1]
    queries = blocks * rows
    return pl.pallas_call(
        attend_body,
        out_shape=jax.ShapeDtypeStruct((blocks, HEAD, rows), BF16),
        in_specs=[pl.BlockSpec(memory_space=pltpu.SMEM)] + vmem_specs(2),
        out_specs=vmem_specs(1)[0],
        scratch_shapes=[
            pltpu.VMEM((keys, 2 * HEAD), BF16),
            pltpu.VMEM((HEAD, keys), BF16),
            pltpu.VMEM((2 * HEAD, queries), BF16),
        ],
        compiler_params=pltpu.CompilerParams(vmem_limit_bytes=40 << 20),
        cost_estimate=pl.CostEstimate(
            flops=4 * keys * queries * HEAD, bytes_accessed=2 << 20, transcendentals=keys * queries
        ),
        name="attend",
    )(count, parts, text)


def layer_norm(values, shift_row, scale_row):
    center = jnp.mean(values, axis=-1, keepdims=True)
    spread = jnp.mean(jnp.square(values - center), axis=-1, keepdims=True)
    normed = (values - center) * lax.rsqrt(spread + norm_eps)
    return (normed * (1.0 + scale_row) + shift_row).astype(BF16)


def gelu(v):
    return 0.5 * v * (1.0 + jnp.tanh(0.7978845608028654 * (v + 0.044715 * v * v * v)))


def middle_body(mixed, hidden, mods, out_w, updated, mlp_in):
    attended = mixed[...].astype(F32).T.astype(BF16)
    projected = jnp.dot(attended, out_w[...], preferred_element_type=F32)
    now = hidden[...].astype(F32) + mods[2:3] * projected
    updated[...] = now
    mlp_in[...] = layer_norm(now, mods[3:4], mods[4:5])


def middle(mixed, hidden, mods, out_w):
    rows, width = hidden.shape
    return pl.pallas_call(
        middle_body,
        out_shape=(
            jax.ShapeDtypeStruct((rows, width), F32),
            jax.ShapeDtypeStruct((rows, width), BF16),
        ),
        in_specs=vmem_specs(4),
        out_specs=tuple(vmem_specs(2)),
        compiler_params=pltpu.CompilerParams(vmem_limit_bytes=24 << 20),
        cost_estimate=pl.CostEstimate(
            flops=2 * mixed.shape[0] * rows * width, bytes_accessed=5 << 20, transcendentals=rows
        ),
        name="middle",
    )(mixed, hidden, mods, out_w)


def first_body(chip_ref, own_x, peer_x, *refs):
    weights, out = refs[:-1], refs[-1]
    both = jnp.concatenate([own_x[...], peer_x[...]], axis=0)
    cols = out.shape[1]
    for k, weight in enumerate(weights):
        part = lax.dot_general(
            weight[:cols], both, (((1,), (1,)), ((), ())), preferred_element_type=F32
        )
        out[place_of(chip_ref[0], k)] = gelu(part).astype(BF16)


def mlp_first(chip, own_x, peer_x, weights):
    rows, width = own_x.shape
    cols = weights[0].shape[0] // 2
    count = len(weights)
    return pl.pallas_call(
        first_body,
        out_shape=jax.ShapeDtypeStruct((count, cols, 2 * rows), BF16),
        in_specs=[pl.BlockSpec(memory_space=pltpu.SMEM)] + vmem_specs(2 + count),
        out_specs=vmem_specs(1)[0],
        compiler_params=pltpu.CompilerParams(vmem_limit_bytes=32 << 20),
        cost_estimate=pl.CostEstimate(
            flops=4 * count * cols * rows * width,
            bytes_accessed=6 << 20,
            transcendentals=2 * count * cols * rows,
        ),
        name="mlp_first",
    )(chip, own_x, peer_x, *weights)


def second_body(chip_ref, core_ref, own_act, peer_act, *refs):
    weights, (own_out, peer_out), act = refs[:-3], refs[-3:-1], refs[-1]
    count, cols, tokens = own_act.shape
    core = core_ref[0]
    for c in range(count):
        start = pl.multiple_of((2 * c + core) * cols, cols)
        act[pl.ds(start, cols), :] = own_act[c]
        start = pl.multiple_of((2 * c + 1 - core) * cols, cols)
        act[pl.ds(start, cols), : tokens // 2] = peer_act[c, :, tokens // 2 :]
        act[pl.ds(start, cols), tokens // 2 :] = peer_act[c, :, : tokens // 2]
    width = weights[0].shape[1]
    half = cols // 2
    for k, weight in enumerate(weights):
        part = jnp.dot(weight[cols : cols + half], act[:width], preferred_element_type=F32)
        part += jnp.dot(weight[cols + half :], act[width:], preferred_element_type=F32)
        place = place_of(chip_ref[0], k)
        own_out[place] = part[:, : tokens // 2]
        peer_out[place] = part[:, tokens // 2 :]


def mlp_second(chip, core, own_act, peer_act, weights):
    count, cols, tokens = own_act.shape
    width = weights[0].shape[1]
    shape = jax.ShapeDtypeStruct((count, cols // 2, tokens // 2), F32)
    return pl.pallas_call(
        second_body,
        out_shape=(shape, shape),
        in_specs=[pl.BlockSpec(memory_space=pltpu.SMEM)] * 2 + vmem_specs(2 + count),
        out_specs=tuple(vmem_specs(2)),
        scratch_shapes=[pltpu.VMEM((2 * count * cols, tokens), BF16)],
        compiler_params=pltpu.CompilerParams(vmem_limit_bytes=32 << 20),
        cost_estimate=pl.CostEstimate(
            flops=2 * count * cols * tokens * width, bytes_accessed=6 << 20, transcendentals=0
        ),
        name="mlp_second",
    )(chip, core, own_act, peer_act, *weights)


def last_body(core_ref, own_part, peer_part, updated, mods, finals, final_w, predicted, mlp_t):
    count, half, _ = own_part.shape
    for source, parity in ((own_part, core_ref[0]), (peer_part, 1 - core_ref[0])):
        for c in range(count):
            start = pl.multiple_of((2 * c + parity) * half, half)
            mlp_t[pl.ds(start, half), :] = source[c]
    refined = updated[...] + mods[5:6] * mlp_t[...].T
    final_in = layer_norm(refined, finals[0:1], finals[1:2])
    predicted[...] = jnp.dot(final_in, final_w[...], preferred_element_type=F32)


def last(core, own_part, peer_part, updated, mods, finals, final_w):
    rows, width = updated.shape
    return pl.pallas_call(
        last_body,
        out_shape=jax.ShapeDtypeStruct((rows, final_w.shape[1]), F32),
        in_specs=[pl.BlockSpec(memory_space=pltpu.SMEM)] + vmem_specs(6),
        out_specs=vmem_specs(1)[0],
        scratch_shapes=[pltpu.VMEM((width, rows), F32)],
        compiler_params=pltpu.CompilerParams(vmem_limit_bytes=24 << 20),
        cost_estimate=pl.CostEstimate(
            flops=2 * rows * width * final_w.shape[1], bytes_accessed=3 << 20, transcendentals=rows
        ),
        name="last",
    )(core, own_part, peer_part, updated, mods, finals, final_w)


def padded(x, axis, width):
    size, length = lax.axis_size(axis), x.shape[0]
    up = [(i, i + 1) for i in range(size - 1)]
    down = [(j, i) for i, j in up]
    before = lax.ppermute(x[length - width :], axis, up)
    after = lax.ppermute(x[:width], axis, down)
    return jnp.concatenate([before, x, after], axis=0)


def per_device(
    hidden,
    text_hidden,
    latent,
    image_mod,
    text_mod,
    final_mod,
    counts,
    step_index,
    qkv_weight,
    text_weight,
    out_weight,
    mlp_in_weight,
    mlp_out_weight,
    final_weight,
    conv_weight,
    conv_bias,
):
    tok_rows, width = hidden.shape[1:]
    width_attn = HEADS * HEAD
    blocks = lax.axis_size("blk")
    blk, img = lax.axis_index("blk"), lax.axis_index("img")
    chip, core = img // 2, img % 2
    mods = image_mod[0]
    chip, core = chip[None], core[None]

    qkv_t = qkv_weight.T
    mlp_mine = jnp.concatenate(
        [mlp_in_weight.T, mlp_out_weight[:width].T, mlp_out_weight[width:].T], axis=0
    )
    qkv_near = ring_first(qkv_t)
    qkv_next = ring_second(*qkv_near)
    qkv_far = ring_third(*qkv_next[:2])
    qkv_pieces = [qkv_t, *qkv_near, qkv_far[0], *qkv_next[2:], qkv_far[1]]

    mlp_mine, qkv_next = lax.optimization_barrier((mlp_mine, qkv_next))
    mlp_near = ring_first(mlp_mine)

    image_in = modulate(hidden[0], mods[0], mods[1])
    peer_in = swap(image_in, "img", 1)
    mine, theirs = project_qkv(chip, image_in, peer_in, qkv_pieces)
    other = swap(theirs, "img", 1)
    first = jnp.where(core[0] == 0, mine, other)
    second = jnp.where(core[0] == 0, other, mine)
    qkv = jnp.stack([first, second], axis=1).reshape(3, HEADS, HEAD, tok_rows)
    heads = qkv.transpose(1, 0, 2, 3).reshape(HEADS, 3 * HEAD, tok_rows)
    heads = jnp.pad(heads, ((0, blocks - HEADS), (0, 0), (0, 0)))
    parts = lax.all_to_all(heads, "blk", 0, 0, tiled=True)

    head = jnp.minimum(blk, HEADS - 1)
    text_in = modulate(text_hidden[0], text_mod[0, 0], text_mod[0, 1])
    text_cols = jnp.concatenate(
        [
            lax.dynamic_slice(text_weight, (0, start + head * HEAD), (width, HEAD))
            for start in (0, width_attn)
        ],
        axis=1,
    )
    text_kv = lax.dot_general(
        text_cols, text_in, (((0,), (1,)), ((), ())), preferred_element_type=F32
    ).astype(BF16)
    text_kv = jnp.pad(text_kv, ((0, 0), (0, -text_kv.shape[1] % tok_rows)))

    parts, mlp_near = lax.optimization_barrier((parts, mlp_near))
    mlp_next = ring_second(*mlp_near)
    mixed = attend(counts, parts, text_kv)
    mixed = lax.all_to_all(mixed, "blk", 0, 0, tiled=True)[:HEADS].reshape(width_attn, tok_rows)

    mixed, mlp_low, mlp_high = lax.optimization_barrier((mixed, mlp_next[0], mlp_next[1]))
    mlp_far = ring_third(mlp_low, mlp_high)
    mlp_pieces = [mlp_mine, *mlp_near, mlp_far[0], *mlp_next[2:], mlp_far[1]]

    updated, mlp_in = middle(mixed, hidden[0], mods, out_weight)
    act = mlp_first(chip, mlp_in, swap(mlp_in, "img", 1), mlp_pieces)
    peer_act = swap(act, "img", 1)
    own_part, sent_part = mlp_second(chip, core, act, peer_act, mlp_pieces)
    peer_part = swap(sent_part, "img", 1)
    predicted = last(core, own_part, peer_part, updated, mods, final_mod[0], final_weight)

    patch_count = counts[0]
    patch_rows = tok_rows // W_P
    lat_rows = 2 * patch_rows
    vel_lat = (
        predicted.reshape(patch_rows, W_P, 2, 2, CH)
        .transpose(0, 2, 1, 3, 4)
        .reshape(lat_rows, 2 * W_P * CH)
    )
    global_rows = blk * lat_rows + jnp.arange(lat_rows, dtype=jnp.int32)
    live_rows = (global_rows < 2 * (patch_count // W_P))[:, None]
    velocity = jnp.where(live_rows, vel_lat, 0.0)
    step_value = step_index[0].astype(F32)
    sigma_gap = plan(step_value + 1.0) - plan(step_value)
    next_lat = jnp.where(live_rows, latent[0] + sigma_gap * vel_lat, 0.0)
    scaled = jnp.where(live_rows, next_lat / vae_scale + vae_offset, 0.0).astype(BF16)
    framed = padded(scaled, "blk", 1)
    padded_grid = jnp.pad(framed.reshape(lat_rows + 2, 2 * W_P, CH), ((0, 0), (1, 1), (0, 0)))
    columns = jnp.concatenate(
        [
            padded_grid[row_off : row_off + lat_rows, col_off : col_off + 2 * W_P, :]
            for row_off in range(3)
            for col_off in range(3)
        ],
        axis=-1,
    ).reshape(lat_rows * 2 * W_P, 9 * CH)
    feature = jnp.dot(columns, conv_weight, preferred_element_type=F32) + conv_bias
    feature = jnp.where(live_rows[:, :, None], feature.reshape(lat_rows, 2 * W_P, -1), 0.0).astype(
        BF16
    )
    return (velocity[None], next_lat[None], feature[None])


def solution(mesh):
    placed = (
        P("img", "blk", None),
        P("img", None, None),
        P("img", "blk", None),
        P("img", None, None),
        P("img", None, None),
        P("img", None, None),
        P("img"),
        P("img"),
        P(None, "img"),
        P(),
        P(),
        P(None, "img"),
        P(None, "img"),
        P(),
        P(),
        P(),
    )
    return jax.shard_map(
        per_device,
        mesh=mesh,
        in_specs=placed,
        out_specs=(P("img", "blk", None), P("img", "blk", None), P("img", "blk", None, None)),
        check_vma=False,
    )
```

```python
import jax
import jax.numpy as jnp
from jax import lax
from jax.experimental import pallas as pl
from jax.experimental.pallas import tpu as pltpu
from jax.sharding import PartitionSpec as P

HEAD = 64
CH = 16
HEADS = 12
W_P = 64
STEPS = 8

norm_eps = 1e-06
sigma_shift = 3.0
vae_scale = 1.5305
vae_offset = 0.0609
masked_score = -1e30

F32 = jnp.float32
BF16 = jnp.bfloat16


def modulate(inputs, shift_row, scale_row):
    values = inputs.astype(F32)
    center = jnp.mean(values, axis=-1, keepdims=True)
    spread = jnp.mean(jnp.square(values - center), axis=-1, keepdims=True)
    normed = (values - center) * lax.rsqrt(spread + norm_eps)
    return (normed * (1.0 + scale_row) + shift_row).astype(BF16)


def plan(step_value):
    remain = 1.0 - step_value / STEPS
    return sigma_shift * remain / (1.0 + (sigma_shift - 1.0) * remain)


def swap(x, axis, bits):
    return lax.ppermute(x, axis, [(i, i ^ bits) for i in range(lax.axis_size(axis))])


def vmem_specs(count):
    return [pl.BlockSpec(memory_space=pltpu.VMEM)] * count


OFFSETS = ((0, 0), (-1, 0), (1, 0), (0, 1), (2, 0), (-1, 1), (1, 1), (2, 1))


def ring(x, axis, step):
    size = lax.axis_size(axis)
    return lax.ppermute(x, axis, [(i, (i + step) % size) for i in range(size)])


def ring_first(x):
    return ring(x, "img", 4), ring(x, "img", -4), swap(x, "img", 2)


def ring_second(left, right, across):
    half = left.shape[0] // 2
    return (
        ring(left[:half], "img", 4),
        ring(right[half:], "img", -4),
        ring(across, "img", 4),
        ring(across, "img", -4),
    )


def ring_third(low, high):
    far = jnp.concatenate([low, high], axis=0)
    return far, swap(far, "img", 2)


def place_of(chip, k):
    dx, dy = OFFSETS[k]
    column = jnp.bitwise_and(chip // 2 + dx + 4, 3)
    return 2 * column + jnp.bitwise_xor(jnp.bitwise_and(chip, 1), dy)


def qkv_body(chip_ref, own_x, peer_x, *refs):
    weights, (own_out, peer_out) = refs[:-2], refs[-2:]
    rows = own_x.shape[0]
    both = jnp.concatenate([own_x[...], peer_x[...]], axis=0)
    for k, weight in enumerate(weights):
        part = lax.dot_general(
            weight[...], both, (((1,), (1,)), ((), ())), preferred_element_type=F32
        ).astype(BF16)
        place = place_of(chip_ref[0], k)
        own_out[place] = part[:, :rows]
        peer_out[place] = part[:, rows:]


def project_qkv(chip, own_x, peer_x, weights):
    cols, rows = weights[0].shape[0], own_x.shape[0]
    shape = jax.ShapeDtypeStruct((len(weights), cols, rows), BF16)
    flops = 4 * len(weights) * cols * rows * own_x.shape[1]
    return pl.pallas_call(
        qkv_body,
        out_shape=(shape, shape),
        in_specs=[pl.BlockSpec(memory_space=pltpu.SMEM)] + vmem_specs(2 + len(weights)),
        out_specs=tuple(vmem_specs(2)),
        compiler_params=pltpu.CompilerParams(vmem_limit_bytes=32 << 20),
        cost_estimate=pl.CostEstimate(flops=1000, bytes_accessed=1000, transcendentals=0),
        name="project_qkv",
    )(chip, own_x, peer_x, *weights)


def attend_body(count_ref, parts, text, out, keys, values, queries):
    blocks, _, rows = parts.shape
    text_blocks = text.shape[1] // rows
    text_len = 154
    tile = 2 * rows
    lane = lax.broadcasted_iota(jnp.int32, (8, rows), 1)
    row = lax.broadcasted_iota(jnp.int32, (8, rows), 0)
    top = row == 0
    zeros = jnp.zeros((HEAD - 8, rows), F32)

    def place_keys(index, key_part, limit):
        bias = jnp.where(jnp.logical_and(top, lane >= limit), masked_score, 0.0)
        full = jnp.concatenate([key_part.astype(F32), bias, zeros], axis=0)
        keys[pl.ds(index * rows, rows), :] = full.T.astype(BF16)

    ones = jnp.concatenate([jnp.where(top, 1.0, 0.0).astype(F32), zeros], axis=0)
    for b in range(blocks):
        part = parts[b]
        place_keys(b, part[HEAD : 2 * HEAD], count_ref[0] - b * rows)
        values[:, b * rows : (b + 1) * rows] = part[2 * HEAD :]
        scaled = part[:HEAD].astype(F32) * 0.125
        queries[:, b * rows : (b + 1) * rows] = jnp.concatenate([scaled, ones], axis=0).astype(BF16)
    for t in range(text_blocks):
        cols = slice(t * rows, (t + 1) * rows)
        place_keys(blocks + t, text[:HEAD, cols], text_len - t * rows)
        values[:, (blocks + t) * rows : (blocks + t + 1) * rows] = text[HEAD:, cols]

    def step(t, carry):
        first = pl.multiple_of(t * tile, tile)
        scores = jnp.dot(keys[...], queries[:, pl.ds(first, tile)], preferred_element_type=F32)
        top_score = jnp.max(scores, axis=0, keepdims=True)
        numer = jnp.exp(scores - top_score)
        total = jnp.sum(numer, axis=0, keepdims=True)
        mixed = jnp.dot(values[...], numer.astype(BF16), preferred_element_type=F32) / total
        mixed = mixed.astype(BF16)
        out[2 * t] = mixed[:, :rows]
        out[2 * t + 1] = mixed[:, rows:]
        return carry

    lax.fori_loop(0, blocks // 2, step, 0)


def attend(count, parts, text):
    blocks, _, rows = parts.shape
    keys = blocks * rows + text.shape[1]
    queries = blocks * rows
    return pl.pallas_call(
        attend_body,
        out_shape=jax.ShapeDtypeStruct((blocks, HEAD, rows), BF16),
        in_specs=[pl.BlockSpec(memory_space=pltpu.SMEM)] + vmem_specs(2),
        out_specs=vmem_specs(1)[0],
        scratch_shapes=[
            pltpu.VMEM((keys, 2 * HEAD), BF16),
            pltpu.VMEM((HEAD, keys), BF16),
            pltpu.VMEM((2 * HEAD, queries), BF16),
        ],
        compiler_params=pltpu.CompilerParams(vmem_limit_bytes=40 << 20),
        cost_estimate=pl.CostEstimate(flops=1000, bytes_accessed=1000, transcendentals=0),
        name="attend",
    )(count, parts, text)


def layer_norm(values, shift_row, scale_row):
    center = jnp.mean(values, axis=-1, keepdims=True)
    spread = jnp.mean(jnp.square(values - center), axis=-1, keepdims=True)
    normed = (values - center) * lax.rsqrt(spread + norm_eps)
    return (normed * (1.0 + scale_row) + shift_row).astype(BF16)


def gelu(v):
    return 0.5 * v * (1.0 + jnp.tanh(0.7978845608028654 * (v + 0.044715 * v * v * v)))


def middle_body(mixed, hidden, mods, out_w, updated, mlp_in):
    attended = mixed[...].astype(F32).T.astype(BF16)
    projected = jnp.dot(attended, out_w[...], preferred_element_type=F32)
    now = hidden[...].astype(F32) + mods[2:3] * projected
    updated[...] = now
    mlp_in[...] = layer_norm(now, mods[3:4], mods[4:5])


def middle(mixed, hidden, mods, out_w):
    rows, width = hidden.shape
    return pl.pallas_call(
        middle_body,
        out_shape=(
            jax.ShapeDtypeStruct((rows, width), F32),
            jax.ShapeDtypeStruct((rows, width), BF16),
        ),
        in_specs=vmem_specs(4),
        out_specs=tuple(vmem_specs(2)),
        compiler_params=pltpu.CompilerParams(vmem_limit_bytes=24 << 20),
        cost_estimate=pl.CostEstimate(flops=1000, bytes_accessed=1000, transcendentals=0),
        name="middle",
    )(mixed, hidden, mods, out_w)


def first_body(chip_ref, own_x, peer_x, *refs):
    weights, out = refs[:-1], refs[-1]
    both = jnp.concatenate([own_x[...], peer_x[...]], axis=0)
    cols = out.shape[1]
    for k, weight in enumerate(weights):
        part = lax.dot_general(
            weight[:cols], both, (((1,), (1,)), ((), ())), preferred_element_type=F32
        )
        out[place_of(chip_ref[0], k)] = gelu(part).astype(BF16)


def mlp_first(chip, own_x, peer_x, weights, cols):
    rows = own_x.shape[0]
    count = len(weights)
    return pl.pallas_call(
        first_body,
        out_shape=jax.ShapeDtypeStruct((count, cols, 2 * rows), BF16),
        in_specs=[pl.BlockSpec(memory_space=pltpu.SMEM)] + vmem_specs(2 + count),
        out_specs=vmem_specs(1)[0],
        compiler_params=pltpu.CompilerParams(vmem_limit_bytes=32 << 20),
        cost_estimate=pl.CostEstimate(flops=1000, bytes_accessed=1000, transcendentals=0),
        name="mlp_first",
    )(chip, own_x, peer_x, *weights)


def second_body(chip_ref, core_ref, own_a, peer_a, own_b, peer_b, *refs):
    weights, (own_out, peer_out), act = refs[:-3], refs[-3:-1], refs[-1]
    count, early, tokens = own_a.shape
    late = own_b.shape[1]
    cols, mid = early + late, tokens // 2
    core = core_ref[0]
    for c in range(count):
        for own, peer, shift, size in ((own_a, peer_a, 0, early), (own_b, peer_b, early, late)):
            mine = pl.ds(pl.multiple_of((2 * c + core) * cols + shift, 16), size)
            act[mine, :] = own[c]
            other = pl.ds(pl.multiple_of((2 * c + 1 - core) * cols + shift, 16), size)
            act[other, :mid] = peer[c, :, mid:]
            act[other, mid:] = peer[c, :, :mid]
    width = weights[0].shape[1]
    half = cols // 2
    for k, weight in enumerate(weights):
        part = jnp.dot(weight[late : late + half], act[:width], preferred_element_type=F32)
        part += jnp.dot(weight[late + half :], act[width:], preferred_element_type=F32)
        place = place_of(chip_ref[0], k)
        own_out[place] = part[:, :mid]
        peer_out[place] = part[:, mid:]


def mlp_second(chip, core, own_a, peer_a, own_b, peer_b, weights):
    count, early, tokens = own_a.shape
    cols = early + own_b.shape[1]
    shape = jax.ShapeDtypeStruct((count, cols // 2, tokens // 2), F32)
    return pl.pallas_call(
        second_body,
        out_shape=(shape, shape),
        in_specs=[pl.BlockSpec(memory_space=pltpu.SMEM)] * 2 + vmem_specs(4 + count),
        out_specs=tuple(vmem_specs(2)),
        scratch_shapes=[pltpu.VMEM((2 * count * cols, tokens), BF16)],
        compiler_params=pltpu.CompilerParams(vmem_limit_bytes=32 << 20),
        cost_estimate=pl.CostEstimate(flops=1000, bytes_accessed=1000, transcendentals=0),
        name="mlp_second",
    )(chip, core, own_a, peer_a, own_b, peer_b, *weights)


def last_body(core_ref, own_part, peer_part, updated, mods, finals, final_w, predicted, mlp_t):
    count, half, _ = own_part.shape
    for source, parity in ((own_part, core_ref[0]), (peer_part, 1 - core_ref[0])):
        for c in range(count):
            start = pl.multiple_of((2 * c + parity) * half, half)
            mlp_t[pl.ds(start, half), :] = source[c]
    refined = updated[...] + mods[5:6] * mlp_t[...].T
    final_in = layer_norm(refined, finals[0:1], finals[1:2])
    predicted[...] = jnp.dot(final_in, final_w[...], preferred_element_type=F32)


def last(core, own_part, peer_part, updated, mods, finals, final_w):
    rows, width = updated.shape
    return pl.pallas_call(
        last_body,
        out_shape=jax.ShapeDtypeStruct((rows, final_w.shape[1]), F32),
        in_specs=[pl.BlockSpec(memory_space=pltpu.SMEM)] + vmem_specs(6),
        out_specs=vmem_specs(1)[0],
        scratch_shapes=[pltpu.VMEM((width, rows), F32)],
        compiler_params=pltpu.CompilerParams(vmem_limit_bytes=24 << 20),
        cost_estimate=pl.CostEstimate(flops=1000, bytes_accessed=1000, transcendentals=0),
        name="last",
    )(core, own_part, peer_part, updated, mods, finals, final_w)


def padded(x, axis, width):
    size, length = lax.axis_size(axis), x.shape[0]
    up = [(i, i + 1) for i in range(size - 1)]
    down = [(j, i) for i, j in up]
    before = lax.ppermute(x[length - width :], axis, up)
    after = lax.ppermute(x[:width], axis, down)
    return jnp.concatenate([before, x, after], axis=0)


def per_device(
    hidden,
    text_hidden,
    latent,
    image_mod,
    text_mod,
    final_mod,
    counts,
    step_index,
    qkv_weight,
    text_weight,
    out_weight,
    mlp_in_weight,
    mlp_out_weight,
    final_weight,
    conv_weight,
    conv_bias,
):
    tok_rows, width = hidden.shape[1:]
    width_attn = HEADS * HEAD
    blocks = lax.axis_size("blk")
    blk, img = lax.axis_index("blk"), lax.axis_index("img")
    chip, core = img // 2, img % 2
    mods = image_mod[0]
    chip, core = chip[None], core[None]

    qkv_t = qkv_weight.T
    early = 7 * tok_rows // 8
    mlp_cols = mlp_in_weight.shape[1]
    mlp_in_t = mlp_in_weight.T
    part_a = mlp_in_t[:early]
    part_b = jnp.concatenate(
        [mlp_in_t[early:], mlp_out_weight[:width].T, mlp_out_weight[width:].T], axis=0
    )
    qkv_near = ring_first(qkv_t)
    part_a, part_b, qkv_near = lax.optimization_barrier((part_a, part_b, qkv_near))
    qkv_next = ring_second(*qkv_near)
    qkv_far = ring_third(*qkv_next[:2])
    qkv_pieces = [qkv_t, *qkv_near, qkv_far[0], *qkv_next[2:], qkv_far[1]]

    part_a, qkv_low, qkv_high = lax.optimization_barrier((part_a, qkv_next[2], qkv_next[3]))
    near_a = ring_first(part_a)

    image_in = modulate(hidden[0], mods[0], mods[1])
    peer_in = swap(image_in, "img", 1)
    head = jnp.minimum(blk, HEADS - 1)
    text_in = modulate(text_hidden[0], text_mod[0, 0], text_mod[0, 1])
    text_cols = jnp.concatenate(
        [
            lax.dynamic_slice(text_weight, (0, start + head * HEAD), (width, HEAD))
            for start in (0, width_attn)
        ],
        axis=1,
    )
    text_kv = lax.dot_general(
        text_cols, text_in, (((0,), (1,)), ((), ())), preferred_element_type=F32
    ).astype(BF16)
    text_kv = jnp.pad(text_kv, ((0, 0), (0, -text_kv.shape[1] % tok_rows)))
    text_kv, peer_in = lax.optimization_barrier((text_kv, peer_in))

    mine, theirs = project_qkv(chip, image_in, peer_in, qkv_pieces)
    theirs, near_a, part_b = lax.optimization_barrier((theirs, near_a, part_b))
    other = swap(theirs, "img", 1)
    first = jnp.where(core[0] == 0, mine, other)
    second = jnp.where(core[0] == 0, other, mine)
    qkv = jnp.stack([first, second], axis=1).reshape(3, HEADS, HEAD, tok_rows)
    heads = qkv.transpose(1, 0, 2, 3).reshape(HEADS, 3 * HEAD, tok_rows)
    heads = jnp.pad(heads, ((0, blocks - HEADS), (0, 0), (0, 0)))
    next_a = ring_second(*near_a)
    near_b = ring_first(part_b)
    parts = lax.all_to_all(heads, "blk", 0, 0, tiled=True)

    parts, next_a, near_b = lax.optimization_barrier((parts, next_a, near_b))
    far_a = ring_third(*next_a[:2])
    next_b = ring_second(*near_b)
    mixed = attend(counts, parts, text_kv)
    mixed, far_a, low_b, high_b = lax.optimization_barrier((mixed, far_a, next_b[0], next_b[1]))
    far_b = ring_third(low_b, high_b)
    mixed = lax.all_to_all(mixed, "blk", 0, 0, tiled=True)[:HEADS].reshape(width_attn, tok_rows)
    pieces_a = [part_a, *near_a, far_a[0], *next_a[2:], far_a[1]]
    pieces_b = [part_b, *near_b, far_b[0], *next_b[2:], far_b[1]]

    updated, mlp_in = middle(mixed, hidden[0], mods, out_weight)
    peer_mlp = swap(mlp_in, "img", 1)
    act_a = mlp_first(chip, mlp_in, peer_mlp, pieces_a, early)
    peer_a = swap(act_a, "img", 1)
    act_b = mlp_first(chip, mlp_in, peer_mlp, pieces_b, mlp_cols - early)
    peer_b = swap(act_b, "img", 1)
    own_part, sent_part = mlp_second(chip, core, act_a, peer_a, act_b, peer_b, pieces_b)
    peer_part = swap(sent_part, "img", 1)
    predicted = last(core, own_part, peer_part, updated, mods, final_mod[0], final_weight)

    patch_count = counts[0]
    patch_rows = tok_rows // W_P
    lat_rows = 2 * patch_rows
    vel_lat = (
        predicted.reshape(patch_rows, W_P, 2, 2, CH)
        .transpose(0, 2, 1, 3, 4)
        .reshape(lat_rows, 2 * W_P * CH)
    )
    global_rows = blk * lat_rows + jnp.arange(lat_rows, dtype=jnp.int32)
    live_rows = (global_rows < 2 * (patch_count // W_P))[:, None]
    velocity = jnp.where(live_rows, vel_lat, 0.0)
    step_value = step_index[0].astype(F32)
    sigma_gap = plan(step_value + 1.0) - plan(step_value)
    next_lat = jnp.where(live_rows, latent[0] + sigma_gap * vel_lat, 0.0)
    scaled = jnp.where(live_rows, next_lat / vae_scale + vae_offset, 0.0).astype(BF16)
    framed = padded(scaled, "blk", 1)
    padded_grid = jnp.pad(framed.reshape(lat_rows + 2, 2 * W_P, CH), ((0, 0), (1, 1), (0, 0)))
    columns = jnp.concatenate(
        [
            padded_grid[row_off : row_off + lat_rows, col_off : col_off + 2 * W_P, :]
            for row_off in range(3)
            for col_off in range(3)
        ],
        axis=-1,
    ).reshape(lat_rows * 2 * W_P, 9 * CH)
    feature = jnp.dot(columns, conv_weight, preferred_element_type=F32) + conv_bias
    feature = jnp.where(live_rows[:, :, None], feature.reshape(lat_rows, 2 * W_P, -1), 0.0).astype(
        BF16
    )
    return (velocity[None], next_lat[None], feature[None])


def solution(mesh):
    placed = (
        P("img", "blk", None),
        P("img", None, None),
        P("img", "blk", None),
        P("img", None, None),
        P("img", None, None),
        P("img", None, None),
        P("img"),
        P("img"),
        P(None, "img"),
        P(),
        P(),
        P(None, "img"),
        P(None, "img"),
        P(),
        P(),
        P(),
    )
    return jax.shard_map(
        per_device,
        mesh=mesh,
        in_specs=placed,
        out_specs=(P("img", "blk", None), P("img", "blk", None), P("img", "blk", None, None)),
        check_vma=False,
    )
```

```python
import jax
import jax.numpy as jnp
from jax import lax
from jax.experimental import pallas as pl
from jax.experimental.pallas import tpu as pltpu
from jax.sharding import PartitionSpec as P

HEAD = 64
CH = 16
HEADS = 12
W_P = 64
STEPS = 8

norm_eps = 1e-06
sigma_shift = 3.0
vae_scale = 1.5305
vae_offset = 0.0609
masked_score = -1e30

F32 = jnp.float32
BF16 = jnp.bfloat16


def modulate(inputs, shift_row, scale_row):
    values = inputs.astype(F32)
    center = jnp.mean(values, axis=-1, keepdims=True)
    spread = jnp.mean(jnp.square(values - center), axis=-1, keepdims=True)
    normed = (values - center) * lax.rsqrt(spread + norm_eps)
    return (normed * (1.0 + scale_row) + shift_row).astype(BF16)


def plan(step_value):
    remain = 1.0 - step_value / STEPS
    return sigma_shift * remain / (1.0 + (sigma_shift - 1.0) * remain)


def swap(x, axis, bits):
    return lax.ppermute(x, axis, [(i, i ^ bits) for i in range(lax.axis_size(axis))])


def vmem_specs(count):
    return [pl.BlockSpec(memory_space=pltpu.VMEM)] * count


OFFSETS = ((0, 0), (-1, 0), (1, 0), (0, 1), (2, 0), (-1, 1), (1, 1), (2, 1))


def ring(x, axis, step):
    size = lax.axis_size(axis)
    return lax.ppermute(x, axis, [(i, (i + step) % size) for i in range(size)])


def ring_first(x):
    return ring(x, "img", 4), ring(x, "img", -4), swap(x, "img", 2)


def ring_second(left, right, across):
    half = left.shape[0] // 2
    return (
        ring(left[:half], "img", 4),
        ring(right[half:], "img", -4),
        ring(across, "img", 4),
        ring(across, "img", -4),
    )


def ring_third(low, high):
    far = jnp.concatenate([low, high], axis=0)
    return far, swap(far, "img", 2)


def place_of(chip, k):
    dx, dy = OFFSETS[k]
    column = jnp.bitwise_and(chip // 2 + dx + 4, 3)
    return 2 * column + jnp.bitwise_xor(jnp.bitwise_and(chip, 1), dy)


def qkv_body(chip_ref, own_x, peer_x, *refs):
    weights, (own_out, peer_out) = refs[:-2], refs[-2:]
    rows = own_x.shape[0]
    both = jnp.concatenate([own_x[...], peer_x[...]], axis=0)
    cols = own_out.shape[1]
    stacked = jnp.concatenate([weight[...] for weight in weights], axis=0)
    parts = lax.dot_general(
        stacked, both, (((1,), (1,)), ((), ())), preferred_element_type=F32
    ).astype(BF16)
    for k in range(len(weights)):
        place = place_of(chip_ref[0], k)
        own_out[place] = parts[k * cols : (k + 1) * cols, :rows]
        peer_out[place] = parts[k * cols : (k + 1) * cols, rows:]


def project_qkv(chip, own_x, peer_x, weights):
    cols, rows = weights[0].shape[0], own_x.shape[0]
    shape = jax.ShapeDtypeStruct((len(weights), cols, rows), BF16)
    flops = 4 * len(weights) * cols * rows * own_x.shape[1]
    return pl.pallas_call(
        qkv_body,
        out_shape=(shape, shape),
        in_specs=[pl.BlockSpec(memory_space=pltpu.SMEM)] + vmem_specs(2 + len(weights)),
        out_specs=tuple(vmem_specs(2)),
        compiler_params=pltpu.CompilerParams(vmem_limit_bytes=32 << 20),
        cost_estimate=pl.CostEstimate(flops=1000, bytes_accessed=1000, transcendentals=0),
        name="project_qkv",
    )(chip, own_x, peer_x, *weights)


def attend_body(count_ref, parts, text, out, keys, values, queries):
    blocks, _, rows = parts.shape
    text_blocks = text.shape[1] // rows
    text_len = 154
    tile = 2 * rows
    lane = lax.broadcasted_iota(jnp.int32, (8, rows), 1)
    row = lax.broadcasted_iota(jnp.int32, (8, rows), 0)
    top = row == 0
    zeros = jnp.zeros((HEAD - 8, rows), F32)

    def place_keys(index, key_part, limit):
        bias = jnp.where(jnp.logical_and(top, lane >= limit), masked_score, 0.0)
        full = jnp.concatenate([key_part.astype(F32), bias, zeros], axis=0)
        keys[pl.ds(index * rows, rows), :] = full.T.astype(BF16)

    ones = jnp.concatenate([jnp.where(top, 1.0, 0.0).astype(F32), zeros], axis=0)
    for b in range(blocks):
        part = parts[b]
        place_keys(b, part[HEAD : 2 * HEAD], count_ref[0] - b * rows)
        values[:, b * rows : (b + 1) * rows] = part[2 * HEAD :]
        scaled = part[:HEAD].astype(F32) * 0.125
        queries[:, b * rows : (b + 1) * rows] = jnp.concatenate([scaled, ones], axis=0).astype(BF16)
    for t in range(text_blocks):
        cols = slice(t * rows, (t + 1) * rows)
        place_keys(blocks + t, text[:HEAD, cols], text_len - t * rows)
        values[:, (blocks + t) * rows : (blocks + t + 1) * rows] = text[HEAD:, cols]

    def step(t, carry):
        first = pl.multiple_of(t * tile, tile)
        scores = jnp.dot(keys[...], queries[:, pl.ds(first, tile)], preferred_element_type=F32)
        top_score = jnp.max(scores, axis=0, keepdims=True)
        numer = jnp.exp(scores - top_score)
        total = jnp.sum(numer, axis=0, keepdims=True)
        mixed = jnp.dot(values[...], numer.astype(BF16), preferred_element_type=F32) / total
        mixed = mixed.astype(BF16)
        out[2 * t] = mixed[:, :rows]
        out[2 * t + 1] = mixed[:, rows:]
        return carry

    lax.fori_loop(0, blocks // 2, step, 0)


def attend(count, parts, text):
    blocks, _, rows = parts.shape
    keys = blocks * rows + text.shape[1]
    queries = blocks * rows
    return pl.pallas_call(
        attend_body,
        out_shape=jax.ShapeDtypeStruct((blocks, HEAD, rows), BF16),
        in_specs=[pl.BlockSpec(memory_space=pltpu.SMEM)] + vmem_specs(2),
        out_specs=vmem_specs(1)[0],
        scratch_shapes=[
            pltpu.VMEM((keys, 2 * HEAD), BF16),
            pltpu.VMEM((HEAD, keys), BF16),
            pltpu.VMEM((2 * HEAD, queries), BF16),
        ],
        compiler_params=pltpu.CompilerParams(vmem_limit_bytes=40 << 20),
        cost_estimate=pl.CostEstimate(flops=1000, bytes_accessed=1000, transcendentals=0),
        name="attend",
    )(count, parts, text)


def layer_norm(values, shift_row, scale_row):
    center = jnp.mean(values, axis=-1, keepdims=True)
    spread = jnp.mean(jnp.square(values - center), axis=-1, keepdims=True)
    normed = (values - center) * lax.rsqrt(spread + norm_eps)
    return (normed * (1.0 + scale_row) + shift_row).astype(BF16)


def gelu(v):
    return 0.5 * v * (1.0 + jnp.tanh(0.7978845608028654 * (v + 0.044715 * v * v * v)))


def middle_body(mixed, hidden, mods, out_w, updated, mlp_in):
    attended = mixed[...].astype(F32).T.astype(BF16)
    projected = jnp.dot(attended, out_w[...], preferred_element_type=F32)
    now = hidden[...].astype(F32) + mods[2:3] * projected
    updated[...] = now
    mlp_in[...] = layer_norm(now, mods[3:4], mods[4:5])


def middle(mixed, hidden, mods, out_w):
    rows, width = hidden.shape
    return pl.pallas_call(
        middle_body,
        out_shape=(
            jax.ShapeDtypeStruct((rows, width), F32),
            jax.ShapeDtypeStruct((rows, width), BF16),
        ),
        in_specs=vmem_specs(4),
        out_specs=tuple(vmem_specs(2)),
        compiler_params=pltpu.CompilerParams(vmem_limit_bytes=24 << 20),
        cost_estimate=pl.CostEstimate(flops=1000, bytes_accessed=1000, transcendentals=0),
        name="middle",
    )(mixed, hidden, mods, out_w)


def first_body(chip_ref, own_x, peer_x, *refs):
    weights, (own_out, peer_out) = refs[:-2], refs[-2:]
    rows = own_x.shape[0]
    both = jnp.concatenate([own_x[...], peer_x[...]], axis=0)
    cols = own_out.shape[1]
    stacked = jnp.concatenate([weight[...] for weight in weights], axis=0)
    parts = lax.dot_general(stacked, both, (((1,), (1,)), ((), ())), preferred_element_type=F32)
    for k in range(len(weights)):
        place = place_of(chip_ref[0], k)
        act = gelu(parts[k * cols : (k + 1) * cols]).astype(BF16)
        own_out[place] = act[:, :rows]
        peer_out[place] = act[:, rows:]


def mlp_first(chip, own_x, peer_x, weights):
    rows = own_x.shape[0]
    count = len(weights)
    shape = jax.ShapeDtypeStruct((count, weights[0].shape[0], rows), BF16)
    return pl.pallas_call(
        first_body,
        out_shape=(shape, shape),
        in_specs=[pl.BlockSpec(memory_space=pltpu.SMEM)] + vmem_specs(2 + count),
        out_specs=tuple(vmem_specs(2)),
        compiler_params=pltpu.CompilerParams(vmem_limit_bytes=40 << 20),
        cost_estimate=pl.CostEstimate(flops=1000, bytes_accessed=1000, transcendentals=0),
        name="mlp_first",
    )(chip, own_x, peer_x, *weights)


def second_body(core_ref, own_act, peer_act, updated, mods, finals, final_t, weight, predicted, act, mlp_t):
    i = pl.program_id(0)
    count, cols, _ = own_act.shape
    half = weight.shape[0]

    @pl.when(i == 0)
    def _():
        for source, parity in ((own_act, core_ref[0]), (peer_act, 1 - core_ref[0])):
            for c in range(count):
                start = pl.multiple_of((2 * c + parity) * cols, cols)
                act[pl.ds(start, cols), :] = source[c]

    mlp_t[pl.ds(pl.multiple_of(i * half, half), half), :] = jnp.dot(
        weight[...], act[...], preferred_element_type=F32
    )

    @pl.when(i == pl.num_programs(0) - 1)
    def _():
        refined = updated[...] + mods[5:6] * mlp_t[...].T
        final_in = layer_norm(refined, finals[0:1], finals[1:2])
        predicted[...] = lax.dot_general(
            final_in, final_t[...], (((1,), (1,)), ((), ())), preferred_element_type=F32
        )


def mlp_second(core, own_act, peer_act, updated, mods, finals, final_t, weight):
    rows, width = updated.shape
    steps = 6
    half = width // steps
    wide = weight.shape[1]

    def whole(x):
        return pl.BlockSpec(x.shape, lambda i: (0,) * x.ndim)

    return pl.pallas_call(
        second_body,
        out_shape=jax.ShapeDtypeStruct((rows, final_t.shape[0]), F32),
        grid=(steps,),
        in_specs=[pl.BlockSpec(memory_space=pltpu.SMEM)]
        + [whole(x) for x in (own_act, peer_act, updated, mods, finals, final_t)]
        + [pl.BlockSpec((half, wide), lambda i: (i, 0))],
        out_specs=pl.BlockSpec((rows, final_t.shape[0]), lambda i: (0, 0)),
        scratch_shapes=[pltpu.VMEM((wide, rows), BF16), pltpu.VMEM((width, rows), F32)],
        compiler_params=pltpu.CompilerParams(vmem_limit_bytes=32 << 20),
        cost_estimate=pl.CostEstimate(flops=1000, bytes_accessed=1000, transcendentals=0),
        name="mlp_second",
    )(core, own_act, peer_act, updated, mods, finals, final_t, weight)


def padded(x, axis, width):
    size, length = lax.axis_size(axis), x.shape[0]
    up = [(i, i + 1) for i in range(size - 1)]
    down = [(j, i) for i, j in up]
    before = lax.ppermute(x[length - width :], axis, up)
    after = lax.ppermute(x[:width], axis, down)
    return jnp.concatenate([before, x, after], axis=0)


def per_device(
    hidden,
    text_hidden,
    latent,
    image_mod,
    text_mod,
    final_mod,
    counts,
    step_index,
    qkv_weight,
    text_weight,
    out_weight,
    mlp_in_weight,
    mlp_out_weight,
    final_weight,
    conv_weight,
    conv_bias,
):
    tok_rows, width = hidden.shape[1:]
    width_attn = HEADS * HEAD
    blocks = lax.axis_size("blk")
    blk, img = lax.axis_index("blk"), lax.axis_index("img")
    chip, core = img // 2, img % 2
    mods = image_mod[0]
    chip, core = chip[None], core[None]

    mlp_out_t = lax.all_gather(mlp_out_weight.T, "img", axis=0, tiled=True)
    qkv_t, mlp_in_t = qkv_weight.T, mlp_in_weight.T
    qkv_near = ring_first(qkv_t)
    qkv_next = ring_second(*qkv_near)
    qkv_far = ring_third(*qkv_next[:2])
    qkv_pieces = [qkv_t, *qkv_near, qkv_far[0], *qkv_next[2:], qkv_far[1]]
    mlp_in_t, qkv_left, qkv_right = lax.optimization_barrier((mlp_in_t, *qkv_next[2:]))
    mlp_near = ring_first(mlp_in_t)

    image_in = modulate(hidden[0], mods[0], mods[1])
    peer_in = swap(image_in, "img", 1)
    head = jnp.minimum(blk, HEADS - 1)
    text_in = modulate(text_hidden[0], text_mod[0, 0], text_mod[0, 1])
    text_cols = jnp.concatenate(
        [
            lax.dynamic_slice(text_weight, (0, start + head * HEAD), (width, HEAD))
            for start in (0, width_attn)
        ],
        axis=1,
    )
    text_kv = lax.dot_general(
        text_cols, text_in, (((0,), (1,)), ((), ())), preferred_element_type=F32
    ).astype(BF16)
    text_kv = jnp.pad(text_kv, ((0, 0), (0, -text_kv.shape[1] % tok_rows)))
    text_kv, peer_in = lax.optimization_barrier((text_kv, peer_in))

    mine, theirs = project_qkv(chip, image_in, peer_in, qkv_pieces)
    other = swap(theirs, "img", 1)
    first = jnp.where(core[0] == 0, mine, other)
    second = jnp.where(core[0] == 0, other, mine)
    qkv = jnp.stack([first, second], axis=1).reshape(3, HEADS, HEAD, tok_rows)
    heads = qkv.transpose(1, 0, 2, 3).reshape(HEADS, 3 * HEAD, tok_rows)
    heads = jnp.pad(heads, ((0, blocks - HEADS), (0, 0), (0, 0)))
    parts = lax.all_to_all(heads, "blk", 0, 0, tiled=True)

    parts, mlp_near = lax.optimization_barrier((parts, mlp_near))
    mlp_next = ring_second(*mlp_near)
    mixed = attend(counts, parts, text_kv)
    mixed, low, high = lax.optimization_barrier((mixed, mlp_next[0], mlp_next[1]))
    mlp_far = ring_third(low, high)
    mixed = lax.all_to_all(mixed, "blk", 0, 0, tiled=True)[:HEADS].reshape(width_attn, tok_rows)
    mlp_pieces = [mlp_in_t, *mlp_near, mlp_far[0], *mlp_next[2:], mlp_far[1]]

    updated, mlp_in = middle(mixed, hidden[0], mods, out_weight)
    act, sent_act = mlp_first(chip, mlp_in, swap(mlp_in, "img", 1), mlp_pieces)
    peer_act = swap(sent_act, "img", 1)
    predicted = mlp_second(
        core, act, peer_act, updated, mods, final_mod[0], final_weight.T, mlp_out_t
    )

    patch_count = counts[0]
    patch_rows = tok_rows // W_P
    lat_rows = 2 * patch_rows
    vel_lat = (
        predicted.reshape(patch_rows, W_P, 2, 2, CH)
        .transpose(0, 2, 1, 3, 4)
        .reshape(lat_rows, 2 * W_P * CH)
    )
    global_rows = blk * lat_rows + jnp.arange(lat_rows, dtype=jnp.int32)
    live_rows = (global_rows < 2 * (patch_count // W_P))[:, None]
    velocity = jnp.where(live_rows, vel_lat, 0.0)
    step_value = step_index[0].astype(F32)
    sigma_gap = plan(step_value + 1.0) - plan(step_value)
    next_lat = jnp.where(live_rows, latent[0] + sigma_gap * vel_lat, 0.0)
    scaled = jnp.where(live_rows, next_lat / vae_scale + vae_offset, 0.0).astype(BF16)
    framed = padded(scaled, "blk", 1)
    padded_grid = jnp.pad(framed.reshape(lat_rows + 2, 2 * W_P, CH), ((0, 0), (1, 1), (0, 0)))
    columns = jnp.concatenate(
        [
            padded_grid[row_off : row_off + lat_rows, col_off : col_off + 2 * W_P, :]
            for row_off in range(3)
            for col_off in range(3)
        ],
        axis=-1,
    ).reshape(lat_rows * 2 * W_P, 9 * CH)
    feature = jnp.dot(columns, conv_weight, preferred_element_type=F32) + conv_bias
    feature = jnp.where(live_rows[:, :, None], feature.reshape(lat_rows, 2 * W_P, -1), 0.0).astype(
        BF16
    )
    return (velocity[None], next_lat[None], feature[None])


def solution(mesh):
    placed = (
        P("img", "blk", None),
        P("img", None, None),
        P("img", "blk", None),
        P("img", None, None),
        P("img", None, None),
        P("img", None, None),
        P("img"),
        P("img"),
        P(None, "img"),
        P(),
        P(),
        P(None, "img"),
        P(None, "img"),
        P(),
        P(),
        P(),
    )
    return jax.shard_map(
        per_device,
        mesh=mesh,
        in_specs=placed,
        out_specs=(P("img", "blk", None), P("img", "blk", None), P("img", "blk", None, None)),
        check_vma=False,
    )
```

```python
import jax
import jax.numpy as jnp
from jax import lax
from jax.experimental import pallas as pl
from jax.experimental.pallas import tpu as pltpu
from jax.sharding import PartitionSpec as P

HEAD = 64
CH = 16
HEADS = 12
W_P = 64
STEPS = 8

norm_eps = 1e-06
sigma_shift = 3.0
vae_scale = 1.5305
vae_offset = 0.0609
masked_score = -1e30

F32 = jnp.float32
BF16 = jnp.bfloat16


def modulate(inputs, shift_row, scale_row):
    values = inputs.astype(F32)
    center = jnp.mean(values, axis=-1, keepdims=True)
    spread = jnp.mean(jnp.square(values - center), axis=-1, keepdims=True)
    normed = (values - center) * lax.rsqrt(spread + norm_eps)
    return (normed * (1.0 + scale_row) + shift_row).astype(BF16)


def plan(step_value):
    remain = 1.0 - step_value / STEPS
    return sigma_shift * remain / (1.0 + (sigma_shift - 1.0) * remain)


def swap(x, axis, bits):
    return lax.ppermute(x, axis, [(i, i ^ bits) for i in range(lax.axis_size(axis))])


def vmem_specs(count):
    return [pl.BlockSpec(memory_space=pltpu.VMEM)] * count


OFFSETS = ((0, 0), (-1, 0), (1, 0), (0, 1), (2, 0), (-1, 1), (1, 1), (2, 1))


def ring(x, axis, step):
    size = lax.axis_size(axis)
    return lax.ppermute(x, axis, [(i, (i + step) % size) for i in range(size)])


def ring_first(x):
    return ring(x, "img", 4), ring(x, "img", -4), swap(x, "img", 2)


def ring_second(left, right, across):
    half = left.shape[0] // 2
    return (
        ring(left[:half], "img", 4),
        ring(right[half:], "img", -4),
        ring(across, "img", 4),
        ring(across, "img", -4),
    )


def ring_third(low, high):
    far = jnp.concatenate([low, high], axis=0)
    return far, swap(far, "img", 2)


def place_of(chip, k):
    dx, dy = OFFSETS[k]
    column = jnp.bitwise_and(chip // 2 + dx + 4, 3)
    return 2 * column + jnp.bitwise_xor(jnp.bitwise_and(chip, 1), dy)


def qkv_body(chip_ref, own_x, peer_x, *refs):
    weights, (own_out, peer_out) = refs[:-2], refs[-2:]
    rows = own_x.shape[0]
    both = jnp.concatenate([own_x[...], peer_x[...]], axis=0)
    cols = own_out.shape[1]
    stacked = jnp.concatenate([weight[...] for weight in weights], axis=0)
    parts = lax.dot_general(
        stacked, both, (((1,), (1,)), ((), ())), preferred_element_type=F32
    ).astype(BF16)
    for k in range(len(weights)):
        place = place_of(chip_ref[0], k)
        own_out[place] = parts[k * cols : (k + 1) * cols, :rows]
        peer_out[place] = parts[k * cols : (k + 1) * cols, rows:]


def project_qkv(chip, own_x, peer_x, weights):
    cols, rows = weights[0].shape[0], own_x.shape[0]
    shape = jax.ShapeDtypeStruct((len(weights), cols, rows), BF16)
    flops = 4 * len(weights) * cols * rows * own_x.shape[1]
    return pl.pallas_call(
        qkv_body,
        out_shape=(shape, shape),
        in_specs=[pl.BlockSpec(memory_space=pltpu.SMEM)] + vmem_specs(2 + len(weights)),
        out_specs=tuple(vmem_specs(2)),
        compiler_params=pltpu.CompilerParams(vmem_limit_bytes=32 << 20),
        cost_estimate=pl.CostEstimate(flops=1000, bytes_accessed=1000, transcendentals=0),
        name="project_qkv",
    )(chip, own_x, peer_x, *weights)


def attend_body(count_ref, parts, text, out, keys, values, queries):
    blocks, _, rows = parts.shape
    text_blocks = text.shape[1] // rows
    text_len = 154
    tile = 2 * rows
    lane = lax.broadcasted_iota(jnp.int32, (8, rows), 1)
    row = lax.broadcasted_iota(jnp.int32, (8, rows), 0)
    top = row == 0
    zeros = jnp.zeros((HEAD - 8, rows), F32)

    def place_keys(index, key_part, limit):
        bias = jnp.where(jnp.logical_and(top, lane >= limit), masked_score, 0.0)
        full = jnp.concatenate([key_part.astype(F32), bias, zeros], axis=0)
        keys[pl.ds(index * rows, rows), :] = full.T.astype(BF16)

    ones = jnp.concatenate([jnp.where(top, 1.0, 0.0).astype(F32), zeros], axis=0)
    for b in range(blocks):
        part = parts[b]
        place_keys(b, part[HEAD : 2 * HEAD], count_ref[0] - b * rows)
        values[:, b * rows : (b + 1) * rows] = part[2 * HEAD :]
        scaled = part[:HEAD].astype(F32) * 0.125
        queries[:, b * rows : (b + 1) * rows] = jnp.concatenate([scaled, ones], axis=0).astype(BF16)
    for t in range(text_blocks):
        cols = slice(t * rows, (t + 1) * rows)
        place_keys(blocks + t, text[:HEAD, cols], text_len - t * rows)
        values[:, (blocks + t) * rows : (blocks + t + 1) * rows] = text[HEAD:, cols]

    def step(t, carry):
        first = pl.multiple_of(t * tile, tile)
        scores = jnp.dot(keys[...], queries[:, pl.ds(first, tile)], preferred_element_type=F32)
        top_score = jnp.max(scores, axis=0, keepdims=True)
        numer = jnp.exp(scores - top_score)
        total = jnp.sum(numer, axis=0, keepdims=True)
        mixed = jnp.dot(values[...], numer.astype(BF16), preferred_element_type=F32) / total
        mixed = mixed.astype(BF16)
        out[2 * t] = mixed[:, :rows]
        out[2 * t + 1] = mixed[:, rows:]
        return carry

    lax.fori_loop(0, blocks // 2, step, 0)


def attend(count, parts, text):
    blocks, _, rows = parts.shape
    keys = blocks * rows + text.shape[1]
    queries = blocks * rows
    return pl.pallas_call(
        attend_body,
        out_shape=jax.ShapeDtypeStruct((blocks, HEAD, rows), BF16),
        in_specs=[pl.BlockSpec(memory_space=pltpu.SMEM)] + vmem_specs(2),
        out_specs=vmem_specs(1)[0],
        scratch_shapes=[
            pltpu.VMEM((keys, 2 * HEAD), BF16),
            pltpu.VMEM((HEAD, keys), BF16),
            pltpu.VMEM((2 * HEAD, queries), BF16),
        ],
        compiler_params=pltpu.CompilerParams(vmem_limit_bytes=40 << 20),
        cost_estimate=pl.CostEstimate(flops=1000, bytes_accessed=1000, transcendentals=0),
        name="attend",
    )(count, parts, text)


def layer_norm(values, shift_row, scale_row):
    center = jnp.mean(values, axis=-1, keepdims=True)
    spread = jnp.mean(jnp.square(values - center), axis=-1, keepdims=True)
    normed = (values - center) * lax.rsqrt(spread + norm_eps)
    return (normed * (1.0 + scale_row) + shift_row).astype(BF16)


def gelu(v):
    return 0.5 * v * (1.0 + jnp.tanh(0.7978845608028654 * (v + 0.044715 * v * v * v)))


def middle_body(mixed, hidden, mods, out_w, updated, mlp_in):
    attended = mixed[...].astype(F32).T.astype(BF16)
    projected = jnp.dot(attended, out_w[...], preferred_element_type=F32)
    now = hidden[...].astype(F32) + mods[2:3] * projected
    updated[...] = now
    mlp_in[...] = layer_norm(now, mods[3:4], mods[4:5])


def middle(mixed, hidden, mods, out_w):
    rows, width = hidden.shape
    return pl.pallas_call(
        middle_body,
        out_shape=(
            jax.ShapeDtypeStruct((rows, width), F32),
            jax.ShapeDtypeStruct((rows, width), BF16),
        ),
        in_specs=vmem_specs(4),
        out_specs=tuple(vmem_specs(2)),
        compiler_params=pltpu.CompilerParams(vmem_limit_bytes=24 << 20),
        cost_estimate=pl.CostEstimate(flops=1000, bytes_accessed=1000, transcendentals=0),
        name="middle",
    )(mixed, hidden, mods, out_w)


def first_body(chip_ref, own_x, peer_x, *refs):
    weights, out = refs[:-1], refs[-1]
    both = jnp.concatenate([own_x[...], peer_x[...]], axis=0)
    cols = out.shape[1]
    stacked = jnp.concatenate([weight[:cols] for weight in weights], axis=0)
    parts = lax.dot_general(stacked, both, (((1,), (1,)), ((), ())), preferred_element_type=F32)
    for k in range(len(weights)):
        out[place_of(chip_ref[0], k)] = gelu(parts[k * cols : (k + 1) * cols]).astype(BF16)


def mlp_first(chip, own_x, peer_x, weights, cols):
    rows = own_x.shape[0]
    count = len(weights)
    return pl.pallas_call(
        first_body,
        out_shape=jax.ShapeDtypeStruct((count, cols, 2 * rows), BF16),
        in_specs=[pl.BlockSpec(memory_space=pltpu.SMEM)] + vmem_specs(2 + count),
        out_specs=vmem_specs(1)[0],
        compiler_params=pltpu.CompilerParams(vmem_limit_bytes=32 << 20),
        cost_estimate=pl.CostEstimate(flops=1000, bytes_accessed=1000, transcendentals=0),
        name="mlp_first",
    )(chip, own_x, peer_x, *weights)


def second_body(chip_ref, core_ref, own_a, peer_a, own_b, peer_b, *refs):
    weights, (own_out, peer_out), act = refs[:-3], refs[-3:-1], refs[-1]
    count, early, tokens = own_a.shape
    late = own_b.shape[1]
    cols, mid = early + late, tokens // 2
    core = core_ref[0]
    for c in range(count):
        for own, peer, shift, size in ((own_a, peer_a, 0, early), (own_b, peer_b, early, late)):
            mine = pl.ds(pl.multiple_of((2 * c + core) * cols + shift, 16), size)
            act[mine, :] = own[c]
            other = pl.ds(pl.multiple_of((2 * c + 1 - core) * cols + shift, 16), size)
            act[other, :mid] = peer[c, :, mid:]
            act[other, mid:] = peer[c, :, :mid]
    width = weights[0].shape[1]
    half = cols // 2
    low = jnp.concatenate([weight[late : late + half] for weight in weights], axis=0)
    parts = jnp.dot(low, act[:width], preferred_element_type=F32)
    high = jnp.concatenate([weight[late + half :] for weight in weights], axis=0)
    parts += jnp.dot(high, act[width:], preferred_element_type=F32)
    for k in range(count):
        place = place_of(chip_ref[0], k)
        own_out[place] = parts[k * half : (k + 1) * half, :mid]
        peer_out[place] = parts[k * half : (k + 1) * half, mid:]


def mlp_second(chip, core, own_a, peer_a, own_b, peer_b, weights):
    count, early, tokens = own_a.shape
    cols = early + own_b.shape[1]
    shape = jax.ShapeDtypeStruct((count, cols // 2, tokens // 2), F32)
    return pl.pallas_call(
        second_body,
        out_shape=(shape, shape),
        in_specs=[pl.BlockSpec(memory_space=pltpu.SMEM)] * 2 + vmem_specs(4 + count),
        out_specs=tuple(vmem_specs(2)),
        scratch_shapes=[pltpu.VMEM((2 * count * cols, tokens), BF16)],
        compiler_params=pltpu.CompilerParams(vmem_limit_bytes=32 << 20),
        cost_estimate=pl.CostEstimate(flops=1000, bytes_accessed=1000, transcendentals=0),
        name="mlp_second",
    )(chip, core, own_a, peer_a, own_b, peer_b, *weights)


def last_body(core_ref, own_part, peer_part, updated, mods, finals, final_w, predicted, mlp_t):
    count, half, _ = own_part.shape
    for source, parity in ((own_part, core_ref[0]), (peer_part, 1 - core_ref[0])):
        for c in range(count):
            start = pl.multiple_of((2 * c + parity) * half, half)
            mlp_t[pl.ds(start, half), :] = source[c]
    refined = updated[...] + mods[5:6] * mlp_t[...].T
    final_in = layer_norm(refined, finals[0:1], finals[1:2])
    predicted[...] = jnp.dot(final_in, final_w[...], preferred_element_type=F32)


def last(core, own_part, peer_part, updated, mods, finals, final_w):
    rows, width = updated.shape
    return pl.pallas_call(
        last_body,
        out_shape=jax.ShapeDtypeStruct((rows, final_w.shape[1]), F32),
        in_specs=[pl.BlockSpec(memory_space=pltpu.SMEM)] + vmem_specs(6),
        out_specs=vmem_specs(1)[0],
        scratch_shapes=[pltpu.VMEM((width, rows), F32)],
        compiler_params=pltpu.CompilerParams(vmem_limit_bytes=24 << 20),
        cost_estimate=pl.CostEstimate(flops=1000, bytes_accessed=1000, transcendentals=0),
        name="last",
    )(core, own_part, peer_part, updated, mods, finals, final_w)


def padded(x, axis, width):
    size, length = lax.axis_size(axis), x.shape[0]
    up = [(i, i + 1) for i in range(size - 1)]
    down = [(j, i) for i, j in up]
    before = lax.ppermute(x[length - width :], axis, up)
    after = lax.ppermute(x[:width], axis, down)
    return jnp.concatenate([before, x, after], axis=0)


def per_device(
    hidden,
    text_hidden,
    latent,
    image_mod,
    text_mod,
    final_mod,
    counts,
    step_index,
    qkv_weight,
    text_weight,
    out_weight,
    mlp_in_weight,
    mlp_out_weight,
    final_weight,
    conv_weight,
    conv_bias,
):
    tok_rows, width = hidden.shape[1:]
    width_attn = HEADS * HEAD
    blocks = lax.axis_size("blk")
    blk, img = lax.axis_index("blk"), lax.axis_index("img")
    chip, core = img // 2, img % 2
    mods = image_mod[0]
    chip, core = chip[None], core[None]

    qkv_t = qkv_weight.T
    early = 7 * tok_rows // 8
    mlp_cols = mlp_in_weight.shape[1]
    mlp_in_t = mlp_in_weight.T
    part_a = mlp_in_t[:early]
    part_b = jnp.concatenate(
        [mlp_in_t[early:], mlp_out_weight[:width].T, mlp_out_weight[width:].T], axis=0
    )
    image_in = modulate(hidden[0], mods[0], mods[1])
    part_a, part_b, image_in = lax.optimization_barrier((part_a, part_b, image_in))
    qkv_near = ring_first(qkv_t)
    qkv_next = ring_second(*qkv_near)
    qkv_far = ring_third(*qkv_next[:2])
    qkv_pieces = [qkv_t, *qkv_near, qkv_far[0], *qkv_next[2:], qkv_far[1]]

    part_a, qkv_low, qkv_high = lax.optimization_barrier((part_a, qkv_next[2], qkv_next[3]))
    near_a = ring_first(part_a)

    peer_in = swap(image_in, "img", 1)
    head = jnp.minimum(blk, HEADS - 1)
    text_in = modulate(text_hidden[0], text_mod[0, 0], text_mod[0, 1])
    text_cols = jnp.concatenate(
        [
            lax.dynamic_slice(text_weight, (0, start + head * HEAD), (width, HEAD))
            for start in (0, width_attn)
        ],
        axis=1,
    )
    text_kv = lax.dot_general(
        text_cols, text_in, (((0,), (1,)), ((), ())), preferred_element_type=F32
    ).astype(BF16)
    text_kv = jnp.pad(text_kv, ((0, 0), (0, -text_kv.shape[1] % tok_rows)))
    text_kv, peer_in = lax.optimization_barrier((text_kv, peer_in))

    mine, theirs = project_qkv(chip, image_in, peer_in, qkv_pieces)
    theirs, near_a = lax.optimization_barrier((theirs, near_a))
    next_a = ring_second(*near_a)
    low_a, high_a, part_b = lax.optimization_barrier((next_a[0], next_a[1], part_b))
    near_b = ring_first(part_b)
    other = swap(theirs, "img", 1)
    first = jnp.where(core[0] == 0, mine, other)
    second = jnp.where(core[0] == 0, other, mine)
    qkv = jnp.stack([first, second], axis=1).reshape(3, HEADS, HEAD, tok_rows)
    heads = qkv.transpose(1, 0, 2, 3).reshape(HEADS, 3 * HEAD, tok_rows)
    heads = jnp.pad(heads, ((0, blocks - HEADS), (0, 0), (0, 0)))
    parts = lax.all_to_all(heads, "blk", 0, 0, tiled=True)

    parts, low_a, high_a = lax.optimization_barrier((parts, low_a, high_a))
    far_a = ring_third(low_a, high_a)
    mixed = attend(counts, parts, text_kv)
    mixed, far_a, near_b, last_a = lax.optimization_barrier((mixed, far_a, near_b, next_a[2:]))
    next_b = ring_second(*near_b)
    mixed = lax.all_to_all(mixed, "blk", 0, 0, tiled=True)[:HEADS].reshape(width_attn, tok_rows)
    mixed, low_b, high_b = lax.optimization_barrier((mixed, next_b[0], next_b[1]))
    far_b = ring_third(low_b, high_b)
    pieces_a = [part_a, *near_a, far_a[0], *last_a, far_a[1]]
    pieces_b = [part_b, *near_b, far_b[0], *next_b[2:], far_b[1]]

    updated, mlp_in = middle(mixed, hidden[0], mods, out_weight)
    peer_mlp = swap(mlp_in, "img", 1)
    act_a = mlp_first(chip, mlp_in, peer_mlp, pieces_a, early)
    peer_a = swap(act_a, "img", 1)
    act_b = mlp_first(chip, mlp_in, peer_mlp, pieces_b, mlp_cols - early)
    peer_b = swap(act_b, "img", 1)
    own_part, sent_part = mlp_second(chip, core, act_a, peer_a, act_b, peer_b, pieces_b)
    peer_part = swap(sent_part, "img", 1)
    predicted = last(core, own_part, peer_part, updated, mods, final_mod[0], final_weight)

    patch_count = counts[0]
    patch_rows = tok_rows // W_P
    lat_rows = 2 * patch_rows
    vel_lat = (
        predicted.reshape(patch_rows, W_P, 2, 2, CH)
        .transpose(0, 2, 1, 3, 4)
        .reshape(lat_rows, 2 * W_P * CH)
    )
    global_rows = blk * lat_rows + jnp.arange(lat_rows, dtype=jnp.int32)
    live_rows = (global_rows < 2 * (patch_count // W_P))[:, None]
    velocity = jnp.where(live_rows, vel_lat, 0.0)
    step_value = step_index[0].astype(F32)
    sigma_gap = plan(step_value + 1.0) - plan(step_value)
    next_lat = jnp.where(live_rows, latent[0] + sigma_gap * vel_lat, 0.0)
    scaled = jnp.where(live_rows, next_lat / vae_scale + vae_offset, 0.0).astype(BF16)
    framed = padded(scaled, "blk", 1)
    padded_grid = jnp.pad(framed.reshape(lat_rows + 2, 2 * W_P, CH), ((0, 0), (1, 1), (0, 0)))
    columns = jnp.concatenate(
        [
            padded_grid[row_off : row_off + lat_rows, col_off : col_off + 2 * W_P, :]
            for row_off in range(3)
            for col_off in range(3)
        ],
        axis=-1,
    ).reshape(lat_rows * 2 * W_P, 9 * CH)
    feature = jnp.dot(columns, conv_weight, preferred_element_type=F32) + conv_bias
    feature = jnp.where(live_rows[:, :, None], feature.reshape(lat_rows, 2 * W_P, -1), 0.0).astype(
        BF16
    )
    return (velocity[None], next_lat[None], feature[None])


def solution(mesh):
    placed = (
        P("img", "blk", None),
        P("img", None, None),
        P("img", "blk", None),
        P("img", None, None),
        P("img", None, None),
        P("img", None, None),
        P("img"),
        P("img"),
        P(None, "img"),
        P(),
        P(),
        P(None, "img"),
        P(None, "img"),
        P(),
        P(),
        P(),
    )
    return jax.shard_map(
        per_device,
        mesh=mesh,
        in_specs=placed,
        out_specs=(P("img", "blk", None), P("img", "blk", None), P("img", "blk", None, None)),
        check_vma=False,
    )
```

```python
import jax
import jax.numpy as jnp
from jax import lax
from jax.experimental import pallas as pl
from jax.experimental.pallas import tpu as pltpu
from jax.sharding import PartitionSpec as P

HEAD = 64
CH = 16
HEADS = 12
W_P = 64
STEPS = 8

norm_eps = 1e-06
sigma_shift = 3.0
vae_scale = 1.5305
vae_offset = 0.0609
masked_score = -1e30

F32 = jnp.float32
BF16 = jnp.bfloat16


def modulate(inputs, shift_row, scale_row):
    values = inputs.astype(F32)
    center = jnp.mean(values, axis=-1, keepdims=True)
    spread = jnp.mean(jnp.square(values - center), axis=-1, keepdims=True)
    normed = (values - center) * lax.rsqrt(spread + norm_eps)
    return (normed * (1.0 + scale_row) + shift_row).astype(BF16)


def plan(step_value):
    remain = 1.0 - step_value / STEPS
    return sigma_shift * remain / (1.0 + (sigma_shift - 1.0) * remain)


def swap(x, axis, bits):
    return lax.ppermute(x, axis, [(i, i ^ bits) for i in range(lax.axis_size(axis))])


def vmem_specs(count):
    return [pl.BlockSpec(memory_space=pltpu.VMEM)] * count


OFFSETS = ((0, 0), (-1, 0), (1, 0), (0, 1), (2, 0), (-1, 1), (1, 1), (2, 1))


def ring(x, axis, step):
    size = lax.axis_size(axis)
    return lax.ppermute(x, axis, [(i, (i + step) % size) for i in range(size)])


def ring_first(x):
    return ring(x, "img", 4), ring(x, "img", -4), swap(x, "img", 2)


def ring_second(left, right, across):
    half = left.shape[0] // 2
    return (
        ring(left[:half], "img", 4),
        ring(right[half:], "img", -4),
        ring(across, "img", 4),
        ring(across, "img", -4),
    )


def ring_third(low, high):
    far = jnp.concatenate([low, high], axis=0)
    return far, swap(far, "img", 2)


def place_of(chip, k):
    dx, dy = OFFSETS[k]
    column = jnp.bitwise_and(chip // 2 + dx + 4, 3)
    return 2 * column + jnp.bitwise_xor(jnp.bitwise_and(chip, 1), dy)


def qkv_body(chip_ref, own_x, peer_x, *refs):
    weights, (own_out, peer_out) = refs[:-2], refs[-2:]
    rows = own_x.shape[0]
    both = jnp.concatenate([own_x[...], peer_x[...]], axis=0)
    cols = own_out.shape[1]
    stacked = jnp.concatenate([weight[...] for weight in weights], axis=0)
    parts = lax.dot_general(
        stacked, both, (((1,), (1,)), ((), ())), preferred_element_type=F32
    ).astype(BF16)
    for k in range(len(weights)):
        place = place_of(chip_ref[0], k)
        own_out[place] = parts[k * cols : (k + 1) * cols, :rows]
        peer_out[place] = parts[k * cols : (k + 1) * cols, rows:]


def project_qkv(chip, own_x, peer_x, weights):
    cols, rows = weights[0].shape[0], own_x.shape[0]
    shape = jax.ShapeDtypeStruct((len(weights), cols, rows), BF16)
    flops = 4 * len(weights) * cols * rows * own_x.shape[1]
    return pl.pallas_call(
        qkv_body,
        out_shape=(shape, shape),
        in_specs=[pl.BlockSpec(memory_space=pltpu.SMEM)] + vmem_specs(2 + len(weights)),
        out_specs=tuple(vmem_specs(2)),
        compiler_params=pltpu.CompilerParams(vmem_limit_bytes=32 << 20),
        cost_estimate=pl.CostEstimate(flops=1000, bytes_accessed=1000, transcendentals=0),
        name="project_qkv",
    )(chip, own_x, peer_x, *weights)


def mark_body(*refs):
    refs[-1][...] = refs[0][...]


def marker(*arrays):
    return pl.pallas_call(
        mark_body,
        out_shape=jax.ShapeDtypeStruct((16, 128), BF16),
        grid=(1,),
        in_specs=[pl.BlockSpec((16, 128), lambda i: (0, 0))] * len(arrays),
        out_specs=pl.BlockSpec((16, 128), lambda i: (0, 0)),
        cost_estimate=pl.CostEstimate(
            flops=100_000_000_000, bytes_accessed=100_000_000, transcendentals=0
        ),
        name="marker",
    )(*arrays)


def attend_body(count_ref, parts, text, mark, out, keys, values, queries):
    blocks, _, rows = parts.shape
    text_blocks = text.shape[1] // rows
    text_len = 154
    tile = 2 * rows
    lane = lax.broadcasted_iota(jnp.int32, (8, rows), 1)
    row = lax.broadcasted_iota(jnp.int32, (8, rows), 0)
    top = row == 0
    zeros = jnp.zeros((HEAD - 8, rows), F32)

    def place_keys(index, key_part, limit):
        bias = jnp.where(jnp.logical_and(top, lane >= limit), masked_score, 0.0)
        full = jnp.concatenate([key_part.astype(F32), bias, zeros], axis=0)
        keys[pl.ds(index * rows, rows), :] = full.T.astype(BF16)

    ones = jnp.concatenate([jnp.where(top, 1.0, 0.0).astype(F32), zeros], axis=0)
    for b in range(blocks):
        part = parts[b]
        place_keys(b, part[HEAD : 2 * HEAD], count_ref[0] - b * rows)
        values[:, b * rows : (b + 1) * rows] = part[2 * HEAD :]
        scaled = part[:HEAD].astype(F32) * 0.125
        queries[:, b * rows : (b + 1) * rows] = jnp.concatenate([scaled, ones], axis=0).astype(BF16)
    for t in range(text_blocks):
        cols = slice(t * rows, (t + 1) * rows)
        place_keys(blocks + t, text[:HEAD, cols], text_len - t * rows)
        values[:, (blocks + t) * rows : (blocks + t + 1) * rows] = text[HEAD:, cols]

    def step(t, carry):
        first = pl.multiple_of(t * tile, tile)
        scores = jnp.dot(keys[...], queries[:, pl.ds(first, tile)], preferred_element_type=F32)
        top_score = jnp.max(scores, axis=0, keepdims=True)
        numer = jnp.exp(scores - top_score)
        total = jnp.sum(numer, axis=0, keepdims=True)
        mixed = jnp.dot(values[...], numer.astype(BF16), preferred_element_type=F32) / total
        mixed = mixed.astype(BF16)
        out[2 * t] = mixed[:, :rows]
        out[2 * t + 1] = mixed[:, rows:]
        return carry

    lax.fori_loop(0, blocks // 2, step, 0)


def attend(count, parts, text, mark):
    blocks, _, rows = parts.shape
    keys = blocks * rows + text.shape[1]
    queries = blocks * rows
    return pl.pallas_call(
        attend_body,
        out_shape=jax.ShapeDtypeStruct((blocks, HEAD, rows), BF16),
        in_specs=[pl.BlockSpec(memory_space=pltpu.SMEM)] + vmem_specs(3),
        out_specs=vmem_specs(1)[0],
        scratch_shapes=[
            pltpu.VMEM((keys, 2 * HEAD), BF16),
            pltpu.VMEM((HEAD, keys), BF16),
            pltpu.VMEM((2 * HEAD, queries), BF16),
        ],
        compiler_params=pltpu.CompilerParams(vmem_limit_bytes=40 << 20),
        cost_estimate=pl.CostEstimate(flops=1000, bytes_accessed=1000, transcendentals=0),
        name="attend",
    )(count, parts, text, mark)


def layer_norm(values, shift_row, scale_row):
    center = jnp.mean(values, axis=-1, keepdims=True)
    spread = jnp.mean(jnp.square(values - center), axis=-1, keepdims=True)
    normed = (values - center) * lax.rsqrt(spread + norm_eps)
    return (normed * (1.0 + scale_row) + shift_row).astype(BF16)


def gelu(v):
    return 0.5 * v * (1.0 + jnp.tanh(0.7978845608028654 * (v + 0.044715 * v * v * v)))


def middle_body(mixed, hidden, mods, out_w, updated, mlp_in):
    attended = mixed[...].astype(F32).T.astype(BF16)
    projected = jnp.dot(attended, out_w[...], preferred_element_type=F32)
    now = hidden[...].astype(F32) + mods[2:3] * projected
    updated[...] = now
    mlp_in[...] = layer_norm(now, mods[3:4], mods[4:5])


def middle(mixed, hidden, mods, out_w):
    rows, width = hidden.shape
    return pl.pallas_call(
        middle_body,
        out_shape=(
            jax.ShapeDtypeStruct((rows, width), F32),
            jax.ShapeDtypeStruct((rows, width), BF16),
        ),
        in_specs=vmem_specs(4),
        out_specs=tuple(vmem_specs(2)),
        compiler_params=pltpu.CompilerParams(vmem_limit_bytes=24 << 20),
        cost_estimate=pl.CostEstimate(flops=1000, bytes_accessed=1000, transcendentals=0),
        name="middle",
    )(mixed, hidden, mods, out_w)


def first_body(chip_ref, own_x, peer_x, *refs):
    weights, out = refs[:-1], refs[-1]
    both = jnp.concatenate([own_x[...], peer_x[...]], axis=0)
    cols = out.shape[1]
    stacked = jnp.concatenate([weight[:cols] for weight in weights], axis=0)
    parts = lax.dot_general(stacked, both, (((1,), (1,)), ((), ())), preferred_element_type=F32)
    for k in range(len(weights)):
        out[place_of(chip_ref[0], k)] = gelu(parts[k * cols : (k + 1) * cols]).astype(BF16)


def mlp_first(chip, own_x, peer_x, weights, cols):
    rows = own_x.shape[0]
    count = len(weights)
    return pl.pallas_call(
        first_body,
        out_shape=jax.ShapeDtypeStruct((count, cols, 2 * rows), BF16),
        in_specs=[pl.BlockSpec(memory_space=pltpu.SMEM)] + vmem_specs(2 + count),
        out_specs=vmem_specs(1)[0],
        compiler_params=pltpu.CompilerParams(vmem_limit_bytes=32 << 20),
        cost_estimate=pl.CostEstimate(flops=1000, bytes_accessed=1000, transcendentals=0),
        name="mlp_first",
    )(chip, own_x, peer_x, *weights)


def second_body(chip_ref, core_ref, own_act, peer_act, *refs):
    weights, (own_out, peer_out), act = refs[:-3], refs[-3:-1], refs[-1]
    count, cols, tokens = own_act.shape
    mid = tokens // 2
    core = core_ref[0]
    for c in range(count):
        mine = pl.ds(pl.multiple_of((2 * c + core) * cols, cols), cols)
        act[mine, :] = own_act[c]
        other = pl.ds(pl.multiple_of((2 * c + 1 - core) * cols, cols), cols)
        act[other, :mid] = peer_act[c, :, mid:]
        act[other, mid:] = peer_act[c, :, :mid]
    width = weights[0].shape[1]
    half = cols // 2
    low = jnp.concatenate([weight[cols : cols + half] for weight in weights], axis=0)
    parts = jnp.dot(low, act[:width], preferred_element_type=F32)
    high = jnp.concatenate([weight[cols + half :] for weight in weights], axis=0)
    parts += jnp.dot(high, act[width:], preferred_element_type=F32)
    for k in range(count):
        place = place_of(chip_ref[0], k)
        own_out[place] = parts[k * half : (k + 1) * half, :mid]
        peer_out[place] = parts[k * half : (k + 1) * half, mid:]


def mlp_second(chip, core, own_act, peer_act, weights):
    count, cols, tokens = own_act.shape
    shape = jax.ShapeDtypeStruct((count, cols // 2, tokens // 2), F32)
    return pl.pallas_call(
        second_body,
        out_shape=(shape, shape),
        in_specs=[pl.BlockSpec(memory_space=pltpu.SMEM)] * 2 + vmem_specs(2 + count),
        out_specs=tuple(vmem_specs(2)),
        scratch_shapes=[pltpu.VMEM((2 * count * cols, tokens), BF16)],
        compiler_params=pltpu.CompilerParams(vmem_limit_bytes=40 << 20),
        cost_estimate=pl.CostEstimate(flops=1000, bytes_accessed=1000, transcendentals=0),
        name="mlp_second",
    )(chip, core, own_act, peer_act, *weights)


def last_body(core_ref, own_part, peer_part, updated, mods, finals, final_t, predicted, mlp_t):
    count, half, _ = own_part.shape
    for source, parity in ((own_part, core_ref[0]), (peer_part, 1 - core_ref[0])):
        for c in range(count):
            start = pl.multiple_of((2 * c + parity) * half, half)
            mlp_t[pl.ds(start, half), :] = source[c]
    refined = updated[...] + mods[5:6] * mlp_t[...].T
    final_in = layer_norm(refined, finals[0:1], finals[1:2])
    predicted[...] = lax.dot_general(
        final_in, final_t[...], (((1,), (1,)), ((), ())), preferred_element_type=F32
    )


def last(core, own_part, peer_part, updated, mods, finals, final_t):
    rows, width = updated.shape
    return pl.pallas_call(
        last_body,
        out_shape=jax.ShapeDtypeStruct((rows, final_t.shape[0]), F32),
        in_specs=[pl.BlockSpec(memory_space=pltpu.SMEM)] + vmem_specs(6),
        out_specs=vmem_specs(1)[0],
        scratch_shapes=[pltpu.VMEM((width, rows), F32)],
        compiler_params=pltpu.CompilerParams(vmem_limit_bytes=24 << 20),
        cost_estimate=pl.CostEstimate(flops=1000, bytes_accessed=1000, transcendentals=0),
        name="last",
    )(core, own_part, peer_part, updated, mods, finals, final_t)


def padded(x, axis, width):
    size, length = lax.axis_size(axis), x.shape[0]
    up = [(i, i + 1) for i in range(size - 1)]
    down = [(j, i) for i, j in up]
    before = lax.ppermute(x[length - width :], axis, up)
    after = lax.ppermute(x[:width], axis, down)
    return jnp.concatenate([before, x, after], axis=0)


def per_device(
    hidden,
    text_hidden,
    latent,
    image_mod,
    text_mod,
    final_mod,
    counts,
    step_index,
    qkv_weight,
    text_weight,
    out_weight,
    mlp_in_weight,
    mlp_out_weight,
    final_weight,
    conv_weight,
    conv_bias,
):
    tok_rows, width = hidden.shape[1:]
    width_attn = HEADS * HEAD
    blocks = lax.axis_size("blk")
    blk, img = lax.axis_index("blk"), lax.axis_index("img")
    chip, core = img // 2, img % 2
    mods = image_mod[0]
    chip, core = chip[None], core[None]

    qkv_t = qkv_weight.T
    mlp_mine = jnp.concatenate(
        [mlp_in_weight.T, mlp_out_weight[:width].T, mlp_out_weight[width:].T], axis=0
    )
    image_in = modulate(hidden[0], mods[0], mods[1])
    mlp_mine, image_in = lax.optimization_barrier((mlp_mine, image_in))
    qkv_near = ring_first(qkv_t)
    qkv_next = ring_second(*qkv_near)
    qkv_far = ring_third(*qkv_next[:2])
    qkv_left, qkv_right, mlp_mine = lax.optimization_barrier((*qkv_next[2:], mlp_mine))
    qkv_pieces = [qkv_t, *qkv_near, qkv_far[0], *qkv_next[2:], qkv_far[1]]
    mlp_near = ring_first(mlp_mine)

    peer_in = swap(image_in, "img", 1)
    mine, theirs = project_qkv(chip, image_in, peer_in, qkv_pieces)
    other = swap(theirs, "img", 1)
    first = jnp.where(core[0] == 0, mine, other)
    second = jnp.where(core[0] == 0, other, mine)
    qkv = jnp.stack([first, second], axis=1).reshape(3, HEADS, HEAD, tok_rows)
    heads = qkv.transpose(1, 0, 2, 3).reshape(HEADS, 3 * HEAD, tok_rows)
    heads = jnp.pad(heads, ((0, blocks - HEADS), (0, 0), (0, 0)))
    parts = lax.all_to_all(heads, "blk", 0, 0, tiled=True)

    head = jnp.minimum(blk, HEADS - 1)
    text_in = modulate(text_hidden[0], text_mod[0, 0], text_mod[0, 1])
    text_cols = jnp.concatenate(
        [
            lax.dynamic_slice(text_weight, (0, start + head * HEAD), (width, HEAD))
            for start in (0, width_attn)
        ],
        axis=1,
    )
    text_kv = lax.dot_general(
        text_cols, text_in, (((0,), (1,)), ((), ())), preferred_element_type=F32
    ).astype(BF16)
    text_kv = jnp.pad(text_kv, ((0, 0), (0, -text_kv.shape[1] % tok_rows)))

    mlp_next = ring_second(*mlp_near)
    mark = marker(text_kv, *mlp_near)
    mixed = attend(counts, parts, text_kv, mark)
    mixed, low, high = lax.optimization_barrier((mixed, mlp_next[0], mlp_next[1]))
    mlp_far = ring_third(low, high)
    mixed = lax.all_to_all(mixed, "blk", 0, 0, tiled=True)[:HEADS].reshape(width_attn, tok_rows)
    mlp_pieces = [mlp_mine, *mlp_near, mlp_far[0], *mlp_next[2:], mlp_far[1]]

    updated, mlp_in = middle(mixed, hidden[0], mods, out_weight)
    mlp_cols = mlp_in_weight.shape[1]
    act = mlp_first(chip, mlp_in, swap(mlp_in, "img", 1), mlp_pieces, mlp_cols)
    peer_act = swap(act, "img", 1)
    own_part, sent_part = mlp_second(chip, core, act, peer_act, mlp_pieces)
    peer_part = swap(sent_part, "img", 1)
    predicted = last(core, own_part, peer_part, updated, mods, final_mod[0], final_weight.T)

    patch_count = counts[0]
    patch_rows = tok_rows // W_P
    lat_rows = 2 * patch_rows
    vel_lat = (
        predicted.reshape(patch_rows, W_P, 2, 2, CH)
        .transpose(0, 2, 1, 3, 4)
        .reshape(lat_rows, 2 * W_P * CH)
    )
    global_rows = blk * lat_rows + jnp.arange(lat_rows, dtype=jnp.int32)
    live_rows = (global_rows < 2 * (patch_count // W_P))[:, None]
    velocity = jnp.where(live_rows, vel_lat, 0.0)
    step_value = step_index[0].astype(F32)
    sigma_gap = plan(step_value + 1.0) - plan(step_value)
    next_lat = jnp.where(live_rows, latent[0] + sigma_gap * vel_lat, 0.0)
    scaled = jnp.where(live_rows, next_lat / vae_scale + vae_offset, 0.0).astype(BF16)
    framed = padded(scaled, "blk", 1)
    padded_grid = jnp.pad(framed.reshape(lat_rows + 2, 2 * W_P, CH), ((0, 0), (1, 1), (0, 0)))
    columns = jnp.concatenate(
        [
            padded_grid[row_off : row_off + lat_rows, col_off : col_off + 2 * W_P, :]
            for row_off in range(3)
            for col_off in range(3)
        ],
        axis=-1,
    ).reshape(lat_rows * 2 * W_P, 9 * CH)
    feature = jnp.dot(columns, conv_weight, preferred_element_type=F32) + conv_bias
    feature = jnp.where(live_rows[:, :, None], feature.reshape(lat_rows, 2 * W_P, -1), 0.0).astype(
        BF16
    )
    return (velocity[None], next_lat[None], feature[None])


def solution(mesh):
    placed = (
        P("img", "blk", None),
        P("img", None, None),
        P("img", "blk", None),
        P("img", None, None),
        P("img", None, None),
        P("img", None, None),
        P("img"),
        P("img"),
        P(None, "img"),
        P(),
        P(),
        P(None, "img"),
        P(None, "img"),
        P(),
        P(),
        P(),
    )
    return jax.shard_map(
        per_device,
        mesh=mesh,
        in_specs=placed,
        out_specs=(P("img", "blk", None), P("img", "blk", None), P("img", "blk", None, None)),
        check_vma=False,
    )
```

```python
import jax
import jax.numpy as jnp
from jax import lax
from jax.experimental import pallas as pl
from jax.experimental.pallas import tpu as pltpu
from jax.sharding import PartitionSpec as P

HEAD = 64
CH = 16
HEADS = 12
W_P = 64
STEPS = 8

norm_eps = 1e-06
sigma_shift = 3.0
vae_scale = 1.5305
vae_offset = 0.0609
masked_score = -1e30

F32 = jnp.float32
BF16 = jnp.bfloat16


def modulate(inputs, shift_row, scale_row):
    values = inputs.astype(F32)
    center = jnp.mean(values, axis=-1, keepdims=True)
    spread = jnp.mean(jnp.square(values - center), axis=-1, keepdims=True)
    normed = (values - center) * lax.rsqrt(spread + norm_eps)
    return (normed * (1.0 + scale_row) + shift_row).astype(BF16)


def plan(step_value):
    remain = 1.0 - step_value / STEPS
    return sigma_shift * remain / (1.0 + (sigma_shift - 1.0) * remain)


def swap(x, axis, bits):
    return lax.ppermute(x, axis, [(i, i ^ bits) for i in range(lax.axis_size(axis))])


def vmem_specs(count):
    return [pl.BlockSpec(memory_space=pltpu.VMEM)] * count


OFFSETS = ((0, 0), (-1, 0), (1, 0), (0, 1), (2, 0), (-1, 1), (1, 1), (2, 1))


def ring(x, axis, step):
    size = lax.axis_size(axis)
    return lax.ppermute(x, axis, [(i, (i + step) % size) for i in range(size)])


def ring_first(x):
    return ring(x, "img", 4), ring(x, "img", -4), swap(x, "img", 2)


def ring_second(left, right, across):
    half = left.shape[0] // 2
    return (
        ring(left[:half], "img", 4),
        ring(right[half:], "img", -4),
        ring(across, "img", 4),
        ring(across, "img", -4),
    )


def place_of(chip, k):
    dx, dy = OFFSETS[k]
    column = jnp.bitwise_and(chip // 2 + dx + 4, 3)
    return 2 * column + jnp.bitwise_xor(jnp.bitwise_and(chip, 1), dy)


def qkv_body(chip_ref, ready, own_x, peer_x, *refs):
    weights, (own_out, peer_out) = refs[:-2], refs[-2:]
    rows = own_x.shape[0]
    both = jnp.concatenate([own_x[...], peer_x[...]], axis=0)
    cols = own_out.shape[1]
    stacked = jnp.concatenate([weight[...] for weight in weights], axis=0)
    parts = lax.dot_general(
        stacked, both, (((1,), (1,)), ((), ())), preferred_element_type=F32
    ).astype(BF16)
    for k in range(len(weights)):
        place = place_of(chip_ref[0], k)
        own_out[place] = parts[k * cols : (k + 1) * cols, :rows]
        peer_out[place] = parts[k * cols : (k + 1) * cols, rows:]


def project_qkv(chip, ready, own_x, peer_x, weights):
    cols, rows = weights[0].shape[0], own_x.shape[0]
    shape = jax.ShapeDtypeStruct((len(weights), cols, rows), BF16)
    flops = 4 * len(weights) * cols * rows * own_x.shape[1]
    return pl.pallas_call(
        qkv_body,
        out_shape=(shape, shape),
        in_specs=[pl.BlockSpec(memory_space=pltpu.SMEM)] + vmem_specs(3 + len(weights)),
        out_specs=tuple(vmem_specs(2)),
        compiler_params=pltpu.CompilerParams(vmem_limit_bytes=32 << 20),
        cost_estimate=pl.CostEstimate(flops=1000, bytes_accessed=1000, transcendentals=0),
        name="project_qkv",
    )(chip, ready, own_x, peer_x, *weights)


def heads_body(core_ref, mine, other, out):
    count, cols, _ = mine.shape
    step = 16
    per_shard, per_head = cols // step, HEAD // step
    section = HEADS * per_head
    for source, parity in ((mine, core_ref[0]), (other, 1 - core_ref[0])):
        for c in range(count):
            for j in range(per_shard):
                piece = (2 * c + parity) * per_shard + j
                kind = (piece >= section).astype(jnp.int32) + (piece >= 2 * section).astype(jnp.int32)
                rest = piece - kind * section
                head = rest // per_head
                start = pl.multiple_of(kind * HEAD + (rest - head * per_head) * step, step)
                out[head, pl.ds(start, step), :] = source[c, j * step : (j + 1) * step]
    out[HEADS:] = jnp.zeros((out.shape[0] - HEADS,) + out.shape[1:], BF16)


def place_heads(core, mine, other, blocks):
    return pl.pallas_call(
        heads_body,
        out_shape=jax.ShapeDtypeStruct((blocks, 3 * HEAD, mine.shape[2]), BF16),
        in_specs=[pl.BlockSpec(memory_space=pltpu.SMEM)] + vmem_specs(2),
        out_specs=vmem_specs(1)[0],
        cost_estimate=pl.CostEstimate(flops=1000, bytes_accessed=1000, transcendentals=0),
        name="place_heads",
    )(core, mine, other)


def mark_body(*refs):
    refs[-1][...] = refs[0][...]


def marker(*arrays):
    return pl.pallas_call(
        mark_body,
        out_shape=jax.ShapeDtypeStruct((16, 128), BF16),
        grid=(1,),
        in_specs=[pl.BlockSpec((16, 128), lambda i: (0, 0))] * len(arrays),
        out_specs=pl.BlockSpec((16, 128), lambda i: (0, 0)),
        cost_estimate=pl.CostEstimate(
            flops=100_000_000_000, bytes_accessed=100_000_000, transcendentals=0
        ),
        name="marker",
    )(*arrays)


def attend_body(count_ref, parts, text, mark, out, keys, values, queries):
    blocks, _, rows = parts.shape
    text_blocks = text.shape[1] // rows
    text_len = 154
    tile = 2 * rows
    lane = lax.broadcasted_iota(jnp.int32, (HEAD, rows), 1)
    row = lax.broadcasted_iota(jnp.int32, (HEAD, rows), 0)
    top = row == 0
    zeros = jnp.zeros((HEAD, rows), F32)
    ones = jnp.where(top, 1.0, 0.0).astype(F32)

    def place(index, key_part, value_part, limit):
        cols = slice(index * rows, (index + 1) * rows)
        keys[:HEAD, cols] = key_part
        bias = jnp.where(jnp.logical_and(top, lane >= limit), masked_score, 0.0)
        keys[HEAD:, cols] = bias.astype(BF16)
        full = jnp.concatenate([value_part.astype(F32), zeros], axis=0)
        values[cols, :] = full.T.astype(BF16)

    for b in range(blocks):
        part = parts[b]
        place(b, part[HEAD : 2 * HEAD], part[2 * HEAD :], count_ref[0] - b * rows)
        scaled = part[:HEAD].astype(F32) * 0.125
        full = jnp.concatenate([scaled, ones], axis=0)
        queries[b * rows : (b + 1) * rows, :] = full.T.astype(BF16)
    for t in range(text_blocks):
        cols = slice(t * rows, (t + 1) * rows)
        place(blocks + t, text[:HEAD, cols], text[HEAD:, cols], text_len - t * rows)

    def step(t, carry):
        first = pl.multiple_of(t * tile, tile)
        scores = jnp.dot(queries[pl.ds(first, tile), :], keys[...], preferred_element_type=F32)
        top_score = jnp.max(scores, axis=1, keepdims=True)
        numer = jnp.exp(scores - top_score)
        total = jnp.sum(numer, axis=1, keepdims=True)
        mixed = jnp.dot(numer.astype(BF16), values[...], preferred_element_type=F32) / total
        turned = mixed.T[:HEAD].astype(BF16)
        out[2 * t] = turned[:, :rows]
        out[2 * t + 1] = turned[:, rows:]
        return carry

    lax.fori_loop(0, blocks // 2, step, 0)


def attend(count, parts, text, mark):
    blocks, _, rows = parts.shape
    keys = blocks * rows + text.shape[1]
    queries = blocks * rows
    return pl.pallas_call(
        attend_body,
        out_shape=jax.ShapeDtypeStruct((blocks, HEAD, rows), BF16),
        in_specs=[pl.BlockSpec(memory_space=pltpu.SMEM)] + vmem_specs(3),
        out_specs=vmem_specs(1)[0],
        scratch_shapes=[
            pltpu.VMEM((2 * HEAD, keys), BF16),
            pltpu.VMEM((keys, 2 * HEAD), BF16),
            pltpu.VMEM((queries, 2 * HEAD), BF16),
        ],
        compiler_params=pltpu.CompilerParams(vmem_limit_bytes=40 << 20),
        cost_estimate=pl.CostEstimate(flops=1000, bytes_accessed=1000, transcendentals=0),
        name="attend",
    )(count, parts, text, mark)


def layer_norm(values, shift_row, scale_row):
    center = jnp.mean(values, axis=-1, keepdims=True)
    spread = jnp.mean(jnp.square(values - center), axis=-1, keepdims=True)
    normed = (values - center) * lax.rsqrt(spread + norm_eps)
    return (normed * (1.0 + scale_row) + shift_row).astype(BF16)


def gelu(v):
    return 0.5 * v * (1.0 + jnp.tanh(0.7978845608028654 * (v + 0.044715 * v * v * v)))


def middle_body(mixed, hidden, mods, out_w, mark, updated, mlp_in):
    attended = mixed[...].astype(F32).T.astype(BF16)
    projected = jnp.dot(attended, out_w[...], preferred_element_type=F32)
    now = hidden[...].astype(F32) + mods[2:3] * projected
    updated[...] = now
    mlp_in[...] = layer_norm(now, mods[3:4], mods[4:5])


def middle(mixed, hidden, mods, out_w, mark):
    rows, width = hidden.shape
    return pl.pallas_call(
        middle_body,
        out_shape=(
            jax.ShapeDtypeStruct((rows, width), F32),
            jax.ShapeDtypeStruct((rows, width), BF16),
        ),
        in_specs=vmem_specs(5),
        out_specs=tuple(vmem_specs(2)),
        compiler_params=pltpu.CompilerParams(vmem_limit_bytes=24 << 20),
        cost_estimate=pl.CostEstimate(flops=1000, bytes_accessed=1000, transcendentals=0),
        name="middle",
    )(mixed, hidden, mods, out_w, mark)


def first_body(chip_ref, own_x, peer_x, *refs):
    weights, out = refs[:-1], refs[-1]
    both = jnp.concatenate([own_x[...], peer_x[...]], axis=0)
    cols = out.shape[1]
    stacked = jnp.concatenate([weight[...] for weight in weights], axis=0)
    parts = lax.dot_general(stacked, both, (((1,), (1,)), ((), ())), preferred_element_type=F32)
    for k in range(len(weights)):
        out[place_of(chip_ref[0], k)] = gelu(parts[k * cols : (k + 1) * cols]).astype(BF16)


def whole(x):
    return pl.BlockSpec(x.shape, lambda i: (0,) * x.ndim)


def half_of(x, cols, index):
    position = index if x.shape[0] > cols else 0
    return pl.BlockSpec((cols, x.shape[1]), lambda i: (position, 0))


def mlp_first(chip, own_x, peer_x, weights, cols):
    rows = own_x.shape[0]
    count = len(weights)
    shape = (count, cols, 2 * rows)
    return pl.pallas_call(
        first_body,
        out_shape=jax.ShapeDtypeStruct(shape, BF16),
        grid=(1,),
        in_specs=[pl.BlockSpec(memory_space=pltpu.SMEM), whole(own_x), whole(peer_x)]
        + [half_of(x, cols, 0) for x in weights],
        out_specs=pl.BlockSpec(shape, lambda i: (0, 0, 0)),
        compiler_params=pltpu.CompilerParams(vmem_limit_bytes=40 << 20),
        cost_estimate=pl.CostEstimate(flops=1000, bytes_accessed=1000, transcendentals=0),
        name="mlp_first",
    )(chip, own_x, peer_x, *weights)


def second_body(chip_ref, core_ref, own_act, peer_act, *refs):
    weights, (own_out, peer_out), act = refs[:-3], refs[-3:-1], refs[-1]
    count, cols, tokens = own_act.shape
    mid = tokens // 2
    core = core_ref[0]
    for c in range(count):
        mine = pl.ds(pl.multiple_of((2 * c + core) * cols, cols), cols)
        act[mine, :] = own_act[c]
        other = pl.ds(pl.multiple_of((2 * c + 1 - core) * cols, cols), cols)
        act[other, :mid] = peer_act[c, :, mid:]
        act[other, mid:] = peer_act[c, :, :mid]
    width = weights[0].shape[1]
    half = cols // 2
    low = jnp.concatenate([weight[:half] for weight in weights], axis=0)
    parts = jnp.dot(low, act[:width], preferred_element_type=F32)
    high = jnp.concatenate([weight[half:] for weight in weights], axis=0)
    parts += jnp.dot(high, act[width:], preferred_element_type=F32)
    for k in range(count):
        place = place_of(chip_ref[0], k)
        own_out[place] = parts[k * half : (k + 1) * half, :mid]
        peer_out[place] = parts[k * half : (k + 1) * half, mid:]


def mlp_second(chip, core, own_act, peer_act, weights):
    count, cols, tokens = own_act.shape
    shape = (count, cols // 2, tokens // 2)
    return pl.pallas_call(
        second_body,
        out_shape=(jax.ShapeDtypeStruct(shape, F32), jax.ShapeDtypeStruct(shape, F32)),
        grid=(1,),
        in_specs=[pl.BlockSpec(memory_space=pltpu.SMEM)] * 2
        + [whole(own_act), whole(peer_act)]
        + [half_of(x, cols, 1) for x in weights],
        out_specs=(pl.BlockSpec(shape, lambda i: (0, 0, 0)),) * 2,
        scratch_shapes=[pltpu.VMEM((2 * count * cols, tokens), BF16)],
        compiler_params=pltpu.CompilerParams(vmem_limit_bytes=40 << 20),
        cost_estimate=pl.CostEstimate(flops=1000, bytes_accessed=1000, transcendentals=0),
        name="mlp_second",
    )(chip, core, own_act, peer_act, *weights)


def last_body(core_ref, own_part, peer_part, updated, mods, finals, final_t, predicted, mlp_t):
    count, half, _ = own_part.shape
    for source, parity in ((own_part, core_ref[0]), (peer_part, 1 - core_ref[0])):
        for c in range(count):
            start = pl.multiple_of((2 * c + parity) * half, half)
            mlp_t[pl.ds(start, half), :] = source[c]
    refined = updated[...] + mods[5:6] * mlp_t[...].T
    final_in = layer_norm(refined, finals[0:1], finals[1:2])
    predicted[...] = lax.dot_general(
        final_in, final_t[...], (((1,), (1,)), ((), ())), preferred_element_type=F32
    )


def last(core, own_part, peer_part, updated, mods, finals, final_t):
    rows, width = updated.shape
    return pl.pallas_call(
        last_body,
        out_shape=jax.ShapeDtypeStruct((rows, final_t.shape[0]), F32),
        in_specs=[pl.BlockSpec(memory_space=pltpu.SMEM)] + vmem_specs(6),
        out_specs=vmem_specs(1)[0],
        scratch_shapes=[pltpu.VMEM((width, rows), F32)],
        compiler_params=pltpu.CompilerParams(vmem_limit_bytes=24 << 20),
        cost_estimate=pl.CostEstimate(flops=1000, bytes_accessed=1000, transcendentals=0),
        name="last",
    )(core, own_part, peer_part, updated, mods, finals, final_t)


def padded(x, axis, width):
    size, length = lax.axis_size(axis), x.shape[0]
    up = [(i, i + 1) for i in range(size - 1)]
    down = [(j, i) for i, j in up]
    before = lax.ppermute(x[length - width :], axis, up)
    after = lax.ppermute(x[:width], axis, down)
    return jnp.concatenate([before, x, after], axis=0)


def per_device(
    hidden,
    text_hidden,
    latent,
    image_mod,
    text_mod,
    final_mod,
    counts,
    step_index,
    qkv_weight,
    text_weight,
    out_weight,
    mlp_in_weight,
    mlp_out_weight,
    final_weight,
    conv_weight,
    conv_bias,
):
    tok_rows, width = hidden.shape[1:]
    width_attn = HEADS * HEAD
    blocks = lax.axis_size("blk")
    blk, img = lax.axis_index("blk"), lax.axis_index("img")
    chip, core = img // 2, img % 2
    mods = image_mod[0]
    chip, core = chip[None], core[None]

    qkv_t = qkv_weight.T
    mlp_mine = jnp.concatenate(
        [mlp_in_weight.T, mlp_out_weight[:width].T, mlp_out_weight[width:].T], axis=0
    )
    image_in = modulate(hidden[0], mods[0], mods[1])
    mlp_mine, image_in = lax.optimization_barrier((mlp_mine, image_in))
    qkv_near = ring_first(qkv_t)
    qkv_next = ring_second(*qkv_near)
    far = jnp.concatenate(qkv_next[:2], axis=0)
    side_left, side_right, mlp_mine = lax.optimization_barrier((*qkv_next[2:], mlp_mine))
    qkv_far = far, swap(far, "img", 2)
    qkv_pieces = [qkv_t, *qkv_near, qkv_far[0], *qkv_next[2:], qkv_far[1]]
    mlp_near = ring_first(mlp_mine)

    peer_in = swap(image_in, "img", 1)
    ready, peer_in = lax.optimization_barrier((marker(qkv_far[1]), peer_in))
    mine, theirs = project_qkv(chip, ready, image_in, peer_in, qkv_pieces)
    other = swap(theirs, "img", 1)
    heads = place_heads(core, mine, other, blocks)
    parts = lax.all_to_all(heads, "blk", 0, 0, tiled=True)

    head = jnp.minimum(blk, HEADS - 1)
    right, head = lax.optimization_barrier((mlp_near[1], head))
    mlp_near = (mlp_near[0], right, mlp_near[2])
    text_in = modulate(text_hidden[0], text_mod[0, 0], text_mod[0, 1])
    text_cols = jnp.concatenate(
        [
            lax.dynamic_slice(text_weight, (0, start + head * HEAD), (width, HEAD))
            for start in (0, width_attn)
        ],
        axis=1,
    )
    text_kv = lax.dot_general(
        text_cols, text_in, (((0,), (1,)), ((), ())), preferred_element_type=F32
    ).astype(BF16)
    text_kv = jnp.pad(text_kv, ((0, 0), (0, -text_kv.shape[1] % tok_rows)))

    mlp_next = ring_second(*mlp_near)
    mark = marker(*mlp_near)
    parts, low, high, mark, text_kv = lax.optimization_barrier(
        (parts, mlp_next[0], mlp_next[1], mark, text_kv)
    )
    peer_low, peer_high = swap(low, "img", 2), swap(high, "img", 2)
    mixed = attend(counts, parts, text_kv, mark)
    mixed = lax.all_to_all(mixed, "blk", 0, 0, tiled=True)[:HEADS].reshape(width_attn, tok_rows)
    near_pieces, next_pieces = [mlp_mine, *mlp_near], list(mlp_next[2:])

    updated, mlp_in = middle(mixed, hidden[0], mods, out_weight, marker(peer_low, peer_high, *next_pieces))
    mlp_cols = mlp_in_weight.shape[1]
    peer_mlp = swap(mlp_in, "img", 1)
    first_pieces = near_pieces + [low] + next_pieces + [peer_low]
    act = mlp_first(chip, mlp_in, peer_mlp, first_pieces, mlp_cols)
    peer_act = swap(act, "img", 1)
    own_part, sent_part = mlp_second(
        chip, core, act, peer_act, near_pieces + [high] + next_pieces + [peer_high]
    )
    peer_part = swap(sent_part, "img", 1)
    predicted = last(core, own_part, peer_part, updated, mods, final_mod[0], final_weight.T)

    patch_count = counts[0]
    patch_rows = tok_rows // W_P
    lat_rows = 2 * patch_rows
    vel_lat = (
        predicted.reshape(patch_rows, W_P, 2, 2, CH)
        .transpose(0, 2, 1, 3, 4)
        .reshape(lat_rows, 2 * W_P * CH)
    )
    global_rows = blk * lat_rows + jnp.arange(lat_rows, dtype=jnp.int32)
    live_rows = (global_rows < 2 * (patch_count // W_P))[:, None]
    velocity = jnp.where(live_rows, vel_lat, 0.0)
    step_value = step_index[0].astype(F32)
    sigma_gap = plan(step_value + 1.0) - plan(step_value)
    next_lat = jnp.where(live_rows, latent[0] + sigma_gap * vel_lat, 0.0)
    scaled = jnp.where(live_rows, next_lat / vae_scale + vae_offset, 0.0).astype(BF16)
    framed = padded(scaled, "blk", 1)
    padded_grid = jnp.pad(framed.reshape(lat_rows + 2, 2 * W_P, CH), ((0, 0), (1, 1), (0, 0)))
    columns = jnp.concatenate(
        [
            padded_grid[row_off : row_off + lat_rows, col_off : col_off + 2 * W_P, :]
            for row_off in range(3)
            for col_off in range(3)
        ],
        axis=-1,
    ).reshape(lat_rows * 2 * W_P, 9 * CH)
    feature = jnp.dot(columns, conv_weight, preferred_element_type=F32) + conv_bias
    feature = jnp.where(live_rows[:, :, None], feature.reshape(lat_rows, 2 * W_P, -1), 0.0).astype(
        BF16
    )
    return (velocity[None], next_lat[None], feature[None])


def solution(mesh):
    placed = (
        P("img", "blk", None),
        P("img", None, None),
        P("img", "blk", None),
        P("img", None, None),
        P("img", None, None),
        P("img", None, None),
        P("img"),
        P("img"),
        P(None, "img"),
        P(),
        P(),
        P(None, "img"),
        P(None, "img"),
        P(),
        P(),
        P(),
    )
    return jax.shard_map(
        per_device,
        mesh=mesh,
        in_specs=placed,
        out_specs=(P("img", "blk", None), P("img", "blk", None), P("img", "blk", None, None)),
        check_vma=False,
    )
```

```python
import jax
import jax.numpy as jnp
from jax import lax
from jax.experimental import pallas as pl
from jax.experimental.pallas import tpu as pltpu
from jax.sharding import PartitionSpec as P

HEAD = 64
CH = 16
HEADS = 12
W_P = 64
STEPS = 8

norm_eps = 1e-06
sigma_shift = 3.0
vae_scale = 1.5305
vae_offset = 0.0609
masked_score = -1e30

F32 = jnp.float32
BF16 = jnp.bfloat16


def modulate(inputs, shift_row, scale_row):
    values = inputs.astype(F32)
    center = jnp.mean(values, axis=-1, keepdims=True)
    spread = jnp.mean(jnp.square(values - center), axis=-1, keepdims=True)
    normed = (values - center) * lax.rsqrt(spread + norm_eps)
    return (normed * (1.0 + scale_row) + shift_row).astype(BF16)


def plan(step_value):
    remain = 1.0 - step_value / STEPS
    return sigma_shift * remain / (1.0 + (sigma_shift - 1.0) * remain)


def swap(x, axis, bits):
    return lax.ppermute(x, axis, [(i, i ^ bits) for i in range(lax.axis_size(axis))])


def vmem_specs(count):
    return [pl.BlockSpec(memory_space=pltpu.VMEM)] * count


def whole(x):
    return pl.BlockSpec(x.shape, lambda i: (0,) * x.ndim)


OFFSETS = ((0, 0), (-1, 0), (1, 0), (0, 1), (2, 0), (-1, 1), (1, 1), (2, 1))


def ring(x, axis, step):
    size = lax.axis_size(axis)
    return lax.ppermute(x, axis, [(i, (i + step) % size) for i in range(size)])


def ring_first(x):
    return ring(x, "img", 4), ring(x, "img", -4), swap(x, "img", 2)


def ring_second(left, right, across):
    half = left.shape[0] // 2
    return (
        ring(left[:half], "img", 4),
        ring(right[half:], "img", -4),
        ring(across, "img", 4),
        ring(across, "img", -4),
    )


def place_of(chip, k):
    dx, dy = OFFSETS[k]
    column = jnp.bitwise_and(chip // 2 + dx + 4, 3)
    return 2 * column + jnp.bitwise_xor(jnp.bitwise_and(chip, 1), dy)


def qkv_body(chip_ref, ready, own_x, peer_x, *refs):
    weights, (own_out, peer_out) = refs[:-2], refs[-2:]
    rows = own_x.shape[0]
    both = jnp.concatenate([own_x[...], peer_x[...]], axis=0)
    cols = own_out.shape[1]
    stacked = jnp.concatenate([weight[...] for weight in weights], axis=0)
    parts = lax.dot_general(
        stacked, both, (((1,), (1,)), ((), ())), preferred_element_type=F32
    ).astype(BF16)
    for k in range(len(weights)):
        place = place_of(chip_ref[0], k)
        own_out[place] = parts[k * cols : (k + 1) * cols, :rows]
        peer_out[place] = parts[k * cols : (k + 1) * cols, rows:]


def project_qkv(chip, ready, own_x, peer_x, weights):
    cols, rows = weights[0].shape[0], own_x.shape[0]
    shape = (len(weights), cols, rows)
    inputs = (ready, own_x, peer_x, *weights)
    return pl.pallas_call(
        qkv_body,
        out_shape=(jax.ShapeDtypeStruct(shape, BF16),) * 2,
        grid=(1,),
        in_specs=[pl.BlockSpec(memory_space=pltpu.SMEM)] + [whole(x) for x in inputs],
        out_specs=(pl.BlockSpec(shape, lambda i: (0, 0, 0)),) * 2,
        compiler_params=pltpu.CompilerParams(vmem_limit_bytes=20 << 20),
        cost_estimate=pl.CostEstimate(flops=1000, bytes_accessed=1000, transcendentals=0),
        name="project_qkv",
    )(chip, *inputs)


def heads_body(core_ref, mine, other, out):
    count, cols, _ = mine.shape
    step = 16
    per_shard, per_head = cols // step, HEAD // step
    section = HEADS * per_head

    def copy(sources):
        for c in range(count):
            for parity, source in enumerate(sources):
                for j in range(per_shard):
                    piece = (2 * c + parity) * per_shard + j
                    kind, rest = piece // section, piece % section
                    start = kind * HEAD + rest % per_head * step
                    rows = source[c, j * step : (j + 1) * step]
                    out[rest // per_head, start : start + step] = rows

    @pl.when(core_ref[0] == 0)
    def _():
        copy((mine, other))

    @pl.when(core_ref[0] != 0)
    def _():
        copy((other, mine))

    out[HEADS:] = jnp.zeros((out.shape[0] - HEADS,) + out.shape[1:], BF16)


def place_heads(core, mine, other, blocks):
    shape = (blocks, 3 * HEAD, mine.shape[2])
    return pl.pallas_call(
        heads_body,
        out_shape=jax.ShapeDtypeStruct(shape, BF16),
        grid=(1,),
        in_specs=[pl.BlockSpec(memory_space=pltpu.SMEM), whole(mine), whole(other)],
        out_specs=pl.BlockSpec(shape, lambda i: (0, 0, 0)),
        compiler_params=pltpu.CompilerParams(vmem_limit_bytes=6 << 20),
        cost_estimate=pl.CostEstimate(flops=1000, bytes_accessed=1000, transcendentals=0),
        name="place_heads",
    )(core, mine, other)


def mark_body(*refs):
    refs[-1][...] = refs[0][...]


def marker(*arrays):
    return pl.pallas_call(
        mark_body,
        out_shape=jax.ShapeDtypeStruct((16, 128), BF16),
        grid=(1,),
        in_specs=[pl.BlockSpec((16, 128), lambda i: (0, 0))] * len(arrays),
        out_specs=pl.BlockSpec((16, 128), lambda i: (0, 0)),
        compiler_params=pltpu.CompilerParams(vmem_limit_bytes=1 << 20),
        cost_estimate=pl.CostEstimate(
            flops=100_000_000_000, bytes_accessed=100_000_000, transcendentals=0
        ),
        name="marker",
    )(*arrays)


def attend_body(count_ref, parts, text, mark, out, keys, values, queries):
    blocks, _, rows = parts.shape
    text_blocks = text.shape[1] // rows
    text_len = 154
    tile = 2 * rows
    lane = lax.broadcasted_iota(jnp.int32, (HEAD, rows), 1)
    row = lax.broadcasted_iota(jnp.int32, (HEAD, rows), 0)
    top = row == 0
    zeros = jnp.zeros((HEAD, rows), F32)
    ones = jnp.where(top, 1.0, 0.0).astype(F32)

    def place(index, key_part, value_part, limit):
        cols = slice(index * rows, (index + 1) * rows)
        keys[:HEAD, cols] = key_part
        bias = jnp.where(jnp.logical_and(top, lane >= limit), masked_score, 0.0)
        keys[HEAD:, cols] = bias.astype(BF16)
        full = jnp.concatenate([value_part.astype(F32), zeros], axis=0)
        values[cols, :] = full.T.astype(BF16)

    for b in range(blocks):
        part = parts[b]
        place(b, part[HEAD : 2 * HEAD], part[2 * HEAD :], count_ref[0] - b * rows)
        scaled = part[:HEAD].astype(F32) * 0.125
        full = jnp.concatenate([scaled, ones], axis=0)
        queries[b * rows : (b + 1) * rows, :] = full.T.astype(BF16)
    for t in range(text_blocks):
        cols = slice(t * rows, (t + 1) * rows)
        place(blocks + t, text[:HEAD, cols], text[HEAD:, cols], text_len - t * rows)

    def step(t, carry):
        first = pl.multiple_of(t * tile, tile)
        scores = jnp.dot(queries[pl.ds(first, tile), :], keys[...], preferred_element_type=F32)
        top_score = jnp.max(scores, axis=1, keepdims=True)
        numer = jnp.exp(scores - top_score)
        total = jnp.sum(numer, axis=1, keepdims=True)
        mixed = jnp.dot(numer.astype(BF16), values[...], preferred_element_type=F32) / total
        turned = mixed.T[:HEAD].astype(BF16)
        out[2 * t] = turned[:, :rows]
        out[2 * t + 1] = turned[:, rows:]
        return carry

    lax.fori_loop(0, blocks // 2, step, 0)


def attend(count, parts, text, mark):
    blocks, _, rows = parts.shape
    keys = blocks * rows + text.shape[1]
    queries = blocks * rows
    return pl.pallas_call(
        attend_body,
        out_shape=jax.ShapeDtypeStruct((blocks, HEAD, rows), BF16),
        in_specs=[pl.BlockSpec(memory_space=pltpu.SMEM)] + vmem_specs(3),
        out_specs=vmem_specs(1)[0],
        scratch_shapes=[
            pltpu.VMEM((2 * HEAD, keys), BF16),
            pltpu.VMEM((keys, 2 * HEAD), BF16),
            pltpu.VMEM((queries, 2 * HEAD), BF16),
        ],
        compiler_params=pltpu.CompilerParams(vmem_limit_bytes=20 << 20),
        cost_estimate=pl.CostEstimate(flops=1000, bytes_accessed=1000, transcendentals=0),
        name="attend",
    )(count, parts, text, mark)


def layer_norm(values, shift_row, scale_row):
    center = jnp.mean(values, axis=-1, keepdims=True)
    spread = jnp.mean(jnp.square(values - center), axis=-1, keepdims=True)
    normed = (values - center) * lax.rsqrt(spread + norm_eps)
    return (normed * (1.0 + scale_row) + shift_row).astype(BF16)


def gelu(v):
    return 0.5 * v * (1.0 + jnp.tanh(0.7978845608028654 * (v + 0.044715 * v * v * v)))


def middle_body(mixed, hidden, mods, out_w, mark, updated, mlp_in):
    attended = mixed[...].astype(F32).T.astype(BF16)
    projected = jnp.dot(attended, out_w[...], preferred_element_type=F32)
    now = hidden[...].astype(F32) + mods[2:3] * projected
    updated[...] = now
    mlp_in[...] = layer_norm(now, mods[3:4], mods[4:5])


def middle(mixed, hidden, mods, out_w, mark):
    rows, width = hidden.shape
    return pl.pallas_call(
        middle_body,
        out_shape=(
            jax.ShapeDtypeStruct((rows, width), F32),
            jax.ShapeDtypeStruct((rows, width), BF16),
        ),
        in_specs=vmem_specs(5),
        out_specs=tuple(vmem_specs(2)),
        compiler_params=pltpu.CompilerParams(vmem_limit_bytes=14 << 20),
        cost_estimate=pl.CostEstimate(flops=1000, bytes_accessed=1000, transcendentals=0),
        name="middle",
    )(mixed, hidden, mods, out_w, mark)


def first_body(chip_ref, own_x, peer_x, *refs):
    weights, out = refs[:-1], refs[-1]
    both = jnp.concatenate([own_x[...], peer_x[...]], axis=0)
    cols = out.shape[1]
    stacked = jnp.concatenate([weight[...] for weight in weights], axis=0)
    parts = lax.dot_general(stacked, both, (((1,), (1,)), ((), ())), preferred_element_type=F32)
    for k in range(len(weights)):
        out[place_of(chip_ref[0], k)] = gelu(parts[k * cols : (k + 1) * cols]).astype(BF16)


def half_of(x, cols, index):
    position = index if x.shape[0] > cols else 0
    return pl.BlockSpec((cols, x.shape[1]), lambda i: (position, 0))


def mlp_first(chip, own_x, peer_x, weights, cols):
    rows = own_x.shape[0]
    count = len(weights)
    shape = (count, cols, 2 * rows)
    return pl.pallas_call(
        first_body,
        out_shape=jax.ShapeDtypeStruct(shape, BF16),
        grid=(1,),
        in_specs=[pl.BlockSpec(memory_space=pltpu.SMEM), whole(own_x), whole(peer_x)]
        + [half_of(x, cols, 0) for x in weights],
        out_specs=pl.BlockSpec(shape, lambda i: (0, 0, 0)),
        compiler_params=pltpu.CompilerParams(vmem_limit_bytes=28 << 20),
        cost_estimate=pl.CostEstimate(flops=1000, bytes_accessed=1000, transcendentals=0),
        name="mlp_first",
    )(chip, own_x, peer_x, *weights)


def second_body(chip_ref, core_ref, own_act, peer_act, *refs):
    weights, (own_out, peer_out), act = refs[:-3], refs[-3:-1], refs[-1]
    count, cols, tokens = own_act.shape
    mid = tokens // 2
    core = core_ref[0]
    for c in range(count):
        mine = pl.ds(pl.multiple_of((2 * c + core) * cols, cols), cols)
        act[mine, :] = own_act[c]
        other = pl.ds(pl.multiple_of((2 * c + 1 - core) * cols, cols), cols)
        act[other, :mid] = peer_act[c, :, mid:]
        act[other, mid:] = peer_act[c, :, :mid]
    width = weights[0].shape[1]
    half = cols // 2
    low = jnp.concatenate([weight[:half] for weight in weights], axis=0)
    parts = jnp.dot(low, act[:width], preferred_element_type=F32)
    high = jnp.concatenate([weight[half:] for weight in weights], axis=0)
    parts += jnp.dot(high, act[width:], preferred_element_type=F32)
    for k in range(count):
        place = place_of(chip_ref[0], k)
        own_out[place] = parts[k * half : (k + 1) * half, :mid]
        peer_out[place] = parts[k * half : (k + 1) * half, mid:]


def mlp_second(chip, core, own_act, peer_act, weights):
    count, cols, tokens = own_act.shape
    shape = (count, cols // 2, tokens // 2)
    return pl.pallas_call(
        second_body,
        out_shape=(jax.ShapeDtypeStruct(shape, F32), jax.ShapeDtypeStruct(shape, F32)),
        grid=(1,),
        in_specs=[pl.BlockSpec(memory_space=pltpu.SMEM)] * 2
        + [whole(own_act), whole(peer_act)]
        + [half_of(x, cols, 1) for x in weights],
        out_specs=(pl.BlockSpec(shape, lambda i: (0, 0, 0)),) * 2,
        scratch_shapes=[pltpu.VMEM((2 * count * cols, tokens), BF16)],
        compiler_params=pltpu.CompilerParams(vmem_limit_bytes=28 << 20),
        cost_estimate=pl.CostEstimate(flops=1000, bytes_accessed=1000, transcendentals=0),
        name="mlp_second",
    )(chip, core, own_act, peer_act, *weights)


def last_body(core_ref, own_part, peer_part, updated, mods, finals, final_t, predicted, mlp_t):
    count, half, _ = own_part.shape
    for source, parity in ((own_part, core_ref[0]), (peer_part, 1 - core_ref[0])):
        for c in range(count):
            start = pl.multiple_of((2 * c + parity) * half, half)
            mlp_t[pl.ds(start, half), :] = source[c]
    refined = updated[...] + mods[5:6] * mlp_t[...].T
    final_in = layer_norm(refined, finals[0:1], finals[1:2])
    predicted[...] = lax.dot_general(
        final_in, final_t[...], (((1,), (1,)), ((), ())), preferred_element_type=F32
    )


def last(core, own_part, peer_part, updated, mods, finals, final_t):
    rows, width = updated.shape
    return pl.pallas_call(
        last_body,
        out_shape=jax.ShapeDtypeStruct((rows, final_t.shape[0]), F32),
        in_specs=[pl.BlockSpec(memory_space=pltpu.SMEM)] + vmem_specs(6),
        out_specs=vmem_specs(1)[0],
        scratch_shapes=[pltpu.VMEM((width, rows), F32)],
        compiler_params=pltpu.CompilerParams(vmem_limit_bytes=8 << 20),
        cost_estimate=pl.CostEstimate(flops=1000, bytes_accessed=1000, transcendentals=0),
        name="last",
    )(core, own_part, peer_part, updated, mods, finals, final_t)


def padded(x, axis, width):
    size, length = lax.axis_size(axis), x.shape[0]
    up = [(i, i + 1) for i in range(size - 1)]
    down = [(j, i) for i, j in up]
    before = lax.ppermute(x[length - width :], axis, up)
    after = lax.ppermute(x[:width], axis, down)
    return jnp.concatenate([before, x, after], axis=0)


def per_device(
    hidden,
    text_hidden,
    latent,
    image_mod,
    text_mod,
    final_mod,
    counts,
    step_index,
    qkv_weight,
    text_weight,
    out_weight,
    mlp_in_weight,
    mlp_out_weight,
    final_weight,
    conv_weight,
    conv_bias,
):
    tok_rows, width = hidden.shape[1:]
    width_attn = HEADS * HEAD
    blocks = lax.axis_size("blk")
    blk, img = lax.axis_index("blk"), lax.axis_index("img")
    chip, core = img // 2, img % 2
    mods = image_mod[0]
    chip, core = chip[None], core[None]

    qkv_t = qkv_weight.T
    mlp_mine = jnp.concatenate(
        [mlp_in_weight.T, mlp_out_weight[:width].T, mlp_out_weight[width:].T], axis=0
    )
    image_in = modulate(hidden[0], mods[0], mods[1])
    mlp_mine, image_in = lax.optimization_barrier((mlp_mine, image_in))
    qkv_near = ring_first(qkv_t)
    qkv_next = ring_second(*qkv_near)
    far = jnp.concatenate(qkv_next[:2], axis=0)
    side_left, side_right, mlp_mine = lax.optimization_barrier((*qkv_next[2:], mlp_mine))
    qkv_far = far, swap(far, "img", 2)
    qkv_pieces = [qkv_t, *qkv_near, qkv_far[0], *qkv_next[2:], qkv_far[1]]
    mlp_near = ring_first(mlp_mine)

    peer_in = swap(image_in, "img", 1)
    ready, peer_in = lax.optimization_barrier((marker(qkv_far[1]), peer_in))
    mine, theirs = project_qkv(chip, ready, image_in, peer_in, qkv_pieces)
    other = swap(theirs, "img", 1)
    heads = place_heads(core, mine, other, blocks)
    parts = lax.all_to_all(heads, "blk", 0, 0, tiled=True)

    head = jnp.minimum(blk, HEADS - 1)
    right, head = lax.optimization_barrier((mlp_near[1], head))
    mlp_near = (mlp_near[0], right, mlp_near[2])
    text_in = modulate(text_hidden[0], text_mod[0, 0], text_mod[0, 1])
    text_cols = jnp.concatenate(
        [
            lax.dynamic_slice(text_weight, (0, start + head * HEAD), (width, HEAD))
            for start in (0, width_attn)
        ],
        axis=1,
    )
    text_kv = lax.dot_general(
        text_cols, text_in, (((0,), (1,)), ((), ())), preferred_element_type=F32
    ).astype(BF16)
    text_kv = jnp.pad(text_kv, ((0, 0), (0, -text_kv.shape[1] % tok_rows)))

    mlp_next = ring_second(*mlp_near)
    mark = marker(*mlp_near)
    parts, mark, text_kv = lax.optimization_barrier((parts, mark, text_kv))
    mixed = attend(counts, parts, text_kv, mark)
    mixed, low, high = lax.optimization_barrier((mixed, mlp_next[0], mlp_next[1]))
    peer_low, peer_high = swap(low, "img", 2), swap(high, "img", 2)
    mixed = lax.all_to_all(mixed, "blk", 0, 0, tiled=True)[:HEADS].reshape(width_attn, tok_rows)
    near_pieces, next_pieces = [mlp_mine, *mlp_near], list(mlp_next[2:])

    updated, mlp_in = middle(mixed, hidden[0], mods, out_weight, marker(peer_low, peer_high, *next_pieces))
    mlp_cols = mlp_in_weight.shape[1]
    peer_mlp = swap(mlp_in, "img", 1)
    first_pieces = near_pieces + [low] + next_pieces + [peer_low]
    act = mlp_first(chip, mlp_in, peer_mlp, first_pieces, mlp_cols)
    peer_act = swap(act, "img", 1)
    own_part, sent_part = mlp_second(
        chip, core, act, peer_act, near_pieces + [high] + next_pieces + [peer_high]
    )
    peer_part = swap(sent_part, "img", 1)
    predicted = last(core, own_part, peer_part, updated, mods, final_mod[0], final_weight.T)

    patch_count = counts[0]
    patch_rows = tok_rows // W_P
    lat_rows = 2 * patch_rows
    vel_lat = (
        predicted.reshape(patch_rows, W_P, 2, 2, CH)
        .transpose(0, 2, 1, 3, 4)
        .reshape(lat_rows, 2 * W_P * CH)
    )
    global_rows = blk * lat_rows + jnp.arange(lat_rows, dtype=jnp.int32)
    live_rows = (global_rows < 2 * (patch_count // W_P))[:, None]
    velocity = jnp.where(live_rows, vel_lat, 0.0)
    step_value = step_index[0].astype(F32)
    sigma_gap = plan(step_value + 1.0) - plan(step_value)
    next_lat = jnp.where(live_rows, latent[0] + sigma_gap * vel_lat, 0.0)
    scaled = jnp.where(live_rows, next_lat / vae_scale + vae_offset, 0.0).astype(BF16)
    framed = padded(scaled, "blk", 1)
    padded_grid = jnp.pad(framed.reshape(lat_rows + 2, 2 * W_P, CH), ((0, 0), (1, 1), (0, 0)))
    columns = jnp.concatenate(
        [
            padded_grid[row_off : row_off + lat_rows, col_off : col_off + 2 * W_P, :]
            for row_off in range(3)
            for col_off in range(3)
        ],
        axis=-1,
    ).reshape(lat_rows * 2 * W_P, 9 * CH)
    feature = jnp.dot(columns, conv_weight, preferred_element_type=F32) + conv_bias
    feature = jnp.where(live_rows[:, :, None], feature.reshape(lat_rows, 2 * W_P, -1), 0.0).astype(
        BF16
    )
    return (velocity[None], next_lat[None], feature[None])


def solution(mesh):
    placed = (
        P("img", "blk", None),
        P("img", None, None),
        P("img", "blk", None),
        P("img", None, None),
        P("img", None, None),
        P("img", None, None),
        P("img"),
        P("img"),
        P(None, "img"),
        P(),
        P(),
        P(None, "img"),
        P(None, "img"),
        P(),
        P(),
        P(),
    )
    return jax.shard_map(
        per_device,
        mesh=mesh,
        in_specs=placed,
        out_specs=(P("img", "blk", None), P("img", "blk", None), P("img", "blk", None, None)),
        check_vma=False,
    )
```

```python
import jax
import jax.numpy as jnp
from jax import lax
from jax.experimental import pallas as pl
from jax.experimental.pallas import tpu as pltpu
from jax.sharding import PartitionSpec as P

HEAD = 64
CH = 16
HEADS = 12
W_P = 64
STEPS = 8

norm_eps = 1e-06
sigma_shift = 3.0
vae_scale = 1.5305
vae_offset = 0.0609
masked_score = -1e30

F32 = jnp.float32
BF16 = jnp.bfloat16


def modulate(inputs, shift_row, gain_row):
    values = inputs.astype(F32)
    center = jnp.mean(values, axis=-1, keepdims=True)
    spread = jnp.mean(jnp.square(values - center), axis=-1, keepdims=True)
    normed = (values - center) * lax.rsqrt(spread + norm_eps)
    return (normed * gain_row + shift_row).astype(BF16)


def plan(step_value):
    remain = 1.0 - step_value / STEPS
    return sigma_shift * remain / (1.0 + (sigma_shift - 1.0) * remain)


def swap(x, axis, bits):
    return lax.ppermute(x, axis, [(i, i ^ bits) for i in range(lax.axis_size(axis))])


def vmem_specs(count):
    return [pl.BlockSpec(memory_space=pltpu.VMEM)] * count


def whole(x):
    return pl.BlockSpec(x.shape, lambda i: (0,) * x.ndim)


OFFSETS = ((0, 0), (-1, 0), (1, 0), (0, 1), (2, 0), (-1, 1), (1, 1), (2, 1))


def ring(x, axis, step):
    size = lax.axis_size(axis)
    return lax.ppermute(x, axis, [(i, (i + step) % size) for i in range(size)])


def ring_first(x, side):
    return ring(x, "img", 4), ring(x, "img", -4), swap(side, "img", 2)


def ring_second(left, right, across):
    half = left.shape[0] // 2
    return (
        ring(left[:half], "img", 4),
        ring(right[half:], "img", -4),
        ring(across, "img", 4),
        ring(across, "img", -4),
    )


def place_of(chip, k):
    dx, dy = OFFSETS[k]
    column = jnp.bitwise_and(chip // 2 + dx + 4, 3)
    return 2 * column + jnp.bitwise_xor(jnp.bitwise_and(chip, 1), dy)


def qkv_body(chip_ref, ready, own_x, peer_x, *refs):
    weights, (own_out, peer_out) = refs[:-2], refs[-2:]
    rows = own_x.shape[0]
    both = jnp.concatenate([own_x[...], peer_x[...]], axis=0)
    cols = own_out.shape[1]
    stacked = jnp.concatenate([weight[...] for weight in weights], axis=0)
    parts = lax.dot_general(
        stacked, both, (((1,), (1,)), ((), ())), preferred_element_type=F32
    ).astype(BF16)
    for k in range(len(weights)):
        place = place_of(chip_ref[0], k)
        own_out[place] = parts[k * cols : (k + 1) * cols, :rows]
        peer_out[place] = parts[k * cols : (k + 1) * cols, rows:]


def project_qkv(chip, ready, own_x, peer_x, weights):
    cols, rows = weights[0].shape[0], own_x.shape[0]
    shape = (len(weights), cols, rows)
    inputs = (ready, own_x, peer_x, *weights)
    return pl.pallas_call(
        qkv_body,
        out_shape=(jax.ShapeDtypeStruct(shape, BF16),) * 2,
        grid=(1,),
        in_specs=[pl.BlockSpec(memory_space=pltpu.SMEM)] + [whole(x) for x in inputs],
        out_specs=(pl.BlockSpec(shape, lambda i: (0, 0, 0)),) * 2,
        compiler_params=pltpu.CompilerParams(vmem_limit_bytes=20 << 20),
        cost_estimate=pl.CostEstimate(flops=1000, bytes_accessed=1000, transcendentals=0),
        name="project_qkv",
    )(chip, *inputs)


def heads_body(core_ref, mine, other, out):
    count, cols, _ = mine.shape
    step = 16
    per_shard, per_head = cols // step, HEAD // step
    section = HEADS * per_head

    def copy(sources):
        for c in range(count):
            for parity, source in enumerate(sources):
                for j in range(per_shard):
                    piece = (2 * c + parity) * per_shard + j
                    kind, rest = piece // section, piece % section
                    start = kind * HEAD + rest % per_head * step
                    rows = source[c, j * step : (j + 1) * step]
                    out[rest // per_head, start : start + step] = rows

    @pl.when(core_ref[0] == 0)
    def _():
        copy((mine, other))

    @pl.when(core_ref[0] != 0)
    def _():
        copy((other, mine))

    out[HEADS:] = jnp.zeros((out.shape[0] - HEADS,) + out.shape[1:], BF16)


def place_heads(core, mine, other, blocks):
    shape = (blocks, 3 * HEAD, mine.shape[2])
    return pl.pallas_call(
        heads_body,
        out_shape=jax.ShapeDtypeStruct(shape, BF16),
        grid=(1,),
        in_specs=[pl.BlockSpec(memory_space=pltpu.SMEM), whole(mine), whole(other)],
        out_specs=pl.BlockSpec(shape, lambda i: (0, 0, 0)),
        compiler_params=pltpu.CompilerParams(vmem_limit_bytes=6 << 20),
        cost_estimate=pl.CostEstimate(flops=1000, bytes_accessed=1000, transcendentals=0),
        name="place_heads",
    )(core, mine, other)


def mark_body(*refs):
    refs[-1][...] = refs[0][...]


def marker(*arrays):
    return pl.pallas_call(
        mark_body,
        out_shape=jax.ShapeDtypeStruct((16, 128), BF16),
        grid=(1,),
        in_specs=[pl.BlockSpec((16, 128), lambda i: (0, 0))] * len(arrays),
        out_specs=pl.BlockSpec((16, 128), lambda i: (0, 0)),
        compiler_params=pltpu.CompilerParams(vmem_limit_bytes=1 << 20),
        cost_estimate=pl.CostEstimate(
            flops=100_000_000_000, bytes_accessed=100_000_000, transcendentals=0
        ),
        name="marker",
    )(*arrays)


def attend_body(count_ref, parts, text, mark, out, keys, values, queries):
    blocks, _, rows = parts.shape
    text_blocks = text.shape[1] // rows
    text_len = 154
    tile = 2 * rows
    lane = lax.broadcasted_iota(jnp.int32, (HEAD, rows), 1)
    row = lax.broadcasted_iota(jnp.int32, (HEAD, rows), 0)
    top = row == 0
    zeros = jnp.zeros((HEAD, rows), F32)
    ones = jnp.where(top, 1.0, 0.0).astype(F32)

    def place(index, key_part, value_part, limit):
        cols = slice(index * rows, (index + 1) * rows)
        keys[:HEAD, cols] = key_part
        bias = jnp.where(jnp.logical_and(top, lane >= limit), masked_score, 0.0)
        keys[HEAD:, cols] = bias.astype(BF16)
        full = jnp.concatenate([value_part.astype(F32), zeros], axis=0)
        values[cols, :] = full.T.astype(BF16)

    for b in range(blocks):
        part = parts[b]
        place(b, part[HEAD : 2 * HEAD], part[2 * HEAD :], count_ref[0] - b * rows)
        scaled = part[:HEAD].astype(F32) * 0.125
        full = jnp.concatenate([scaled, ones], axis=0)
        queries[b * rows : (b + 1) * rows, :] = full.T.astype(BF16)
    for t in range(text_blocks):
        cols = slice(t * rows, (t + 1) * rows)
        place(blocks + t, text[:HEAD, cols], text[HEAD:, cols], text_len - t * rows)

    def step(t, carry):
        first = pl.multiple_of(t * tile, tile)
        scores = jnp.dot(queries[pl.ds(first, tile), :], keys[...], preferred_element_type=F32)
        top_score = jnp.max(scores, axis=1, keepdims=True)
        numer = jnp.exp(scores - top_score)
        total = jnp.sum(numer, axis=1, keepdims=True)
        mixed = jnp.dot(numer.astype(BF16), values[...], preferred_element_type=F32) / total
        turned = mixed.T[:HEAD].astype(BF16)
        out[2 * t] = turned[:, :rows]
        out[2 * t + 1] = turned[:, rows:]
        return carry

    lax.fori_loop(0, blocks // 2, step, 0)


def attend(count, parts, text, mark):
    blocks, _, rows = parts.shape
    keys = blocks * rows + text.shape[1]
    queries = blocks * rows
    return pl.pallas_call(
        attend_body,
        out_shape=jax.ShapeDtypeStruct((blocks, HEAD, rows), BF16),
        in_specs=[pl.BlockSpec(memory_space=pltpu.SMEM)] + vmem_specs(3),
        out_specs=vmem_specs(1)[0],
        scratch_shapes=[
            pltpu.VMEM((2 * HEAD, keys), BF16),
            pltpu.VMEM((keys, 2 * HEAD), BF16),
            pltpu.VMEM((queries, 2 * HEAD), BF16),
        ],
        compiler_params=pltpu.CompilerParams(vmem_limit_bytes=20 << 20),
        cost_estimate=pl.CostEstimate(flops=1000, bytes_accessed=1000, transcendentals=0),
        name="attend",
    )(count, parts, text, mark)


def layer_norm(values, shift_row, scale_row):
    center = jnp.mean(values, axis=-1, keepdims=True)
    spread = jnp.mean(jnp.square(values - center), axis=-1, keepdims=True)
    normed = (values - center) * lax.rsqrt(spread + norm_eps)
    return (normed * (1.0 + scale_row) + shift_row).astype(BF16)


def gelu(v):
    return 0.5 * v * (1.0 + jnp.tanh(0.7978845608028654 * (v + 0.044715 * v * v * v)))


def middle_body(mixed, hidden, mods, out_w, mark, updated, mlp_in):
    attended = mixed[...].astype(F32).T.astype(BF16)
    projected = jnp.dot(attended, out_w[...], preferred_element_type=F32)
    now = hidden[...].astype(F32) + mods[2:3] * projected
    updated[...] = now
    mlp_in[...] = layer_norm(now, mods[3:4], mods[4:5])


def middle(mixed, hidden, mods, out_w, mark):
    rows, width = hidden.shape
    return pl.pallas_call(
        middle_body,
        out_shape=(
            jax.ShapeDtypeStruct((rows, width), F32),
            jax.ShapeDtypeStruct((rows, width), BF16),
        ),
        in_specs=vmem_specs(5),
        out_specs=tuple(vmem_specs(2)),
        compiler_params=pltpu.CompilerParams(vmem_limit_bytes=14 << 20),
        cost_estimate=pl.CostEstimate(flops=1000, bytes_accessed=1000, transcendentals=0),
        name="middle",
    )(mixed, hidden, mods, out_w, mark)


def first_body(chip_ref, own_x, peer_x, *refs):
    weights, out = refs[:-1], refs[-1]
    both = jnp.concatenate([own_x[...], peer_x[...]], axis=0)
    cols = out.shape[1]
    stacked = jnp.concatenate([weight[...] for weight in weights], axis=0)
    parts = lax.dot_general(stacked, both, (((1,), (1,)), ((), ())), preferred_element_type=F32)
    for k in range(len(weights)):
        out[place_of(chip_ref[0], k)] = gelu(parts[k * cols : (k + 1) * cols]).astype(BF16)


def half_of(x, cols, index):
    position = index if x.shape[0] > cols else 0
    return pl.BlockSpec((cols, x.shape[1]), lambda i: (position, 0))


def mlp_first(chip, own_x, peer_x, weights, cols):
    rows = own_x.shape[0]
    count = len(weights)
    shape = (count, cols, 2 * rows)
    return pl.pallas_call(
        first_body,
        out_shape=jax.ShapeDtypeStruct(shape, BF16),
        grid=(1,),
        in_specs=[pl.BlockSpec(memory_space=pltpu.SMEM), whole(own_x), whole(peer_x)]
        + [half_of(x, cols, 0) for x in weights],
        out_specs=pl.BlockSpec(shape, lambda i: (0, 0, 0)),
        compiler_params=pltpu.CompilerParams(vmem_limit_bytes=28 << 20),
        cost_estimate=pl.CostEstimate(flops=1000, bytes_accessed=1000, transcendentals=0),
        name="mlp_first",
    )(chip, own_x, peer_x, *weights)


def second_body(chip_ref, core_ref, own_act, peer_act, *refs):
    weights, (own_out, peer_out), act = refs[:-3], refs[-3:-1], refs[-1]
    count, cols, tokens = own_act.shape
    mid = tokens // 2
    core = core_ref[0]
    for c in range(count):
        mine = pl.ds(pl.multiple_of((2 * c + core) * cols, cols), cols)
        act[mine, :] = own_act[c]
        other = pl.ds(pl.multiple_of((2 * c + 1 - core) * cols, cols), cols)
        act[other, :mid] = peer_act[c, :, mid:]
        act[other, mid:] = peer_act[c, :, :mid]
    width = weights[0].shape[1]
    half = cols // 2
    low = jnp.concatenate([weight[:half] for weight in weights], axis=0)
    parts = jnp.dot(low, act[:width], preferred_element_type=F32)
    high = jnp.concatenate([weight[half:] for weight in weights], axis=0)
    parts += jnp.dot(high, act[width:], preferred_element_type=F32)
    for k in range(count):
        place = place_of(chip_ref[0], k)
        own_out[place] = parts[k * half : (k + 1) * half, :mid]
        peer_out[place] = parts[k * half : (k + 1) * half, mid:]


def mlp_second(chip, core, own_act, peer_act, weights):
    count, cols, tokens = own_act.shape
    shape = (count, cols // 2, tokens // 2)
    return pl.pallas_call(
        second_body,
        out_shape=(jax.ShapeDtypeStruct(shape, F32), jax.ShapeDtypeStruct(shape, F32)),
        grid=(1,),
        in_specs=[pl.BlockSpec(memory_space=pltpu.SMEM)] * 2
        + [whole(own_act), whole(peer_act)]
        + [half_of(x, cols, 1) for x in weights],
        out_specs=(pl.BlockSpec(shape, lambda i: (0, 0, 0)),) * 2,
        scratch_shapes=[pltpu.VMEM((2 * count * cols, tokens), BF16)],
        compiler_params=pltpu.CompilerParams(vmem_limit_bytes=28 << 20),
        cost_estimate=pl.CostEstimate(flops=1000, bytes_accessed=1000, transcendentals=0),
        name="mlp_second",
    )(chip, core, own_act, peer_act, *weights)


def last_body(
    core_ref, live_ref, gap_ref, own_part, peer_part, updated, mods, finals, final_t, latent,
    velocity, next_latent, scaled, top, bottom, mlp_t,
):
    count, half, _ = own_part.shape
    for source, parity in ((own_part, core_ref[0]), (peer_part, 1 - core_ref[0])):
        for c in range(count):
            start = pl.multiple_of((2 * c + parity) * half, half)
            mlp_t[pl.ds(start, half), :] = source[c]
    refined = updated[...] + mods[5:6] * mlp_t[...].T
    final_in = layer_norm(refined, finals[0:1], finals[1:2])
    predicted = lax.dot_general(
        final_in, final_t[...], (((1,), (1,)), ((), ())), preferred_element_type=F32
    )
    live = jnp.full(predicted.shape, live_ref[0], jnp.int32) != 0
    moved = latent[...] + gap_ref[0] * predicted
    inner = (moved / vae_scale + vae_offset).astype(F32)
    velocity[...] = jnp.where(live, predicted, 0.0)
    next_latent[...] = jnp.where(live, moved, 0.0)
    inner = jnp.where(live, inner, 0.0).astype(BF16)
    scaled[...] = inner
    lanes = inner.shape[1] // 2
    top[...] = inner[:W_P, :lanes]
    bottom[...] = inner[inner.shape[0] - W_P :, lanes:]


def last(core, live, gap, own_part, peer_part, updated, mods, finals, final_t, latent):
    rows, width = updated.shape
    cols = final_t.shape[0]
    smem = pl.BlockSpec(memory_space=pltpu.SMEM)
    return pl.pallas_call(
        last_body,
        out_shape=(
            jax.ShapeDtypeStruct((rows, cols), F32),
            jax.ShapeDtypeStruct((rows, cols), F32),
            jax.ShapeDtypeStruct((rows, cols), BF16),
            jax.ShapeDtypeStruct((W_P, cols // 2), BF16),
            jax.ShapeDtypeStruct((W_P, cols // 2), BF16),
        ),
        in_specs=[smem] * 3 + vmem_specs(7),
        out_specs=tuple(vmem_specs(5)),
        scratch_shapes=[pltpu.VMEM((width, rows), F32)],
        compiler_params=pltpu.CompilerParams(vmem_limit_bytes=8 << 20),
        cost_estimate=pl.CostEstimate(flops=1000, bytes_accessed=1000, transcendentals=0),
        name="last",
    )(core, live, gap, own_part, peer_part, updated, mods, finals, final_t, latent)


def conv_body(live_ref, scaled, before, after, weights, bias, out):
    lanes = before.shape[1]
    lines = [before[...]]
    for r in range(scaled.shape[0] // W_P):
        rows = scaled[r * W_P : (r + 1) * W_P]
        lines += [rows[:, :lanes], rows[:, lanes:]]
    lines.append(after[...])
    grid = jnp.concatenate([line.astype(F32) for line in lines], axis=1).astype(BF16)
    pixels = 2 * W_P
    pixel = lax.broadcasted_iota(jnp.int32, (pixels, W_P), 0)
    patch = lax.broadcasted_iota(jnp.int32, (pixels, W_P), 1)
    half, odd = pixel // 2, pixel % 2
    shifted = []
    for parity, offset in ((0, -1), (0, 0), (1, 0), (1, 1)):
        pick = jnp.logical_and(odd == parity, patch == half + offset)
        pick = jnp.where(pick, 1.0, 0.0).astype(BF16)
        shifted.append(jnp.dot(pick, grid, preferred_element_type=F32).astype(BF16))
    live = live_ref[0] != 0
    for line in range(out.shape[0]):
        total = jnp.zeros((pixels, out.shape[2]), F32)
        for k in range(4):
            window = shifted[k][:, line * lanes : (line + 3) * lanes]
            total += jnp.dot(window, weights[k], preferred_element_type=F32)
        total = jnp.where(live, total + bias[...], 0.0)
        out[line] = total.astype(BF16)


def convolve(live, scaled, before, after, weights, bias):
    lines = 2 * scaled.shape[0] // W_P
    shape = (lines, 2 * W_P, weights.shape[2])
    return pl.pallas_call(
        conv_body,
        out_shape=jax.ShapeDtypeStruct(shape, BF16),
        in_specs=[pl.BlockSpec(memory_space=pltpu.SMEM)] + vmem_specs(5),
        out_specs=vmem_specs(1)[0],
        compiler_params=pltpu.CompilerParams(vmem_limit_bytes=12 << 20),
        cost_estimate=pl.CostEstimate(flops=1000, bytes_accessed=1000, transcendentals=0),
        name="convolve",
    )(live, scaled, before, after, weights, bias)


def conv_weights(conv_weight):
    taps = conv_weight.reshape(3, 3, CH, -1)
    none = jnp.zeros_like(taps[:, 0])
    pairs = ((none, taps[:, 0]), (taps[:, 1], taps[:, 2]), (taps[:, 0], taps[:, 1]), (taps[:, 2], none))
    return jnp.stack([jnp.stack(pair, axis=1).reshape(6 * CH, -1) for pair in pairs])


def per_device(
    hidden,
    text_hidden,
    latent,
    image_mod,
    text_mod,
    final_mod,
    counts,
    step_index,
    qkv_weight,
    text_weight,
    out_weight,
    mlp_in_weight,
    mlp_out_weight,
    final_weight,
    conv_weight,
    conv_bias,
):
    tok_rows, width = hidden.shape[1:]
    width_attn = HEADS * HEAD
    blocks = lax.axis_size("blk")
    blk, img = lax.axis_index("blk"), lax.axis_index("img")
    chip, core = img // 2, img % 2
    mods = image_mod[0]
    chip, core = chip[None], core[None]

    qkv_t = qkv_weight.T
    mlp_mine = jnp.concatenate(
        [mlp_in_weight.T, mlp_out_weight[:width].T, mlp_out_weight[width:].T], axis=0
    )
    gain, qkv_side = lax.optimization_barrier((1.0 + mods[1], qkv_t))
    image_in = modulate(hidden[0], mods[0], gain)
    mlp_mine, image_in = lax.optimization_barrier((mlp_mine, image_in))
    qkv_near = ring_first(qkv_t, qkv_side)
    qkv_next = ring_second(*qkv_near)
    far = jnp.concatenate(qkv_next[:2], axis=0)
    side_left, side_right, mlp_mine = lax.optimization_barrier((*qkv_next[2:], mlp_mine))
    qkv_far = far, swap(far, "img", 2)
    qkv_pieces = [qkv_t, *qkv_near, qkv_far[0], *qkv_next[2:], qkv_far[1]]
    mlp_near = ring_first(mlp_mine, mlp_mine)

    peer_in = swap(image_in, "img", 1)
    ready, peer_in = lax.optimization_barrier((marker(qkv_far[1]), peer_in))
    mine, theirs = project_qkv(chip, ready, image_in, peer_in, qkv_pieces)
    other = swap(theirs, "img", 1)
    heads = place_heads(core, mine, other, blocks)
    head = jnp.minimum(blk, HEADS - 1)
    right, head = lax.optimization_barrier((mlp_near[1], head))
    mlp_near = (mlp_near[0], right, mlp_near[2])
    parts = lax.all_to_all(heads, "blk", 0, 0, tiled=True)
    text_in = modulate(text_hidden[0], text_mod[0, 0], 1.0 + text_mod[0, 1])
    text_cols = jnp.concatenate(
        [
            lax.dynamic_slice(text_weight, (0, start + head * HEAD), (width, HEAD))
            for start in (0, width_attn)
        ],
        axis=1,
    )
    text_kv = lax.dot_general(
        text_cols, text_in, (((0,), (1,)), ((), ())), preferred_element_type=F32
    ).astype(BF16)
    text_kv = jnp.pad(text_kv, ((0, 0), (0, -text_kv.shape[1] % tok_rows)))

    mlp_next = ring_second(*mlp_near)
    mark = marker(*mlp_near)
    parts, mark, text_kv = lax.optimization_barrier((parts, mark, text_kv))
    mixed = attend(counts, parts, text_kv, mark)
    mixed, low, high = lax.optimization_barrier((mixed, mlp_next[0], mlp_next[1]))
    peer_low, peer_high = swap(low, "img", 2), swap(high, "img", 2)
    mixed = lax.all_to_all(mixed, "blk", 0, 0, tiled=True)[:HEADS].reshape(width_attn, tok_rows)
    near_pieces, next_pieces = [mlp_mine, *mlp_near], list(mlp_next[2:])

    latent_p = latent[0].reshape(-1, 2, W_P, 2 * CH).transpose(0, 2, 1, 3)
    latent_p = latent_p.reshape(tok_rows, 4 * CH)
    conv_w = conv_weights(conv_weight)
    live = (blk * tok_rows < counts).astype(jnp.int32)
    step_value = step_index.astype(F32)
    gap = plan(step_value + 1.0) - plan(step_value)
    mixed, latent_p, conv_w = lax.optimization_barrier((mixed, latent_p, conv_w))
    updated, mlp_in = middle(mixed, hidden[0], mods, out_weight, marker(peer_low, peer_high, *next_pieces))
    mlp_cols = mlp_in_weight.shape[1]
    peer_mlp = swap(mlp_in, "img", 1)
    first_pieces = near_pieces + [low] + next_pieces + [peer_low]
    act = mlp_first(chip, mlp_in, peer_mlp, first_pieces, mlp_cols)
    peer_act = swap(act, "img", 1)
    own_part, sent_part = mlp_second(
        chip, core, act, peer_act, near_pieces + [high] + next_pieces + [peer_high]
    )
    peer_part = swap(sent_part, "img", 1)
    velocity, next_lat, scaled, top, bottom = last(
        core, live, gap, own_part, peer_part, updated, mods, final_mod[0], final_weight.T, latent_p
    )
    size = blocks
    before = lax.ppermute(bottom, "blk", [(i, i + 1) for i in range(size - 1)])
    after = lax.ppermute(top, "blk", [(i + 1, i) for i in range(size - 1)])
    feature = convolve(live, scaled, before, after, conv_w, conv_bias[None])

    def by_rows(x):
        return x.reshape(-1, W_P, 2, 2 * CH).transpose(0, 2, 1, 3).reshape(latent[0].shape)

    return (by_rows(velocity)[None], by_rows(next_lat)[None], feature[None])


def solution(mesh):
    placed = (
        P("img", "blk", None),
        P("img", None, None),
        P("img", "blk", None),
        P("img", None, None),
        P("img", None, None),
        P("img", None, None),
        P("img"),
        P("img"),
        P(None, "img"),
        P(),
        P(),
        P(None, "img"),
        P(None, "img"),
        P(),
        P(),
        P(),
    )
    return jax.shard_map(
        per_device,
        mesh=mesh,
        in_specs=placed,
        out_specs=(P("img", "blk", None), P("img", "blk", None), P("img", "blk", None, None)),
        check_vma=False,
    )
```

```python
import jax
import jax.numpy as jnp
from jax import lax
from jax.experimental import pallas as pl
from jax.experimental.pallas import tpu as pltpu
from jax.sharding import PartitionSpec as P

HEAD = 64
CH = 16
HEADS = 12
W_P = 64
STEPS = 8

norm_eps = 1e-06
sigma_shift = 3.0
vae_scale = 1.5305
vae_offset = 0.0609
masked_score = -1e30

F32 = jnp.float32
BF16 = jnp.bfloat16


def modulate(inputs, shift_row, gain_row):
    values = inputs.astype(F32)
    center = jnp.mean(values, axis=-1, keepdims=True)
    spread = jnp.mean(jnp.square(values - center), axis=-1, keepdims=True)
    normed = (values - center) * lax.rsqrt(spread + norm_eps)
    return (normed * gain_row + shift_row).astype(BF16)


def plan(step_value):
    remain = 1.0 - step_value / STEPS
    return sigma_shift * remain / (1.0 + (sigma_shift - 1.0) * remain)


def swap(x, axis, bits):
    return lax.ppermute(x, axis, [(i, i ^ bits) for i in range(lax.axis_size(axis))])


def vmem_specs(count):
    return [pl.BlockSpec(memory_space=pltpu.VMEM)] * count


def whole(x):
    return pl.BlockSpec(x.shape, lambda i: (0,) * x.ndim)


OFFSETS = ((0, 0), (-1, 0), (1, 0), (0, 1), (2, 0), (-1, 1), (1, 1), (2, 1))


def ring(x, axis, step):
    size = lax.axis_size(axis)
    return lax.ppermute(x, axis, [(i, (i + step) % size) for i in range(size)])


def ring_first(x, side):
    return ring(x, "img", 4), ring(x, "img", -4), swap(side, "img", 2)


def ring_second(left, right, across):
    half = left.shape[0] // 2
    return (
        ring(left[:half], "img", 4),
        ring(right[half:], "img", -4),
        ring(across, "img", 4),
        ring(across, "img", -4),
    )


def place_of(chip, k):
    dx, dy = OFFSETS[k]
    column = jnp.bitwise_and(chip // 2 + dx + 4, 3)
    return 2 * column + jnp.bitwise_xor(jnp.bitwise_and(chip, 1), dy)


def qkv_body(chip_ref, ready, own_x, peer_x, *refs):
    weights, (own_out, peer_out) = refs[:-2], refs[-2:]
    rows = own_x.shape[0]
    both = jnp.concatenate([own_x[...], peer_x[...]], axis=0)
    cols = own_out.shape[1]
    stacked = jnp.concatenate([weight[...] for weight in weights], axis=0)
    parts = lax.dot_general(
        stacked, both, (((1,), (1,)), ((), ())), preferred_element_type=F32
    ).astype(BF16)
    for k in range(len(weights)):
        place = place_of(chip_ref[0], k)
        own_out[place] = parts[k * cols : (k + 1) * cols, :rows]
        peer_out[place] = parts[k * cols : (k + 1) * cols, rows:]


def project_qkv(chip, ready, own_x, peer_x, weights):
    cols, rows = weights[0].shape[0], own_x.shape[0]
    shape = (len(weights), cols, rows)
    inputs = (ready, own_x, peer_x, *weights)
    return pl.pallas_call(
        qkv_body,
        out_shape=(jax.ShapeDtypeStruct(shape, BF16),) * 2,
        grid=(1,),
        in_specs=[pl.BlockSpec(memory_space=pltpu.SMEM)] + [whole(x) for x in inputs],
        out_specs=(pl.BlockSpec(shape, lambda i: (0, 0, 0)),) * 2,
        compiler_params=pltpu.CompilerParams(vmem_limit_bytes=20 << 20),
        cost_estimate=pl.CostEstimate(flops=1000, bytes_accessed=1000, transcendentals=0),
        name="project_qkv",
    )(chip, *inputs)


def heads_body(core_ref, mine, other, out):
    count, cols, _ = mine.shape
    step = 16
    per_shard, per_head = cols // step, HEAD // step
    section = HEADS * per_head

    def copy(sources):
        for c in range(count):
            for parity, source in enumerate(sources):
                for j in range(per_shard):
                    piece = (2 * c + parity) * per_shard + j
                    kind, rest = piece // section, piece % section
                    start = kind * HEAD + rest % per_head * step
                    rows = source[c, j * step : (j + 1) * step]
                    out[rest // per_head, start : start + step] = rows

    @pl.when(core_ref[0] == 0)
    def _():
        copy((mine, other))

    @pl.when(core_ref[0] != 0)
    def _():
        copy((other, mine))

    out[HEADS:] = jnp.zeros((out.shape[0] - HEADS,) + out.shape[1:], BF16)


def place_heads(core, mine, other, blocks):
    shape = (blocks, 3 * HEAD, mine.shape[2])
    return pl.pallas_call(
        heads_body,
        out_shape=jax.ShapeDtypeStruct(shape, BF16),
        grid=(1,),
        in_specs=[pl.BlockSpec(memory_space=pltpu.SMEM), whole(mine), whole(other)],
        out_specs=pl.BlockSpec(shape, lambda i: (0, 0, 0)),
        compiler_params=pltpu.CompilerParams(vmem_limit_bytes=6 << 20),
        cost_estimate=pl.CostEstimate(flops=1000, bytes_accessed=1000, transcendentals=0),
        name="place_heads",
    )(core, mine, other)


def text_body(head_ref, hidden, mods, key_w, value_w, out, turned):
    odd = head_ref[0] % 2 != 0
    rows = hidden.shape[0]
    states = layer_norm(hidden[...].astype(F32), mods[0:1], mods[1:2])
    turned[...] = jnp.zeros_like(turned)
    for part, weight in enumerate((key_w, value_w)):
        turned[:rows, :] = jnp.dot(states, weight[...], preferred_element_type=F32)
        both = turned[...].T
        chosen = jnp.where(odd, both[HEAD:], both[:HEAD])
        out[part * HEAD : (part + 1) * HEAD, :] = chosen.astype(BF16)


def text_keys(head, hidden, mods, weight, rows):
    width = hidden.shape[1]
    pair = 2 * HEAD
    values_at = HEADS * HEAD // pair
    return pl.pallas_call(
        text_body,
        out_shape=jax.ShapeDtypeStruct((pair, rows), BF16),
        grid_spec=pltpu.PrefetchScalarGridSpec(
            num_scalar_prefetch=1,
            grid=(1,),
            in_specs=[
                pl.BlockSpec(hidden.shape, lambda i, h: (0, 0)),
                pl.BlockSpec(mods.shape, lambda i, h: (0, 0)),
                pl.BlockSpec((width, pair), lambda i, h: (0, h[0] // 2)),
                pl.BlockSpec((width, pair), lambda i, h: (0, values_at + h[0] // 2)),
            ],
            out_specs=pl.BlockSpec((pair, rows), lambda i, h: (0, 0)),
            scratch_shapes=[pltpu.VMEM((rows, pair), F32)],
        ),
        compiler_params=pltpu.CompilerParams(vmem_limit_bytes=10 << 20),
        cost_estimate=pl.CostEstimate(flops=1000, bytes_accessed=1000, transcendentals=0),
        name="text_keys",
    )(head, hidden, mods, weight, weight)


def mark_body(*refs):
    refs[-1][...] = refs[0][...]


def marker(*arrays):
    return pl.pallas_call(
        mark_body,
        out_shape=jax.ShapeDtypeStruct((16, 128), BF16),
        grid=(1,),
        in_specs=[pl.BlockSpec((16, 128), lambda i: (0, 0))] * len(arrays),
        out_specs=pl.BlockSpec((16, 128), lambda i: (0, 0)),
        compiler_params=pltpu.CompilerParams(vmem_limit_bytes=1 << 20),
        cost_estimate=pl.CostEstimate(
            flops=100_000_000_000, bytes_accessed=100_000_000, transcendentals=0
        ),
        name="marker",
    )(*arrays)


def attend_body(count_ref, parts, text, mark, out, keys, values, queries):
    blocks, _, rows = parts.shape
    text_blocks = text.shape[1] // rows
    text_len = 154
    tile = 2 * rows
    lane = lax.broadcasted_iota(jnp.int32, (HEAD, rows), 1)
    row = lax.broadcasted_iota(jnp.int32, (HEAD, rows), 0)
    top = row == 0
    zeros = jnp.zeros((HEAD, rows), F32)
    ones = jnp.where(top, 1.0, 0.0).astype(F32)

    def place(index, key_part, value_part, limit):
        cols = slice(index * rows, (index + 1) * rows)
        keys[:HEAD, cols] = key_part
        bias = jnp.where(jnp.logical_and(top, lane >= limit), masked_score, 0.0)
        keys[HEAD:, cols] = bias.astype(BF16)
        full = jnp.concatenate([value_part.astype(F32), zeros], axis=0)
        values[cols, :] = full.T.astype(BF16)

    for b in range(blocks):
        part = parts[b]
        place(b, part[HEAD : 2 * HEAD], part[2 * HEAD :], count_ref[0] - b * rows)
        scaled = part[:HEAD].astype(F32) * 0.125
        full = jnp.concatenate([scaled, ones], axis=0)
        queries[b * rows : (b + 1) * rows, :] = full.T.astype(BF16)
    for t in range(text_blocks):
        cols = slice(t * rows, (t + 1) * rows)
        place(blocks + t, text[:HEAD, cols], text[HEAD:, cols], text_len - t * rows)

    def step(t, carry):
        first = pl.multiple_of(t * tile, tile)
        scores = jnp.dot(queries[pl.ds(first, tile), :], keys[...], preferred_element_type=F32)
        top_score = jnp.max(scores, axis=1, keepdims=True)
        numer = jnp.exp(scores - top_score)
        total = jnp.sum(numer, axis=1, keepdims=True)
        mixed = jnp.dot(numer.astype(BF16), values[...], preferred_element_type=F32) / total
        turned = mixed.T[:HEAD].astype(BF16)
        out[2 * t] = turned[:, :rows]
        out[2 * t + 1] = turned[:, rows:]
        return carry

    lax.fori_loop(0, blocks // 2, step, 0)


def attend(count, parts, text, mark):
    blocks, _, rows = parts.shape
    keys = blocks * rows + text.shape[1]
    queries = blocks * rows
    return pl.pallas_call(
        attend_body,
        out_shape=jax.ShapeDtypeStruct((blocks, HEAD, rows), BF16),
        in_specs=[pl.BlockSpec(memory_space=pltpu.SMEM)] + vmem_specs(3),
        out_specs=vmem_specs(1)[0],
        scratch_shapes=[
            pltpu.VMEM((2 * HEAD, keys), BF16),
            pltpu.VMEM((keys, 2 * HEAD), BF16),
            pltpu.VMEM((queries, 2 * HEAD), BF16),
        ],
        compiler_params=pltpu.CompilerParams(vmem_limit_bytes=20 << 20),
        cost_estimate=pl.CostEstimate(flops=1000, bytes_accessed=1000, transcendentals=0),
        name="attend",
    )(count, parts, text, mark)


def layer_norm(values, shift_row, scale_row):
    center = jnp.mean(values, axis=-1, keepdims=True)
    spread = jnp.mean(jnp.square(values - center), axis=-1, keepdims=True)
    normed = (values - center) * lax.rsqrt(spread + norm_eps)
    return (normed * (1.0 + scale_row) + shift_row).astype(BF16)


def gelu(v):
    return 0.5 * v * (1.0 + jnp.tanh(0.7978845608028654 * (v + 0.044715 * v * v * v)))


def middle_body(mixed, hidden, mods, out_w, mark, updated, mlp_in):
    attended = mixed[...].astype(F32).T.astype(BF16)
    projected = jnp.dot(attended, out_w[...], preferred_element_type=F32)
    now = hidden[...].astype(F32) + mods[2:3] * projected
    updated[...] = now
    mlp_in[...] = layer_norm(now, mods[3:4], mods[4:5])


def middle(mixed, hidden, mods, out_w, mark):
    rows, width = hidden.shape
    inputs = (mixed, hidden, mods, out_w, mark)
    return pl.pallas_call(
        middle_body,
        out_shape=(
            jax.ShapeDtypeStruct((rows, width), F32),
            jax.ShapeDtypeStruct((rows, width), BF16),
        ),
        grid=(1,),
        in_specs=[whole(x) for x in inputs],
        out_specs=(pl.BlockSpec((rows, width), lambda i: (0, 0)),) * 2,
        compiler_params=pltpu.CompilerParams(vmem_limit_bytes=14 << 20),
        cost_estimate=pl.CostEstimate(flops=1000, bytes_accessed=1000, transcendentals=0),
        name="middle",
    )(*inputs)


def first_body(chip_ref, own_x, peer_x, *refs):
    weights, out = refs[:-1], refs[-1]
    both = jnp.concatenate([own_x[...], peer_x[...]], axis=0)
    cols = out.shape[1]
    stacked = jnp.concatenate([weight[...] for weight in weights], axis=0)
    parts = lax.dot_general(stacked, both, (((1,), (1,)), ((), ())), preferred_element_type=F32)
    for k in range(len(weights)):
        out[place_of(chip_ref[0], k)] = gelu(parts[k * cols : (k + 1) * cols]).astype(BF16)


def half_of(x, cols, index):
    position = index if x.shape[0] > cols else 0
    return pl.BlockSpec((cols, x.shape[1]), lambda i: (position, 0))


def mlp_first(chip, own_x, peer_x, weights, cols):
    rows = own_x.shape[0]
    count = len(weights)
    shape = (count, cols, 2 * rows)
    return pl.pallas_call(
        first_body,
        out_shape=jax.ShapeDtypeStruct(shape, BF16),
        grid=(1,),
        in_specs=[pl.BlockSpec(memory_space=pltpu.SMEM), whole(own_x), whole(peer_x)]
        + [half_of(x, cols, 0) for x in weights],
        out_specs=pl.BlockSpec(shape, lambda i: (0, 0, 0)),
        compiler_params=pltpu.CompilerParams(vmem_limit_bytes=28 << 20),
        cost_estimate=pl.CostEstimate(flops=1000, bytes_accessed=1000, transcendentals=0),
        name="mlp_first",
    )(chip, own_x, peer_x, *weights)


def second_body(chip_ref, core_ref, own_act, peer_act, *refs):
    weights, (own_out, peer_out), act = refs[:-3], refs[-3:-1], refs[-1]
    count, cols, tokens = own_act.shape
    mid = tokens // 2
    core = core_ref[0]
    for c in range(count):
        mine = pl.ds(pl.multiple_of((2 * c + core) * cols, cols), cols)
        act[mine, :] = own_act[c]
        other = pl.ds(pl.multiple_of((2 * c + 1 - core) * cols, cols), cols)
        act[other, :mid] = peer_act[c, :, mid:]
        act[other, mid:] = peer_act[c, :, :mid]
    width = weights[0].shape[1]
    half = cols // 2
    low = jnp.concatenate([weight[:half] for weight in weights], axis=0)
    parts = jnp.dot(low, act[:width], preferred_element_type=F32)
    high = jnp.concatenate([weight[half:] for weight in weights], axis=0)
    parts += jnp.dot(high, act[width:], preferred_element_type=F32)
    for k in range(count):
        place = place_of(chip_ref[0], k)
        own_out[place] = parts[k * half : (k + 1) * half, :mid]
        peer_out[place] = parts[k * half : (k + 1) * half, mid:]


def mlp_second(chip, core, own_act, peer_act, weights):
    count, cols, tokens = own_act.shape
    shape = (count, cols // 2, tokens // 2)
    return pl.pallas_call(
        second_body,
        out_shape=(jax.ShapeDtypeStruct(shape, F32), jax.ShapeDtypeStruct(shape, F32)),
        grid=(1,),
        in_specs=[pl.BlockSpec(memory_space=pltpu.SMEM)] * 2
        + [whole(own_act), whole(peer_act)]
        + [half_of(x, cols, 1) for x in weights],
        out_specs=(pl.BlockSpec(shape, lambda i: (0, 0, 0)),) * 2,
        scratch_shapes=[pltpu.VMEM((2 * count * cols, tokens), BF16)],
        compiler_params=pltpu.CompilerParams(vmem_limit_bytes=28 << 20),
        cost_estimate=pl.CostEstimate(flops=1000, bytes_accessed=1000, transcendentals=0),
        name="mlp_second",
    )(chip, core, own_act, peer_act, *weights)


def last_body(
    core_ref, live_ref, gap_ref, own_part, peer_part, updated, mods, finals, final_t, latent,
    velocity, next_latent, scaled, top, bottom, mlp_t,
):
    count, half, _ = own_part.shape
    for source, parity in ((own_part, core_ref[0]), (peer_part, 1 - core_ref[0])):
        for c in range(count):
            start = pl.multiple_of((2 * c + parity) * half, half)
            mlp_t[pl.ds(start, half), :] = source[c]
    refined = updated[...] + mods[5:6] * mlp_t[...].T
    final_in = layer_norm(refined, finals[0:1], finals[1:2])
    predicted = lax.dot_general(
        final_in, final_t[...], (((1,), (1,)), ((), ())), preferred_element_type=F32
    )
    live = jnp.full(predicted.shape, live_ref[0], jnp.int32) != 0
    moved = latent[...] + gap_ref[0] * predicted
    inner = (moved / vae_scale + vae_offset).astype(F32)
    velocity[...] = jnp.where(live, predicted, 0.0)
    next_latent[...] = jnp.where(live, moved, 0.0)
    inner = jnp.where(live, inner, 0.0).astype(BF16)
    scaled[...] = inner
    lanes = inner.shape[1] // 2
    top[...] = inner[:W_P, :lanes]
    bottom[...] = inner[inner.shape[0] - W_P :, lanes:]


def last(core, live, gap, own_part, peer_part, updated, mods, finals, final_t, latent):
    rows, width = updated.shape
    cols = final_t.shape[0]
    smem = pl.BlockSpec(memory_space=pltpu.SMEM)
    inputs = (own_part, peer_part, updated, mods, finals, final_t, latent)
    shapes = ((rows, cols), (rows, cols), (rows, cols), (W_P, cols // 2), (W_P, cols // 2))
    return pl.pallas_call(
        last_body,
        out_shape=(
            jax.ShapeDtypeStruct((rows, cols), F32),
            jax.ShapeDtypeStruct((rows, cols), F32),
            jax.ShapeDtypeStruct((rows, cols), BF16),
            jax.ShapeDtypeStruct((W_P, cols // 2), BF16),
            jax.ShapeDtypeStruct((W_P, cols // 2), BF16),
        ),
        grid=(1,),
        in_specs=[smem] * 3 + [whole(x) for x in inputs],
        out_specs=tuple(pl.BlockSpec(x, lambda i: (0, 0)) for x in shapes),
        scratch_shapes=[pltpu.VMEM((width, rows), F32)],
        compiler_params=pltpu.CompilerParams(vmem_limit_bytes=12 << 20),
        cost_estimate=pl.CostEstimate(flops=1000, bytes_accessed=1000, transcendentals=0),
        name="last",
    )(core, live, gap, *inputs)


def conv_body(live_ref, scaled, before, after, weights, bias, out):
    lanes = before.shape[1]
    lines = [before[...]]
    for r in range(scaled.shape[0] // W_P):
        rows = scaled[r * W_P : (r + 1) * W_P]
        lines += [rows[:, :lanes], rows[:, lanes:]]
    lines.append(after[...])
    grid = jnp.concatenate([line.astype(F32) for line in lines], axis=1).astype(BF16)
    pixels = 2 * W_P
    pixel = lax.broadcasted_iota(jnp.int32, (pixels, W_P), 0)
    patch = lax.broadcasted_iota(jnp.int32, (pixels, W_P), 1)
    half, odd = pixel // 2, pixel % 2
    shifted = []
    for parity, offset in ((0, -1), (0, 0), (1, 0), (1, 1)):
        pick = jnp.logical_and(odd == parity, patch == half + offset)
        pick = jnp.where(pick, 1.0, 0.0).astype(BF16)
        shifted.append(jnp.dot(pick, grid, preferred_element_type=F32).astype(BF16))
    live = live_ref[0] != 0
    for line in range(out.shape[0]):
        total = jnp.zeros((pixels, out.shape[2]), F32)
        for k in range(4):
            window = shifted[k][:, line * lanes : (line + 3) * lanes]
            total += jnp.dot(window, weights[k], preferred_element_type=F32)
        total = jnp.where(live, total + bias[...], 0.0)
        out[line] = total.astype(BF16)


def convolve(live, scaled, before, after, weights, bias):
    lines = 2 * scaled.shape[0] // W_P
    shape = (lines, 2 * W_P, weights.shape[2])
    inputs = (scaled, before, after, weights, bias)
    return pl.pallas_call(
        conv_body,
        out_shape=jax.ShapeDtypeStruct(shape, BF16),
        grid=(1,),
        in_specs=[pl.BlockSpec(memory_space=pltpu.SMEM)] + [whole(x) for x in inputs],
        out_specs=pl.BlockSpec(shape, lambda i: (0, 0, 0)),
        compiler_params=pltpu.CompilerParams(vmem_limit_bytes=12 << 20),
        cost_estimate=pl.CostEstimate(flops=1000, bytes_accessed=1000, transcendentals=0),
        name="convolve",
    )(live, *inputs)


def conv_weights(conv_weight):
    taps = conv_weight.reshape(3, 3, CH, -1)
    none = jnp.zeros_like(taps[:, 0])
    pairs = ((none, taps[:, 0]), (taps[:, 1], taps[:, 2]), (taps[:, 0], taps[:, 1]), (taps[:, 2], none))
    return jnp.stack([jnp.stack(pair, axis=1).reshape(6 * CH, -1) for pair in pairs])


def per_device(
    hidden,
    text_hidden,
    latent,
    image_mod,
    text_mod,
    final_mod,
    counts,
    step_index,
    qkv_weight,
    text_weight,
    out_weight,
    mlp_in_weight,
    mlp_out_weight,
    final_weight,
    conv_weight,
    conv_bias,
):
    tok_rows, width = hidden.shape[1:]
    width_attn = HEADS * HEAD
    blocks = lax.axis_size("blk")
    blk, img = lax.axis_index("blk"), lax.axis_index("img")
    chip, core = img // 2, img % 2
    mods = image_mod[0]
    chip, core = chip[None], core[None]

    qkv_t = qkv_weight.T
    mlp_mine = jnp.concatenate(
        [mlp_in_weight.T, mlp_out_weight[:width].T, mlp_out_weight[width:].T], axis=0
    )
    gain, qkv_side = lax.optimization_barrier((1.0 + mods[1], qkv_t))
    image_in = modulate(hidden[0], mods[0], gain)
    mlp_mine, image_in = lax.optimization_barrier((mlp_mine, image_in))
    qkv_near = ring_first(qkv_t, qkv_side)
    qkv_next = ring_second(*qkv_near)
    far = jnp.concatenate(qkv_next[:2], axis=0)
    side_left, side_right, mlp_mine = lax.optimization_barrier((*qkv_next[2:], mlp_mine))
    qkv_far = far, swap(far, "img", 2)
    qkv_pieces = [qkv_t, *qkv_near, qkv_far[0], *qkv_next[2:], qkv_far[1]]
    mlp_near = ring_first(mlp_mine, mlp_mine)

    peer_in = swap(image_in, "img", 1)
    ready, peer_in = lax.optimization_barrier((marker(qkv_far[1]), peer_in))
    mine, theirs = project_qkv(chip, ready, image_in, peer_in, qkv_pieces)
    other = swap(theirs, "img", 1)
    heads = place_heads(core, mine, other, blocks)
    head = jnp.minimum(blk, HEADS - 1)
    right, head = lax.optimization_barrier((mlp_near[1], head))
    mlp_near = (mlp_near[0], right, mlp_near[2])
    parts = lax.all_to_all(heads, "blk", 0, 0, tiled=True)
    text_rows = tok_rows * pl.cdiv(text_hidden.shape[1], tok_rows)
    text_kv = text_keys(head[None], text_hidden[0], text_mod[0], text_weight, text_rows)

    mlp_next = ring_second(*mlp_near)
    mark = marker(*mlp_near)
    parts, mark, text_kv = lax.optimization_barrier((parts, mark, text_kv))
    mixed = attend(counts, parts, text_kv, mark)
    mixed, low, high = lax.optimization_barrier((mixed, mlp_next[0], mlp_next[1]))
    peer_low, peer_high = swap(low, "img", 2), swap(high, "img", 2)
    mixed = lax.all_to_all(mixed, "blk", 0, 0, tiled=True)[:HEADS].reshape(width_attn, tok_rows)
    near_pieces, next_pieces = [mlp_mine, *mlp_near], list(mlp_next[2:])

    latent_p = latent[0].reshape(-1, 2, W_P, 2 * CH).transpose(0, 2, 1, 3)
    latent_p = latent_p.reshape(tok_rows, 4 * CH)
    conv_w = conv_weights(conv_weight)
    live = (blk * tok_rows < counts).astype(jnp.int32)
    step_value = step_index.astype(F32)
    gap = plan(step_value + 1.0) - plan(step_value)
    mixed, latent_p, conv_w = lax.optimization_barrier((mixed, latent_p, conv_w))
    updated, mlp_in = middle(mixed, hidden[0], mods, out_weight, marker(peer_low, peer_high, *next_pieces))
    mlp_cols = mlp_in_weight.shape[1]
    peer_mlp = swap(mlp_in, "img", 1)
    first_pieces = near_pieces + [low] + next_pieces + [peer_low]
    act = mlp_first(chip, mlp_in, peer_mlp, first_pieces, mlp_cols)
    peer_act = swap(act, "img", 1)
    own_part, sent_part = mlp_second(
        chip, core, act, peer_act, near_pieces + [high] + next_pieces + [peer_high]
    )
    peer_part = swap(sent_part, "img", 1)
    velocity, next_lat, scaled, top, bottom = last(
        core, live, gap, own_part, peer_part, updated, mods, final_mod[0], final_weight.T, latent_p
    )
    size = blocks
    before = lax.ppermute(bottom, "blk", [(i, i + 1) for i in range(size - 1)])
    after = lax.ppermute(top, "blk", [(i + 1, i) for i in range(size - 1)])
    feature = convolve(live, scaled, before, after, conv_w, conv_bias[None])

    def by_rows(x):
        return x.reshape(-1, W_P, 2, 2 * CH).transpose(0, 2, 1, 3).reshape(latent[0].shape)

    return (by_rows(velocity)[None], by_rows(next_lat)[None], feature[None])


def solution(mesh):
    placed = (
        P("img", "blk", None),
        P("img", None, None),
        P("img", "blk", None),
        P("img", None, None),
        P("img", None, None),
        P("img", None, None),
        P("img"),
        P("img"),
        P(None, "img"),
        P(),
        P(),
        P(None, "img"),
        P(None, "img"),
        P(),
        P(),
        P(),
    )
    return jax.shard_map(
        per_device,
        mesh=mesh,
        in_specs=placed,
        out_specs=(P("img", "blk", None), P("img", "blk", None), P("img", "blk", None, None)),
        check_vma=False,
    )
```

```python
import jax
import jax.numpy as jnp
from jax import lax
from jax.experimental import pallas as pl
from jax.experimental.pallas import tpu as pltpu
from jax.sharding import PartitionSpec as P

HEAD = 64
CH = 16
HEADS = 12
W_P = 64
STEPS = 8

norm_eps = 1e-06
sigma_shift = 3.0
vae_scale = 1.5305
vae_offset = 0.0609
masked_score = -1e30

F32 = jnp.float32
BF16 = jnp.bfloat16


def modulate(inputs, shift_row, gain_row):
    values = inputs.astype(F32)
    center = jnp.mean(values, axis=-1, keepdims=True)
    spread = jnp.mean(jnp.square(values - center), axis=-1, keepdims=True)
    normed = (values - center) * lax.rsqrt(spread + norm_eps)
    return (normed * gain_row + shift_row).astype(BF16)


def plan(step_value):
    remain = 1.0 - step_value / STEPS
    return sigma_shift * remain / (1.0 + (sigma_shift - 1.0) * remain)


def swap(x, axis, bits):
    return lax.ppermute(x, axis, [(i, i ^ bits) for i in range(lax.axis_size(axis))])


def vmem_specs(count):
    return [pl.BlockSpec(memory_space=pltpu.VMEM)] * count


def whole(x):
    return pl.BlockSpec(x.shape, lambda i: (0,) * x.ndim)


OFFSETS = ((0, 0), (-1, 0), (1, 0), (0, 1), (2, 0), (-1, 1), (1, 1), (2, 1))


def ring(x, axis, step):
    size = lax.axis_size(axis)
    return lax.ppermute(x, axis, [(i, (i + step) % size) for i in range(size)])


def ring_first(x, side):
    return ring(x, "img", 4), ring(x, "img", -4), swap(side, "img", 2)


def ring_second(left, right, across):
    half = left.shape[0] // 2
    return (
        ring(left[:half], "img", 4),
        ring(right[half:], "img", -4),
        ring(across, "img", 4),
        ring(across, "img", -4),
    )


def place_of(chip, k):
    dx, dy = OFFSETS[k]
    column = jnp.bitwise_and(chip // 2 + dx + 4, 3)
    return 2 * column + jnp.bitwise_xor(jnp.bitwise_and(chip, 1), dy)


def qkv_body(chip_ref, ready, own_x, peer_x, *refs):
    weights, (own_out, peer_out) = refs[:-2], refs[-2:]
    rows = own_x.shape[0]
    both = jnp.concatenate([own_x[...], peer_x[...]], axis=0)
    cols = own_out.shape[1]
    stacked = jnp.concatenate([weight[...] for weight in weights], axis=0)
    parts = lax.dot_general(
        stacked, both, (((1,), (1,)), ((), ())), preferred_element_type=F32
    ).astype(BF16)
    for k in range(len(weights)):
        place = place_of(chip_ref[0], k)
        own_out[place] = parts[k * cols : (k + 1) * cols, :rows]
        peer_out[place] = parts[k * cols : (k + 1) * cols, rows:]


def project_qkv(chip, ready, own_x, peer_x, weights):
    cols, rows = weights[0].shape[0], own_x.shape[0]
    shape = (len(weights), cols, rows)
    inputs = (ready, own_x, peer_x, *weights)
    return pl.pallas_call(
        qkv_body,
        out_shape=(jax.ShapeDtypeStruct(shape, BF16),) * 2,
        grid=(1,),
        in_specs=[pl.BlockSpec(memory_space=pltpu.SMEM)] + [whole(x) for x in inputs],
        out_specs=(pl.BlockSpec(shape, lambda i: (0, 0, 0)),) * 2,
        compiler_params=pltpu.CompilerParams(vmem_limit_bytes=20 << 20),
        cost_estimate=pl.CostEstimate(flops=1000, bytes_accessed=1000, transcendentals=0),
        name="project_qkv",
    )(chip, *inputs)


def heads_body(core_ref, mine, other, out):
    count, cols, _ = mine.shape
    step = 16
    per_shard, per_head = cols // step, HEAD // step
    section = HEADS * per_head

    def copy(sources):
        for c in range(count):
            for parity, source in enumerate(sources):
                for j in range(per_shard):
                    piece = (2 * c + parity) * per_shard + j
                    kind, rest = piece // section, piece % section
                    start = kind * HEAD + rest % per_head * step
                    rows = source[c, j * step : (j + 1) * step]
                    out[rest // per_head, start : start + step] = rows

    @pl.when(core_ref[0] == 0)
    def _():
        copy((mine, other))

    @pl.when(core_ref[0] != 0)
    def _():
        copy((other, mine))

    out[HEADS:] = jnp.zeros((out.shape[0] - HEADS,) + out.shape[1:], BF16)


def place_heads(core, mine, other, blocks):
    shape = (blocks, 3 * HEAD, mine.shape[2])
    return pl.pallas_call(
        heads_body,
        out_shape=jax.ShapeDtypeStruct(shape, BF16),
        grid=(1,),
        in_specs=[pl.BlockSpec(memory_space=pltpu.SMEM), whole(mine), whole(other)],
        out_specs=pl.BlockSpec(shape, lambda i: (0, 0, 0)),
        compiler_params=pltpu.CompilerParams(vmem_limit_bytes=6 << 20),
        cost_estimate=pl.CostEstimate(flops=1000, bytes_accessed=1000, transcendentals=0),
        name="place_heads",
    )(core, mine, other)


def text_body(head_ref, hidden, mods, key_w, value_w, out, turned):
    odd = head_ref[0] % 2 != 0
    rows = hidden.shape[0]
    states = layer_norm(hidden[...].astype(F32), mods[0:1], mods[1:2])
    turned[...] = jnp.zeros_like(turned)
    for part, weight in enumerate((key_w, value_w)):
        turned[:rows, :] = jnp.dot(states, weight[...], preferred_element_type=F32)
        both = turned[...].T
        chosen = jnp.where(odd, both[HEAD:], both[:HEAD])
        out[part * HEAD : (part + 1) * HEAD, :] = chosen.astype(BF16)


def text_keys(head, hidden, mods, weight, rows):
    width = hidden.shape[1]
    pair = 2 * HEAD
    values_at = HEADS * HEAD // pair
    return pl.pallas_call(
        text_body,
        out_shape=jax.ShapeDtypeStruct((pair, rows), BF16),
        grid_spec=pltpu.PrefetchScalarGridSpec(
            num_scalar_prefetch=1,
            grid=(1,),
            in_specs=[
                pl.BlockSpec(hidden.shape, lambda i, h: (0, 0)),
                pl.BlockSpec(mods.shape, lambda i, h: (0, 0)),
                pl.BlockSpec((width, pair), lambda i, h: (0, h[0] // 2)),
                pl.BlockSpec((width, pair), lambda i, h: (0, values_at + h[0] // 2)),
            ],
            out_specs=pl.BlockSpec((pair, rows), lambda i, h: (0, 0)),
            scratch_shapes=[pltpu.VMEM((rows, pair), F32)],
        ),
        compiler_params=pltpu.CompilerParams(vmem_limit_bytes=10 << 20),
        cost_estimate=pl.CostEstimate(flops=1000, bytes_accessed=1000, transcendentals=0),
        name="text_keys",
    )(head, hidden, mods, weight, weight)


def mark_body(*refs):
    refs[-1][...] = refs[0][...]


def marker(*arrays):
    return pl.pallas_call(
        mark_body,
        out_shape=jax.ShapeDtypeStruct((16, 128), BF16),
        grid=(1,),
        in_specs=[pl.BlockSpec((16, 128), lambda i: (0, 0))] * len(arrays),
        out_specs=pl.BlockSpec((16, 128), lambda i: (0, 0)),
        compiler_params=pltpu.CompilerParams(vmem_limit_bytes=1 << 20),
        cost_estimate=pl.CostEstimate(
            flops=100_000_000_000, bytes_accessed=100_000_000, transcendentals=0
        ),
        name="marker",
    )(*arrays)


def attend_body(count_ref, parts, text, mark, out, keys, values, queries):
    blocks, _, rows = parts.shape
    text_blocks = text.shape[1] // rows
    text_len = 154
    tile = 2 * rows
    lane = lax.broadcasted_iota(jnp.int32, (HEAD, rows), 1)
    row = lax.broadcasted_iota(jnp.int32, (HEAD, rows), 0)
    top = row == 0
    zeros = jnp.zeros((HEAD, rows), F32)
    ones = jnp.where(top, 1.0, 0.0).astype(F32)

    def place(index, key_part, value_part, limit):
        cols = slice(index * rows, (index + 1) * rows)
        keys[:HEAD, cols] = key_part
        bias = jnp.where(jnp.logical_and(top, lane >= limit), masked_score, 0.0)
        keys[HEAD:, cols] = bias.astype(BF16)
        full = jnp.concatenate([value_part.astype(F32), zeros], axis=0)
        values[cols, :] = full.T.astype(BF16)

    for b in range(blocks):
        part = parts[b]
        place(b, part[HEAD : 2 * HEAD], part[2 * HEAD :], count_ref[0] - b * rows)
        scaled = part[:HEAD].astype(F32) * 0.125
        full = jnp.concatenate([scaled, ones], axis=0)
        queries[b * rows : (b + 1) * rows, :] = full.T.astype(BF16)
    for t in range(text_blocks):
        cols = slice(t * rows, (t + 1) * rows)
        place(blocks + t, text[:HEAD, cols], text[HEAD:, cols], text_len - t * rows)

    def step(t, carry):
        first = pl.multiple_of(t * tile, tile)
        scores = jnp.dot(queries[pl.ds(first, tile), :], keys[...], preferred_element_type=F32)
        top_score = jnp.max(scores, axis=1, keepdims=True)
        numer = jnp.exp(scores - top_score)
        total = jnp.sum(numer, axis=1, keepdims=True)
        mixed = jnp.dot(numer.astype(BF16), values[...], preferred_element_type=F32) / total
        turned = mixed.T[:HEAD].astype(BF16)
        out[2 * t] = turned[:, :rows]
        out[2 * t + 1] = turned[:, rows:]
        return carry

    lax.fori_loop(0, blocks // 2, step, 0)


def attend(count, parts, text, mark):
    blocks, _, rows = parts.shape
    keys = blocks * rows + text.shape[1]
    queries = blocks * rows
    return pl.pallas_call(
        attend_body,
        out_shape=jax.ShapeDtypeStruct((blocks, HEAD, rows), BF16),
        in_specs=[pl.BlockSpec(memory_space=pltpu.SMEM)] + vmem_specs(3),
        out_specs=vmem_specs(1)[0],
        scratch_shapes=[
            pltpu.VMEM((2 * HEAD, keys), BF16),
            pltpu.VMEM((keys, 2 * HEAD), BF16),
            pltpu.VMEM((queries, 2 * HEAD), BF16),
        ],
        compiler_params=pltpu.CompilerParams(vmem_limit_bytes=20 << 20),
        cost_estimate=pl.CostEstimate(flops=1000, bytes_accessed=1000, transcendentals=0),
        name="attend",
    )(count, parts, text, mark)


def layer_norm(values, shift_row, scale_row):
    center = jnp.mean(values, axis=-1, keepdims=True)
    spread = jnp.mean(jnp.square(values - center), axis=-1, keepdims=True)
    normed = (values - center) * lax.rsqrt(spread + norm_eps)
    return (normed * (1.0 + scale_row) + shift_row).astype(BF16)


def gelu(v):
    return 0.5 * v * (1.0 + jnp.tanh(0.7978845608028654 * (v + 0.044715 * v * v * v)))


def middle_body(mixed, hidden, mods, out_w, mark, updated, mlp_in):
    attended = mixed[...].astype(F32).T.astype(BF16)
    projected = jnp.dot(attended, out_w[...], preferred_element_type=F32)
    now = hidden[...].astype(F32) + mods[2:3] * projected
    updated[...] = now
    mlp_in[...] = layer_norm(now, mods[3:4], mods[4:5])


def middle(mixed, hidden, mods, out_w, mark):
    rows, width = hidden.shape
    inputs = (mixed, hidden, mods, out_w, mark)
    return pl.pallas_call(
        middle_body,
        out_shape=(
            jax.ShapeDtypeStruct((rows, width), F32),
            jax.ShapeDtypeStruct((rows, width), BF16),
        ),
        grid=(1,),
        in_specs=[whole(x) for x in inputs],
        out_specs=(pl.BlockSpec((rows, width), lambda i: (0, 0)),) * 2,
        compiler_params=pltpu.CompilerParams(vmem_limit_bytes=14 << 20),
        cost_estimate=pl.CostEstimate(flops=1000, bytes_accessed=1000, transcendentals=0),
        name="middle",
    )(*inputs)


def first_body(chip_ref, own_x, peer_x, *refs):
    weights, out = refs[:-1], refs[-1]
    both = jnp.concatenate([own_x[...], peer_x[...]], axis=0)
    cols = out.shape[1]
    stacked = jnp.concatenate([weight[...] for weight in weights], axis=0)
    parts = lax.dot_general(stacked, both, (((1,), (1,)), ((), ())), preferred_element_type=F32)
    for k in range(len(weights)):
        out[place_of(chip_ref[0], k)] = gelu(parts[k * cols : (k + 1) * cols]).astype(BF16)


def half_of(x, cols, index):
    position = index if x.shape[0] > cols else 0
    return pl.BlockSpec((cols, x.shape[1]), lambda i: (position, 0))


def mlp_first(chip, own_x, peer_x, weights, cols):
    rows = own_x.shape[0]
    count = len(weights)
    shape = (count, cols, 2 * rows)
    return pl.pallas_call(
        first_body,
        out_shape=jax.ShapeDtypeStruct(shape, BF16),
        grid=(1,),
        in_specs=[pl.BlockSpec(memory_space=pltpu.SMEM), whole(own_x), whole(peer_x)]
        + [half_of(x, cols, 0) for x in weights],
        out_specs=pl.BlockSpec(shape, lambda i: (0, 0, 0)),
        compiler_params=pltpu.CompilerParams(vmem_limit_bytes=28 << 20),
        cost_estimate=pl.CostEstimate(flops=1000, bytes_accessed=1000, transcendentals=0),
        name="mlp_first",
    )(chip, own_x, peer_x, *weights)


def second_body(chip_ref, core_ref, own_act, peer_act, *refs):
    weights, (far_low, far_high) = refs[:-5], refs[-5:-3]
    (own_out, peer_out), act = refs[-3:-1], refs[-1]
    count, cols, tokens = own_act.shape
    mid = tokens // 2
    core = core_ref[0]
    for c in range(count):
        mine = pl.ds(pl.multiple_of((2 * c + core) * cols, cols), cols)
        act[mine, :] = own_act[c]
        other = pl.ds(pl.multiple_of((2 * c + 1 - core) * cols, cols), cols)
        act[other, :mid] = peer_act[c, :, mid:]
        act[other, mid:] = peer_act[c, :, :mid]
    width = weights[0].shape[1]
    half = cols // 2
    low = jnp.concatenate([weight[:half] for weight in weights] + [far_low[...]], axis=0)
    parts = jnp.dot(low, act[:width], preferred_element_type=F32)
    high = jnp.concatenate([weight[half:] for weight in weights] + [far_high[...]], axis=0)
    parts += jnp.dot(high, act[width:], preferred_element_type=F32)
    for k in range(count):
        place = place_of(chip_ref[0], k)
        own_out[place] = parts[k * half : (k + 1) * half, :mid]
        peer_out[place] = parts[k * half : (k + 1) * half, mid:]


def mlp_second(chip, core, own_act, peer_act, weights, far):
    count, cols, tokens = own_act.shape
    shape = (count, cols // 2, tokens // 2)
    return pl.pallas_call(
        second_body,
        out_shape=(jax.ShapeDtypeStruct(shape, F32), jax.ShapeDtypeStruct(shape, F32)),
        grid=(1,),
        in_specs=[pl.BlockSpec(memory_space=pltpu.SMEM)] * 2
        + [whole(own_act), whole(peer_act)]
        + [half_of(x, cols, 1) for x in weights]
        + [whole(x) for x in far],
        out_specs=(pl.BlockSpec(shape, lambda i: (0, 0, 0)),) * 2,
        scratch_shapes=[pltpu.VMEM((2 * count * cols, tokens), BF16)],
        compiler_params=pltpu.CompilerParams(vmem_limit_bytes=28 << 20),
        cost_estimate=pl.CostEstimate(flops=1000, bytes_accessed=1000, transcendentals=0),
        name="mlp_second",
    )(chip, core, own_act, peer_act, *weights, *far)


def last_body(
    core_ref, live_ref, gap_ref, own_part, peer_part, updated, mods, finals, final_t, latent,
    velocity, next_latent, scaled, top, bottom, mlp_t,
):
    count, half, _ = own_part.shape
    for source, parity in ((own_part, core_ref[0]), (peer_part, 1 - core_ref[0])):
        for c in range(count):
            start = pl.multiple_of((2 * c + parity) * half, half)
            mlp_t[pl.ds(start, half), :] = source[c]
    refined = updated[...] + mods[5:6] * mlp_t[...].T
    final_in = layer_norm(refined, finals[0:1], finals[1:2])
    predicted = lax.dot_general(
        final_in, final_t[...], (((1,), (1,)), ((), ())), preferred_element_type=F32
    )
    live = jnp.full(predicted.shape, live_ref[0], jnp.int32) != 0
    moved = latent[...] + gap_ref[0] * predicted
    inner = (moved / vae_scale + vae_offset).astype(F32)
    velocity[...] = jnp.where(live, predicted, 0.0)
    next_latent[...] = jnp.where(live, moved, 0.0)
    inner = jnp.where(live, inner, 0.0).astype(BF16)
    scaled[...] = inner
    lanes = inner.shape[1] // 2
    top[...] = inner[:W_P, :lanes]
    bottom[...] = inner[inner.shape[0] - W_P :, lanes:]


def last(core, live, gap, own_part, peer_part, updated, mods, finals, final_t, latent):
    rows, width = updated.shape
    cols = final_t.shape[0]
    smem = pl.BlockSpec(memory_space=pltpu.SMEM)
    inputs = (own_part, peer_part, updated, mods, finals, final_t, latent)
    shapes = ((rows, cols), (rows, cols), (rows, cols), (W_P, cols // 2), (W_P, cols // 2))
    return pl.pallas_call(
        last_body,
        out_shape=(
            jax.ShapeDtypeStruct((rows, cols), F32),
            jax.ShapeDtypeStruct((rows, cols), F32),
            jax.ShapeDtypeStruct((rows, cols), BF16),
            jax.ShapeDtypeStruct((W_P, cols // 2), BF16),
            jax.ShapeDtypeStruct((W_P, cols // 2), BF16),
        ),
        grid=(1,),
        in_specs=[smem] * 3 + [whole(x) for x in inputs],
        out_specs=tuple(pl.BlockSpec(x, lambda i: (0, 0)) for x in shapes),
        scratch_shapes=[pltpu.VMEM((width, rows), F32)],
        compiler_params=pltpu.CompilerParams(vmem_limit_bytes=12 << 20),
        cost_estimate=pl.CostEstimate(flops=1000, bytes_accessed=1000, transcendentals=0),
        name="last",
    )(core, live, gap, *inputs)


def conv_body(live_ref, scaled, before, after, weights, bias, out):
    lanes = before.shape[1]
    lines = [before[...]]
    for r in range(scaled.shape[0] // W_P):
        rows = scaled[r * W_P : (r + 1) * W_P]
        lines += [rows[:, :lanes], rows[:, lanes:]]
    lines.append(after[...])
    grid = jnp.concatenate([line.astype(F32) for line in lines], axis=1).astype(BF16)
    pixels = 2 * W_P
    pixel = lax.broadcasted_iota(jnp.int32, (pixels, W_P), 0)
    patch = lax.broadcasted_iota(jnp.int32, (pixels, W_P), 1)
    half, odd = pixel // 2, pixel % 2
    shifted = []
    for parity, offset in ((0, -1), (0, 0), (1, 0), (1, 1)):
        pick = jnp.logical_and(odd == parity, patch == half + offset)
        pick = jnp.where(pick, 1.0, 0.0).astype(BF16)
        shifted.append(jnp.dot(pick, grid, preferred_element_type=F32).astype(BF16))
    live = live_ref[0] != 0
    for line in range(out.shape[0]):
        total = jnp.zeros((pixels, out.shape[2]), F32)
        for k in range(4):
            window = shifted[k][:, line * lanes : (line + 3) * lanes]
            total += jnp.dot(window, weights[k], preferred_element_type=F32)
        total = jnp.where(live, total + bias[...], 0.0)
        out[line] = total.astype(BF16)


def convolve(live, scaled, before, after, weights, bias):
    lines = 2 * scaled.shape[0] // W_P
    shape = (lines, 2 * W_P, weights.shape[2])
    inputs = (scaled, before, after, weights, bias)
    return pl.pallas_call(
        conv_body,
        out_shape=jax.ShapeDtypeStruct(shape, BF16),
        grid=(1,),
        in_specs=[pl.BlockSpec(memory_space=pltpu.SMEM)] + [whole(x) for x in inputs],
        out_specs=pl.BlockSpec(shape, lambda i: (0, 0, 0)),
        compiler_params=pltpu.CompilerParams(vmem_limit_bytes=12 << 20),
        cost_estimate=pl.CostEstimate(flops=1000, bytes_accessed=1000, transcendentals=0),
        name="convolve",
    )(live, *inputs)


def conv_weights(conv_weight):
    taps = conv_weight.reshape(3, 3, CH, -1)
    none = jnp.zeros_like(taps[:, 0])
    pairs = ((none, taps[:, 0]), (taps[:, 1], taps[:, 2]), (taps[:, 0], taps[:, 1]), (taps[:, 2], none))
    return jnp.stack([jnp.stack(pair, axis=1).reshape(6 * CH, -1) for pair in pairs])


def per_device(
    hidden,
    text_hidden,
    latent,
    image_mod,
    text_mod,
    final_mod,
    counts,
    step_index,
    qkv_weight,
    text_weight,
    out_weight,
    mlp_in_weight,
    mlp_out_weight,
    final_weight,
    conv_weight,
    conv_bias,
):
    tok_rows, width = hidden.shape[1:]
    width_attn = HEADS * HEAD
    blocks = lax.axis_size("blk")
    blk, img = lax.axis_index("blk"), lax.axis_index("img")
    chip, core = img // 2, img % 2
    mods = image_mod[0]
    chip, core = chip[None], core[None]

    qkv_t = qkv_weight.T
    mlp_mine = jnp.concatenate(
        [mlp_in_weight.T, mlp_out_weight[:width].T, mlp_out_weight[width:].T], axis=0
    )
    gain, qkv_side = lax.optimization_barrier((1.0 + mods[1], qkv_t))
    image_in = modulate(hidden[0], mods[0], gain)
    mlp_mine, image_in = lax.optimization_barrier((mlp_mine, image_in))
    qkv_near = ring_first(qkv_t, qkv_side)
    qkv_next = ring_second(*qkv_near)
    far = jnp.concatenate(qkv_next[:2], axis=0)
    side_left, side_right, mlp_mine = lax.optimization_barrier((*qkv_next[2:], mlp_mine))
    qkv_far = far, swap(far, "img", 2)
    qkv_pieces = [qkv_t, *qkv_near, qkv_far[0], *qkv_next[2:], qkv_far[1]]
    mlp_near = ring_first(mlp_mine, mlp_mine)

    peer_in = swap(image_in, "img", 1)
    ready, peer_in = lax.optimization_barrier((marker(qkv_far[1]), peer_in))
    mine, theirs = project_qkv(chip, ready, image_in, peer_in, qkv_pieces)
    other = swap(theirs, "img", 1)
    heads = place_heads(core, mine, other, blocks)
    head = jnp.minimum(blk, HEADS - 1)
    right, head = lax.optimization_barrier((mlp_near[1], head))
    mlp_near = (mlp_near[0], right, mlp_near[2])
    parts = lax.all_to_all(heads, "blk", 0, 0, tiled=True)
    text_rows = tok_rows * pl.cdiv(text_hidden.shape[1], tok_rows)
    text_kv = text_keys(head[None], text_hidden[0], text_mod[0], text_weight, text_rows)

    mlp_next = ring_second(*mlp_near)
    mark = marker(*mlp_near)
    parts, mark, text_kv = lax.optimization_barrier((parts, mark, text_kv))
    mixed = attend(counts, parts, text_kv, mark)
    mixed, low, high = lax.optimization_barrier((mixed, mlp_next[0], mlp_next[1]))
    peer_low = swap(low, "img", 2)
    quarter = mlp_next[2].shape[0] // 4
    far = (
        ring(mlp_next[2][2 * quarter : 3 * quarter], "img", 4),
        ring(mlp_next[3][3 * quarter :], "img", -4),
    )
    mixed = lax.all_to_all(mixed, "blk", 0, 0, tiled=True)[:HEADS].reshape(width_attn, tok_rows)
    near_pieces, next_pieces = [mlp_mine, *mlp_near], list(mlp_next[2:])

    latent_p = latent[0].reshape(-1, 2, W_P, 2 * CH).transpose(0, 2, 1, 3)
    latent_p = latent_p.reshape(tok_rows, 4 * CH)
    conv_w = conv_weights(conv_weight)
    live = (blk * tok_rows < counts).astype(jnp.int32)
    step_value = step_index.astype(F32)
    gap = plan(step_value + 1.0) - plan(step_value)
    mixed, latent_p, conv_w = lax.optimization_barrier((mixed, latent_p, conv_w))
    updated, mlp_in = middle(mixed, hidden[0], mods, out_weight, marker(peer_low, *next_pieces, *far))
    mlp_cols = mlp_in_weight.shape[1]
    peer_mlp = swap(mlp_in, "img", 1)
    first_pieces = near_pieces + [low] + next_pieces + [peer_low]
    act = mlp_first(chip, mlp_in, peer_mlp, first_pieces, mlp_cols)
    peer_act = swap(act, "img", 1)
    own_part, sent_part = mlp_second(
        chip, core, act, peer_act, near_pieces + [high] + next_pieces, far
    )
    peer_part = swap(sent_part, "img", 1)
    velocity, next_lat, scaled, top, bottom = last(
        core, live, gap, own_part, peer_part, updated, mods, final_mod[0], final_weight.T, latent_p
    )
    size = blocks
    before = lax.ppermute(bottom, "blk", [(i, i + 1) for i in range(size - 1)])
    after = lax.ppermute(top, "blk", [(i + 1, i) for i in range(size - 1)])
    feature = convolve(live, scaled, before, after, conv_w, conv_bias[None])

    def by_rows(x):
        return x.reshape(-1, W_P, 2, 2 * CH).transpose(0, 2, 1, 3).reshape(latent[0].shape)

    return (by_rows(velocity)[None], by_rows(next_lat)[None], feature[None])


def solution(mesh):
    placed = (
        P("img", "blk", None),
        P("img", None, None),
        P("img", "blk", None),
        P("img", None, None),
        P("img", None, None),
        P("img", None, None),
        P("img"),
        P("img"),
        P(None, "img"),
        P(),
        P(),
        P(None, "img"),
        P(None, "img"),
        P(),
        P(),
        P(),
    )
    return jax.shard_map(
        per_device,
        mesh=mesh,
        in_specs=placed,
        out_specs=(P("img", "blk", None), P("img", "blk", None), P("img", "blk", None, None)),
        check_vma=False,
    )
```

```python
import jax
import jax.numpy as jnp
from jax import lax
from jax.experimental import pallas as pl
from jax.experimental.pallas import tpu as pltpu
from jax.sharding import PartitionSpec as P

HEAD = 64
CH = 16
HEADS = 12
W_P = 64
STEPS = 8

norm_eps = 1e-06
sigma_shift = 3.0
vae_scale = 1.5305
vae_offset = 0.0609
masked_score = -1e30

F32 = jnp.float32
BF16 = jnp.bfloat16


def modulate(inputs, shift_row, gain_row):
    values = inputs.astype(F32)
    center = jnp.mean(values, axis=-1, keepdims=True)
    spread = jnp.mean(jnp.square(values - center), axis=-1, keepdims=True)
    normed = (values - center) * lax.rsqrt(spread + norm_eps)
    return (normed * gain_row + shift_row).astype(BF16)


def plan(step_value):
    remain = 1.0 - step_value / STEPS
    return sigma_shift * remain / (1.0 + (sigma_shift - 1.0) * remain)


def swap(x, axis, bits):
    return lax.ppermute(x, axis, [(i, i ^ bits) for i in range(lax.axis_size(axis))])


def vmem_specs(count):
    return [pl.BlockSpec(memory_space=pltpu.VMEM)] * count


def whole(x):
    return pl.BlockSpec(x.shape, lambda i: (0,) * x.ndim)


OFFSETS = ((0, 0), (-1, 0), (1, 0), (0, 1), (2, 0), (-1, 1), (1, 1), (2, 1))


def ring(x, axis, step):
    size = lax.axis_size(axis)
    return lax.ppermute(x, axis, [(i, (i + step) % size) for i in range(size)])


def ring_first(x, side):
    return ring(x, "img", 4), ring(x, "img", -4), swap(side, "img", 2)


def ring_second(left, right, across):
    half = left.shape[0] // 2
    return (
        ring(left[:half], "img", 4),
        ring(right[half:], "img", -4),
        ring(across, "img", 4),
        ring(across, "img", -4),
    )


def place_of(chip, k):
    dx, dy = OFFSETS[k]
    column = jnp.bitwise_and(chip // 2 + dx + 4, 3)
    return 2 * column + jnp.bitwise_xor(jnp.bitwise_and(chip, 1), dy)


def qkv_body(chip_ref, ready, own_x, peer_x, *refs):
    weights, (own_out, peer_out) = refs[:-2], refs[-2:]
    rows = own_x.shape[0]
    both = jnp.concatenate([own_x[...], peer_x[...]], axis=0)
    cols = own_out.shape[1]
    stacked = jnp.concatenate([weight[...] for weight in weights], axis=0)
    parts = lax.dot_general(
        stacked, both, (((1,), (1,)), ((), ())), preferred_element_type=F32
    ).astype(BF16)
    for k in range(len(weights)):
        place = place_of(chip_ref[0], k)
        own_out[place] = parts[k * cols : (k + 1) * cols, :rows]
        peer_out[place] = parts[k * cols : (k + 1) * cols, rows:]


def project_qkv(chip, ready, own_x, peer_x, weights):
    cols, rows = weights[0].shape[0], own_x.shape[0]
    shape = (len(weights), cols, rows)
    inputs = (ready, own_x, peer_x, *weights)
    return pl.pallas_call(
        qkv_body,
        out_shape=(pltpu.HBM(shape, BF16), jax.ShapeDtypeStruct(shape, BF16)),
        grid=(1,),
        in_specs=[pl.BlockSpec(memory_space=pltpu.SMEM)] + [whole(x) for x in inputs],
        out_specs=(pl.BlockSpec(shape, lambda i: (0, 0, 0)),) * 2,
        compiler_params=pltpu.CompilerParams(vmem_limit_bytes=20 << 20),
        cost_estimate=pl.CostEstimate(flops=1000, bytes_accessed=1000, transcendentals=0),
        name="project_qkv",
    )(chip, *inputs)


def heads_body(core_ref, mine, other, out):
    count, cols, _ = mine.shape
    step = 16
    per_shard, per_head = cols // step, HEAD // step
    section = HEADS * per_head

    def copy(sources):
        for c in range(count):
            for parity, source in enumerate(sources):
                for j in range(per_shard):
                    piece = (2 * c + parity) * per_shard + j
                    kind, rest = piece // section, piece % section
                    start = kind * HEAD + rest % per_head * step
                    rows = source[c, j * step : (j + 1) * step]
                    out[rest // per_head, start : start + step] = rows

    @pl.when(core_ref[0] == 0)
    def _():
        copy((mine, other))

    @pl.when(core_ref[0] != 0)
    def _():
        copy((other, mine))

    out[HEADS:] = jnp.zeros((out.shape[0] - HEADS,) + out.shape[1:], BF16)


def place_heads(core, mine, other, blocks):
    shape = (blocks, 3 * HEAD, mine.shape[2])
    mine = pltpu.with_memory_space_constraint(mine, pltpu.HBM)
    return pl.pallas_call(
        heads_body,
        out_shape=pltpu.HBM(shape, BF16),
        grid=(1,),
        in_specs=[pl.BlockSpec(memory_space=pltpu.SMEM), whole(mine), whole(other)],
        out_specs=pl.BlockSpec(shape, lambda i: (0, 0, 0)),
        compiler_params=pltpu.CompilerParams(vmem_limit_bytes=6 << 20),
        cost_estimate=pl.CostEstimate(flops=1000, bytes_accessed=1000, transcendentals=0),
        name="place_heads",
    )(core, mine, other)


def text_body(head_ref, hidden, mods, key_w, value_w, out, turned):
    odd = head_ref[0] % 2 != 0
    rows = hidden.shape[0]
    states = layer_norm(hidden[...].astype(F32), mods[0:1], mods[1:2])
    turned[...] = jnp.zeros_like(turned)
    for part, weight in enumerate((key_w, value_w)):
        turned[:rows, :] = jnp.dot(states, weight[...], preferred_element_type=F32)
        both = turned[...].T
        chosen = jnp.where(odd, both[HEAD:], both[:HEAD])
        out[part * HEAD : (part + 1) * HEAD, :] = chosen.astype(BF16)


def text_keys(head, hidden, mods, weight, rows):
    width = hidden.shape[1]
    pair = 2 * HEAD
    values_at = HEADS * HEAD // pair
    return pl.pallas_call(
        text_body,
        out_shape=jax.ShapeDtypeStruct((pair, rows), BF16),
        grid_spec=pltpu.PrefetchScalarGridSpec(
            num_scalar_prefetch=1,
            grid=(1,),
            in_specs=[
                pl.BlockSpec(hidden.shape, lambda i, h: (0, 0)),
                pl.BlockSpec(mods.shape, lambda i, h: (0, 0)),
                pl.BlockSpec((width, pair), lambda i, h: (0, h[0] // 2)),
                pl.BlockSpec((width, pair), lambda i, h: (0, values_at + h[0] // 2)),
            ],
            out_specs=pl.BlockSpec((pair, rows), lambda i, h: (0, 0)),
            scratch_shapes=[pltpu.VMEM((rows, pair), F32)],
        ),
        compiler_params=pltpu.CompilerParams(vmem_limit_bytes=10 << 20),
        cost_estimate=pl.CostEstimate(flops=1000, bytes_accessed=1000, transcendentals=0),
        name="text_keys",
    )(head, hidden, mods, weight, weight)


def mark_body(*refs):
    refs[-1][...] = refs[0][...]


def marker(*arrays):
    return pl.pallas_call(
        mark_body,
        out_shape=jax.ShapeDtypeStruct((16, 128), BF16),
        grid=(1,),
        in_specs=[pl.BlockSpec((16, 128), lambda i: (0, 0))] * len(arrays),
        out_specs=pl.BlockSpec((16, 128), lambda i: (0, 0)),
        compiler_params=pltpu.CompilerParams(vmem_limit_bytes=1 << 20),
        cost_estimate=pl.CostEstimate(
            flops=100_000_000_000, bytes_accessed=100_000_000, transcendentals=0
        ),
        name="marker",
    )(*arrays)


def attend_body(count_ref, parts, text, mark, out, keys, values, queries):
    blocks, _, rows = parts.shape
    text_blocks = text.shape[1] // rows
    text_len = 154
    tile = 2 * rows
    lane = lax.broadcasted_iota(jnp.int32, (HEAD, rows), 1)
    row = lax.broadcasted_iota(jnp.int32, (HEAD, rows), 0)
    top = row == 0
    zeros = jnp.zeros((HEAD, rows), F32)
    ones = jnp.where(top, 1.0, 0.0).astype(F32)

    def place(index, key_part, value_part, limit):
        cols = slice(index * rows, (index + 1) * rows)
        keys[:HEAD, cols] = key_part
        bias = jnp.where(jnp.logical_and(top, lane >= limit), masked_score, 0.0)
        keys[HEAD:, cols] = bias.astype(BF16)
        full = jnp.concatenate([value_part.astype(F32), zeros], axis=0)
        values[cols, :] = full.T.astype(BF16)

    for b in range(blocks):
        part = parts[b]
        place(b, part[HEAD : 2 * HEAD], part[2 * HEAD :], count_ref[0] - b * rows)
        scaled = part[:HEAD].astype(F32) * 0.125
        full = jnp.concatenate([scaled, ones], axis=0)
        queries[b * rows : (b + 1) * rows, :] = full.T.astype(BF16)
    for t in range(text_blocks):
        cols = slice(t * rows, (t + 1) * rows)
        place(blocks + t, text[:HEAD, cols], text[HEAD:, cols], text_len - t * rows)

    def step(t, carry):
        first = pl.multiple_of(t * tile, tile)
        scores = jnp.dot(queries[pl.ds(first, tile), :], keys[...], preferred_element_type=F32)
        top_score = jnp.max(scores, axis=1, keepdims=True)
        numer = jnp.exp(scores - top_score)
        total = jnp.sum(numer, axis=1, keepdims=True)
        mixed = jnp.dot(numer.astype(BF16), values[...], preferred_element_type=F32) / total
        turned = mixed.T[:HEAD].astype(BF16)
        out[2 * t] = turned[:, :rows]
        out[2 * t + 1] = turned[:, rows:]
        return carry

    lax.fori_loop(0, blocks // 2, step, 0)


def attend(count, parts, text, mark):
    blocks, _, rows = parts.shape
    keys = blocks * rows + text.shape[1]
    queries = blocks * rows
    return pl.pallas_call(
        attend_body,
        out_shape=jax.ShapeDtypeStruct((blocks, HEAD, rows), BF16),
        in_specs=[pl.BlockSpec(memory_space=pltpu.SMEM)] + vmem_specs(3),
        out_specs=vmem_specs(1)[0],
        scratch_shapes=[
            pltpu.VMEM((2 * HEAD, keys), BF16),
            pltpu.VMEM((keys, 2 * HEAD), BF16),
            pltpu.VMEM((queries, 2 * HEAD), BF16),
        ],
        compiler_params=pltpu.CompilerParams(vmem_limit_bytes=20 << 20),
        cost_estimate=pl.CostEstimate(flops=1000, bytes_accessed=1000, transcendentals=0),
        name="attend",
    )(count, parts, text, mark)


def layer_norm(values, shift_row, scale_row):
    center = jnp.mean(values, axis=-1, keepdims=True)
    spread = jnp.mean(jnp.square(values - center), axis=-1, keepdims=True)
    normed = (values - center) * lax.rsqrt(spread + norm_eps)
    return (normed * (1.0 + scale_row) + shift_row).astype(BF16)


def gelu(v):
    return 0.5 * v * (1.0 + jnp.tanh(0.7978845608028654 * (v + 0.044715 * v * v * v)))


def middle_body(mixed, hidden, mods, out_w, mark, updated, mlp_in):
    attended = mixed[...].astype(F32).T.astype(BF16)
    projected = jnp.dot(attended, out_w[...], preferred_element_type=F32)
    now = hidden[...].astype(F32) + mods[2:3] * projected
    updated[...] = now
    mlp_in[...] = layer_norm(now, mods[3:4], mods[4:5])


def middle(mixed, hidden, mods, out_w, mark):
    rows, width = hidden.shape
    inputs = (mixed, hidden, mods, out_w, mark)
    return pl.pallas_call(
        middle_body,
        out_shape=(
            pltpu.HBM((rows, width), F32),
            jax.ShapeDtypeStruct((rows, width), BF16),
        ),
        grid=(1,),
        in_specs=[whole(x) for x in inputs],
        out_specs=(pl.BlockSpec((rows, width), lambda i: (0, 0)),) * 2,
        compiler_params=pltpu.CompilerParams(vmem_limit_bytes=14 << 20),
        cost_estimate=pl.CostEstimate(flops=1000, bytes_accessed=1000, transcendentals=0),
        name="middle",
    )(*inputs)


def first_body(chip_ref, own_x, peer_x, *refs):
    weights, out = refs[:-1], refs[-1]
    both = jnp.concatenate([own_x[...], peer_x[...]], axis=0)
    cols = out.shape[1]
    stacked = jnp.concatenate([weight[...] for weight in weights], axis=0)
    parts = lax.dot_general(stacked, both, (((1,), (1,)), ((), ())), preferred_element_type=F32)
    for k in range(len(weights)):
        out[place_of(chip_ref[0], k)] = gelu(parts[k * cols : (k + 1) * cols]).astype(BF16)


def half_of(x, cols, index):
    position = index if x.shape[0] > cols else 0
    return pl.BlockSpec((cols, x.shape[1]), lambda i: (position, 0))


def mlp_first(chip, own_x, peer_x, weights, cols):
    rows = own_x.shape[0]
    count = len(weights)
    shape = (count, cols, 2 * rows)
    return pl.pallas_call(
        first_body,
        out_shape=jax.ShapeDtypeStruct(shape, BF16),
        grid=(1,),
        in_specs=[pl.BlockSpec(memory_space=pltpu.SMEM), whole(own_x), whole(peer_x)]
        + [half_of(x, cols, 0) for x in weights],
        out_specs=pl.BlockSpec(shape, lambda i: (0, 0, 0)),
        compiler_params=pltpu.CompilerParams(vmem_limit_bytes=28 << 20),
        cost_estimate=pl.CostEstimate(flops=1000, bytes_accessed=1000, transcendentals=0),
        name="mlp_first",
    )(chip, own_x, peer_x, *weights)


def second_body(chip_ref, core_ref, own_act, peer_act, *refs):
    weights, (far_low, far_high) = refs[:-5], refs[-5:-3]
    (own_out, peer_out), act = refs[-3:-1], refs[-1]
    count, cols, tokens = own_act.shape
    mid = tokens // 2
    core = core_ref[0]
    for c in range(count):
        mine = pl.ds(pl.multiple_of((2 * c + core) * cols, cols), cols)
        act[mine, :] = own_act[c]
        other = pl.ds(pl.multiple_of((2 * c + 1 - core) * cols, cols), cols)
        act[other, :mid] = peer_act[c, :, mid:]
        act[other, mid:] = peer_act[c, :, :mid]
    width = weights[0].shape[1]
    half = cols // 2
    low = jnp.concatenate([weight[:half] for weight in weights] + [far_low[...]], axis=0)
    parts = jnp.dot(low, act[:width], preferred_element_type=F32)
    high = jnp.concatenate([weight[half:] for weight in weights] + [far_high[...]], axis=0)
    parts += jnp.dot(high, act[width:], preferred_element_type=F32)
    for k in range(count):
        place = place_of(chip_ref[0], k)
        own_out[place] = parts[k * half : (k + 1) * half, :mid]
        peer_out[place] = parts[k * half : (k + 1) * half, mid:]


def mlp_second(chip, core, own_act, peer_act, weights, far):
    count, cols, tokens = own_act.shape
    shape = (count, cols // 2, tokens // 2)
    return pl.pallas_call(
        second_body,
        out_shape=(pltpu.HBM(shape, F32), jax.ShapeDtypeStruct(shape, F32)),
        grid=(1,),
        in_specs=[pl.BlockSpec(memory_space=pltpu.SMEM)] * 2
        + [whole(own_act), whole(peer_act)]
        + [half_of(x, cols, 1) for x in weights]
        + [whole(x) for x in far],
        out_specs=(pl.BlockSpec(shape, lambda i: (0, 0, 0)),) * 2,
        scratch_shapes=[pltpu.VMEM((2 * count * cols, tokens), BF16)],
        compiler_params=pltpu.CompilerParams(vmem_limit_bytes=28 << 20),
        cost_estimate=pl.CostEstimate(flops=1000, bytes_accessed=1000, transcendentals=0),
        name="mlp_second",
    )(chip, core, own_act, peer_act, *weights, *far)


def last_body(
    core_ref, live_ref, gap_ref, own_part, peer_part, updated, mods, finals, final_t, latent,
    velocity, next_latent, scaled, top, bottom, mlp_t,
):
    count, half, _ = own_part.shape
    for source, parity in ((own_part, core_ref[0]), (peer_part, 1 - core_ref[0])):
        for c in range(count):
            start = pl.multiple_of((2 * c + parity) * half, half)
            mlp_t[pl.ds(start, half), :] = source[c]
    refined = updated[...] + mods[5:6] * mlp_t[...].T
    final_in = layer_norm(refined, finals[0:1], finals[1:2])
    predicted = lax.dot_general(
        final_in, final_t[...], (((1,), (1,)), ((), ())), preferred_element_type=F32
    )
    live = jnp.full(predicted.shape, live_ref[0], jnp.int32) != 0
    moved = latent[...] + gap_ref[0] * predicted
    inner = (moved / vae_scale + vae_offset).astype(F32)
    velocity[...] = jnp.where(live, predicted, 0.0)
    next_latent[...] = jnp.where(live, moved, 0.0)
    inner = jnp.where(live, inner, 0.0).astype(BF16)
    scaled[...] = inner
    lanes = inner.shape[1] // 2
    top[...] = inner[:W_P, :lanes]
    bottom[...] = inner[inner.shape[0] - W_P :, lanes:]


def last(core, live, gap, own_part, peer_part, updated, mods, finals, final_t, latent):
    rows, width = updated.shape
    cols = final_t.shape[0]
    smem = pl.BlockSpec(memory_space=pltpu.SMEM)
    updated, final_t, own_part = (
        pltpu.with_memory_space_constraint(x, pltpu.HBM) for x in (updated, final_t, own_part)
    )
    inputs = (own_part, peer_part, updated, mods, finals, final_t, latent)
    shapes = ((rows, cols), (rows, cols), (rows, cols), (W_P, cols // 2), (W_P, cols // 2))
    return pl.pallas_call(
        last_body,
        out_shape=(
            jax.ShapeDtypeStruct((rows, cols), F32),
            jax.ShapeDtypeStruct((rows, cols), F32),
            jax.ShapeDtypeStruct((rows, cols), BF16),
            jax.ShapeDtypeStruct((W_P, cols // 2), BF16),
            jax.ShapeDtypeStruct((W_P, cols // 2), BF16),
        ),
        grid=(1,),
        in_specs=[smem] * 3 + [whole(x) for x in inputs],
        out_specs=tuple(pl.BlockSpec(x, lambda i: (0, 0)) for x in shapes),
        scratch_shapes=[pltpu.VMEM((width, rows), F32)],
        compiler_params=pltpu.CompilerParams(vmem_limit_bytes=12 << 20),
        cost_estimate=pl.CostEstimate(flops=1000, bytes_accessed=1000, transcendentals=0),
        name="last",
    )(core, live, gap, *inputs)


def conv_body(live_ref, scaled, before, after, weights, bias, out):
    lanes = before.shape[1]
    lines = [before[...]]
    for r in range(scaled.shape[0] // W_P):
        rows = scaled[r * W_P : (r + 1) * W_P]
        lines += [rows[:, :lanes], rows[:, lanes:]]
    lines.append(after[...])
    grid = jnp.concatenate([line.astype(F32) for line in lines], axis=1).astype(BF16)
    pixels = 2 * W_P
    pixel = lax.broadcasted_iota(jnp.int32, (pixels, W_P), 0)
    patch = lax.broadcasted_iota(jnp.int32, (pixels, W_P), 1)
    half, odd = pixel // 2, pixel % 2
    shifted = []
    for parity, offset in ((0, -1), (0, 0), (1, 0), (1, 1)):
        pick = jnp.logical_and(odd == parity, patch == half + offset)
        pick = jnp.where(pick, 1.0, 0.0).astype(BF16)
        shifted.append(jnp.dot(pick, grid, preferred_element_type=F32).astype(BF16))
    live = live_ref[0] != 0
    for line in range(out.shape[0]):
        total = jnp.zeros((pixels, out.shape[2]), F32)
        for k in range(4):
            window = shifted[k][:, line * lanes : (line + 3) * lanes]
            total += jnp.dot(window, weights[k], preferred_element_type=F32)
        total = jnp.where(live, total + bias[...], 0.0)
        out[line] = total.astype(BF16)


def convolve(live, scaled, before, after, weights, bias):
    lines = 2 * scaled.shape[0] // W_P
    shape = (lines, 2 * W_P, weights.shape[2])
    inputs = (scaled, before, after, weights, bias)
    return pl.pallas_call(
        conv_body,
        out_shape=jax.ShapeDtypeStruct(shape, BF16),
        grid=(1,),
        in_specs=[pl.BlockSpec(memory_space=pltpu.SMEM)] + [whole(x) for x in inputs],
        out_specs=pl.BlockSpec(shape, lambda i: (0, 0, 0)),
        compiler_params=pltpu.CompilerParams(vmem_limit_bytes=12 << 20),
        cost_estimate=pl.CostEstimate(flops=1000, bytes_accessed=1000, transcendentals=0),
        name="convolve",
    )(live, *inputs)


def conv_weights(conv_weight):
    taps = conv_weight.reshape(3, 3, CH, -1)
    none = jnp.zeros_like(taps[:, 0])
    pairs = ((none, taps[:, 0]), (taps[:, 1], taps[:, 2]), (taps[:, 0], taps[:, 1]), (taps[:, 2], none))
    return jnp.stack([jnp.stack(pair, axis=1).reshape(6 * CH, -1) for pair in pairs])


def per_device(
    hidden,
    text_hidden,
    latent,
    image_mod,
    text_mod,
    final_mod,
    counts,
    step_index,
    qkv_weight,
    text_weight,
    out_weight,
    mlp_in_weight,
    mlp_out_weight,
    final_weight,
    conv_weight,
    conv_bias,
):
    tok_rows, width = hidden.shape[1:]
    width_attn = HEADS * HEAD
    blocks = lax.axis_size("blk")
    blk, img = lax.axis_index("blk"), lax.axis_index("img")
    chip, core = img // 2, img % 2
    mods = image_mod[0]
    chip, core = chip[None], core[None]

    qkv_t = qkv_weight.T
    mlp_mine = jnp.concatenate(
        [mlp_in_weight.T, mlp_out_weight[:width].T, mlp_out_weight[width:].T], axis=0
    )
    gain, qkv_side = lax.optimization_barrier((1.0 + mods[1], qkv_t))
    image_in = modulate(hidden[0], mods[0], gain)
    mlp_mine, image_in = lax.optimization_barrier((mlp_mine, image_in))
    qkv_near = ring_first(qkv_t, qkv_side)
    qkv_next = ring_second(*qkv_near)
    far = jnp.concatenate(qkv_next[:2], axis=0)
    side_left, side_right, mlp_mine = lax.optimization_barrier((*qkv_next[2:], mlp_mine))
    qkv_far = far, swap(far, "img", 2)
    qkv_pieces = [qkv_t, *qkv_near, qkv_far[0], *qkv_next[2:], qkv_far[1]]
    mlp_near = ring_first(mlp_mine, mlp_mine)

    peer_in = swap(image_in, "img", 1)
    ready, peer_in = lax.optimization_barrier((marker(qkv_far[1]), peer_in))
    mine, theirs = project_qkv(chip, ready, image_in, peer_in, qkv_pieces)
    other = swap(theirs, "img", 1)
    heads = place_heads(core, mine, other, blocks)
    head = jnp.minimum(blk, HEADS - 1)
    right, head = lax.optimization_barrier((mlp_near[1], head))
    mlp_near = (mlp_near[0], right, mlp_near[2])
    parts = lax.all_to_all(heads, "blk", 0, 0, tiled=True)
    text_rows = tok_rows * pl.cdiv(text_hidden.shape[1], tok_rows)
    text_kv = text_keys(head[None], text_hidden[0], text_mod[0], text_weight, text_rows)

    mlp_next = ring_second(*mlp_near)
    mark = marker(*mlp_near)
    parts, mark, text_kv = lax.optimization_barrier((parts, mark, text_kv))
    mixed = attend(counts, parts, text_kv, mark)
    mixed, low, high = lax.optimization_barrier((mixed, mlp_next[0], mlp_next[1]))
    peer_low = swap(low, "img", 2)
    quarter = mlp_next[2].shape[0] // 4
    far = (
        ring(mlp_next[2][2 * quarter : 3 * quarter], "img", 4),
        ring(mlp_next[3][3 * quarter :], "img", -4),
    )
    mixed = lax.all_to_all(mixed, "blk", 0, 0, tiled=True)[:HEADS].reshape(width_attn, tok_rows)
    near_pieces, next_pieces = [mlp_mine, *mlp_near], list(mlp_next[2:])

    latent_p = latent[0].reshape(-1, 2, W_P, 2 * CH).transpose(0, 2, 1, 3)
    latent_p = latent_p.reshape(tok_rows, 4 * CH)
    conv_w = conv_weights(conv_weight)
    live = (blk * tok_rows < counts).astype(jnp.int32)
    step_value = step_index.astype(F32)
    gap = plan(step_value + 1.0) - plan(step_value)
    mixed, latent_p, conv_w = lax.optimization_barrier((mixed, latent_p, conv_w))
    updated, mlp_in = middle(mixed, hidden[0], mods, out_weight, marker(peer_low, *next_pieces, *far))
    mlp_cols = mlp_in_weight.shape[1]
    peer_mlp = swap(mlp_in, "img", 1)
    first_pieces = near_pieces + [low] + next_pieces + [peer_low]
    act = mlp_first(chip, mlp_in, peer_mlp, first_pieces, mlp_cols)
    peer_act = swap(act, "img", 1)
    own_part, sent_part = mlp_second(
        chip, core, act, peer_act, near_pieces + [high] + next_pieces, far
    )
    peer_part = swap(sent_part, "img", 1)
    velocity, next_lat, scaled, top, bottom = last(
        core, live, gap, own_part, peer_part, updated, mods, final_mod[0], final_weight.T, latent_p
    )
    size = blocks
    before = lax.ppermute(bottom, "blk", [(i, i + 1) for i in range(size - 1)])
    after = lax.ppermute(top, "blk", [(i + 1, i) for i in range(size - 1)])
    feature = convolve(live, scaled, before, after, conv_w, conv_bias[None])

    def by_rows(x):
        return x.reshape(-1, W_P, 2, 2 * CH).transpose(0, 2, 1, 3).reshape(latent[0].shape)

    return (by_rows(velocity)[None], by_rows(next_lat)[None], feature[None])


def solution(mesh):
    placed = (
        P("img", "blk", None),
        P("img", None, None),
        P("img", "blk", None),
        P("img", None, None),
        P("img", None, None),
        P("img", None, None),
        P("img"),
        P("img"),
        P(None, "img"),
        P(),
        P(),
        P(None, "img"),
        P(None, "img"),
        P(),
        P(),
        P(),
    )
    return jax.shard_map(
        per_device,
        mesh=mesh,
        in_specs=placed,
        out_specs=(P("img", "blk", None), P("img", "blk", None), P("img", "blk", None, None)),
        check_vma=False,
    )
```

```python
import jax
import jax.numpy as jnp
from jax import lax
from jax.experimental import pallas as pl
from jax.experimental.pallas import tpu as pltpu
from jax.sharding import PartitionSpec as P

HEAD = 64
CH = 16
HEADS = 12
W_P = 64
STEPS = 8

norm_eps = 1e-06
sigma_shift = 3.0
vae_scale = 1.5305
vae_offset = 0.0609
masked_score = -1e30

F32 = jnp.float32
BF16 = jnp.bfloat16


def modulate(inputs, shift_row, gain_row):
    values = inputs.astype(F32)
    center = jnp.mean(values, axis=-1, keepdims=True)
    spread = jnp.mean(jnp.square(values - center), axis=-1, keepdims=True)
    normed = (values - center) * lax.rsqrt(spread + norm_eps)
    return (normed * gain_row + shift_row).astype(BF16)


def plan(step_value):
    remain = 1.0 - step_value / STEPS
    return sigma_shift * remain / (1.0 + (sigma_shift - 1.0) * remain)


def swap(x, axis, bits):
    return lax.ppermute(x, axis, [(i, i ^ bits) for i in range(lax.axis_size(axis))])


def vmem_specs(count):
    return [pl.BlockSpec(memory_space=pltpu.VMEM)] * count


def whole(x):
    return pl.BlockSpec(x.shape, lambda i: (0,) * x.ndim)


OFFSETS = ((0, 0), (-1, 0), (1, 0), (0, 1), (2, 0), (-1, 1), (1, 1), (2, 1))


def ring(x, axis, step):
    size = lax.axis_size(axis)
    return lax.ppermute(x, axis, [(i, (i + step) % size) for i in range(size)])


def ring_first(x, side):
    return ring(x, "img", 4), ring(x, "img", -4), swap(side, "img", 2)


def ring_second(left, right, across):
    half = left.shape[0] // 2
    return (
        ring(left[:half], "img", 4),
        ring(right[half:], "img", -4),
        ring(across, "img", 4),
        ring(across, "img", -4),
    )


def place_of(chip, k):
    dx, dy = OFFSETS[k]
    column = jnp.bitwise_and(chip // 2 + dx + 4, 3)
    return 2 * column + jnp.bitwise_xor(jnp.bitwise_and(chip, 1), dy)


def qkv_body(chip_ref, ready, own_x, peer_x, *refs):
    weights, (own_out, peer_out) = refs[:-2], refs[-2:]
    rows = own_x.shape[0]
    both = jnp.concatenate([own_x[...], peer_x[...]], axis=0)
    cols = own_out.shape[1]
    stacked = jnp.concatenate([weight[...] for weight in weights], axis=0)
    parts = lax.dot_general(
        stacked, both, (((1,), (1,)), ((), ())), preferred_element_type=F32
    ).astype(BF16)
    for k in range(len(weights)):
        place = place_of(chip_ref[0], k)
        own_out[place] = parts[k * cols : (k + 1) * cols, :rows]
        peer_out[place] = parts[k * cols : (k + 1) * cols, rows:]


def project_qkv(chip, ready, own_x, peer_x, weights):
    cols, rows = weights[0].shape[0], own_x.shape[0]
    shape = (len(weights), cols, rows)
    inputs = (ready, own_x, peer_x, *weights)
    return pl.pallas_call(
        qkv_body,
        out_shape=(pltpu.HBM(shape, BF16), jax.ShapeDtypeStruct(shape, BF16)),
        grid=(1,),
        in_specs=[pl.BlockSpec(memory_space=pltpu.SMEM)] + [whole(x) for x in inputs],
        out_specs=(pl.BlockSpec(shape, lambda i: (0, 0, 0)),) * 2,
        compiler_params=pltpu.CompilerParams(vmem_limit_bytes=20 << 20),
        cost_estimate=pl.CostEstimate(flops=1000, bytes_accessed=1000, transcendentals=0),
        name="project_qkv",
    )(chip, *inputs)


def heads_body(core_ref, mine, other, out):
    count, cols, _ = mine.shape
    step = 16
    per_shard, per_head = cols // step, HEAD // step
    section = HEADS * per_head

    def copy(sources):
        for c in range(count):
            for parity, source in enumerate(sources):
                for j in range(per_shard):
                    piece = (2 * c + parity) * per_shard + j
                    kind, rest = piece // section, piece % section
                    start = kind * HEAD + rest % per_head * step
                    rows = source[c, j * step : (j + 1) * step]
                    out[rest // per_head, start : start + step] = rows

    @pl.when(core_ref[0] == 0)
    def _():
        copy((mine, other))

    @pl.when(core_ref[0] != 0)
    def _():
        copy((other, mine))

    out[HEADS:] = jnp.zeros((out.shape[0] - HEADS,) + out.shape[1:], BF16)


def place_heads(core, mine, other, blocks):
    shape = (blocks, 3 * HEAD, mine.shape[2])
    mine = pltpu.with_memory_space_constraint(mine, pltpu.HBM)
    return pl.pallas_call(
        heads_body,
        out_shape=pltpu.HBM(shape, BF16),
        grid=(1,),
        in_specs=[pl.BlockSpec(memory_space=pltpu.SMEM), whole(mine), whole(other)],
        out_specs=pl.BlockSpec(shape, lambda i: (0, 0, 0)),
        compiler_params=pltpu.CompilerParams(vmem_limit_bytes=6 << 20),
        cost_estimate=pl.CostEstimate(flops=1000, bytes_accessed=1000, transcendentals=0),
        name="place_heads",
    )(core, mine, other)


def text_body(head_ref, hidden, mods, key_w, value_w, out, turned):
    odd = head_ref[0] % 2 != 0
    rows = hidden.shape[0]
    states = layer_norm(hidden[...].astype(F32), mods[0:1], mods[1:2])
    turned[...] = jnp.zeros_like(turned)
    for part, weight in enumerate((key_w, value_w)):
        turned[:rows, :] = jnp.dot(states, weight[...], preferred_element_type=F32)
        both = turned[...].T
        chosen = jnp.where(odd, both[HEAD:], both[:HEAD])
        out[part * HEAD : (part + 1) * HEAD, :] = chosen.astype(BF16)


def text_keys(head, hidden, mods, weight, rows):
    width = hidden.shape[1]
    pair = 2 * HEAD
    values_at = HEADS * HEAD // pair
    return pl.pallas_call(
        text_body,
        out_shape=jax.ShapeDtypeStruct((pair, rows), BF16),
        grid_spec=pltpu.PrefetchScalarGridSpec(
            num_scalar_prefetch=1,
            grid=(1,),
            in_specs=[
                pl.BlockSpec(hidden.shape, lambda i, h: (0, 0)),
                pl.BlockSpec(mods.shape, lambda i, h: (0, 0)),
                pl.BlockSpec((width, pair), lambda i, h: (0, h[0] // 2)),
                pl.BlockSpec((width, pair), lambda i, h: (0, values_at + h[0] // 2)),
            ],
            out_specs=pl.BlockSpec((pair, rows), lambda i, h: (0, 0)),
            scratch_shapes=[pltpu.VMEM((rows, pair), F32)],
        ),
        compiler_params=pltpu.CompilerParams(vmem_limit_bytes=10 << 20),
        cost_estimate=pl.CostEstimate(flops=1000, bytes_accessed=1000, transcendentals=0),
        name="text_keys",
    )(head, hidden, mods, weight, weight)


def mark_body(*refs):
    refs[-1][...] = refs[0][...]


def marker(*arrays):
    return pl.pallas_call(
        mark_body,
        out_shape=jax.ShapeDtypeStruct((16, 128), BF16),
        grid=(1,),
        in_specs=[pl.BlockSpec((16, 128), lambda i: (0, 0))] * len(arrays),
        out_specs=pl.BlockSpec((16, 128), lambda i: (0, 0)),
        compiler_params=pltpu.CompilerParams(vmem_limit_bytes=1 << 20),
        cost_estimate=pl.CostEstimate(
            flops=100_000_000_000, bytes_accessed=100_000_000, transcendentals=0
        ),
        name="marker",
    )(*arrays)


def attend_body(count_ref, parts, text, mark, out, keys, values, queries):
    blocks, _, rows = parts.shape
    text_blocks = text.shape[1] // rows
    text_len = 154
    tile = 2 * rows
    lane = lax.broadcasted_iota(jnp.int32, (HEAD, rows), 1)
    row = lax.broadcasted_iota(jnp.int32, (HEAD, rows), 0)
    top = row == 0
    zeros = jnp.zeros((HEAD, rows), F32)
    ones = jnp.where(top, 1.0, 0.0).astype(F32)

    def place(index, key_part, value_part, limit):
        cols = slice(index * rows, (index + 1) * rows)
        keys[:HEAD, cols] = key_part
        bias = jnp.where(jnp.logical_and(top, lane >= limit), masked_score, 0.0)
        keys[HEAD:, cols] = bias.astype(BF16)
        full = jnp.concatenate([value_part.astype(F32), zeros], axis=0)
        values[cols, :] = full.T.astype(BF16)

    for b in range(blocks):
        part = parts[b]
        place(b, part[HEAD : 2 * HEAD], part[2 * HEAD :], count_ref[0] - b * rows)
        scaled = part[:HEAD].astype(F32) * 0.125
        full = jnp.concatenate([scaled, ones], axis=0)
        queries[b * rows : (b + 1) * rows, :] = full.T.astype(BF16)
    for t in range(text_blocks):
        cols = slice(t * rows, (t + 1) * rows)
        place(blocks + t, text[:HEAD, cols], text[HEAD:, cols], text_len - t * rows)

    def step(t, carry):
        first = pl.multiple_of(t * tile, tile)
        scores = jnp.dot(queries[pl.ds(first, tile), :], keys[...], preferred_element_type=F32)
        top_score = jnp.max(scores, axis=1, keepdims=True)
        numer = jnp.exp(scores - top_score)
        total = jnp.sum(numer, axis=1, keepdims=True)
        mixed = jnp.dot(numer.astype(BF16), values[...], preferred_element_type=F32) / total
        turned = mixed.T[:HEAD].astype(BF16)
        out[2 * t] = turned[:, :rows]
        out[2 * t + 1] = turned[:, rows:]
        return carry

    lax.fori_loop(0, blocks // 2, step, 0, unroll=2)


def attend(count, parts, text, mark):
    blocks, _, rows = parts.shape
    keys = blocks * rows + text.shape[1]
    queries = blocks * rows
    return pl.pallas_call(
        attend_body,
        out_shape=jax.ShapeDtypeStruct((blocks, HEAD, rows), BF16),
        in_specs=[pl.BlockSpec(memory_space=pltpu.SMEM)] + vmem_specs(3),
        out_specs=vmem_specs(1)[0],
        scratch_shapes=[
            pltpu.VMEM((2 * HEAD, keys), BF16),
            pltpu.VMEM((keys, 2 * HEAD), BF16),
            pltpu.VMEM((queries, 2 * HEAD), BF16),
        ],
        compiler_params=pltpu.CompilerParams(vmem_limit_bytes=20 << 20),
        cost_estimate=pl.CostEstimate(flops=1000, bytes_accessed=1000, transcendentals=0),
        name="attend",
    )(count, parts, text, mark)


def layer_norm(values, shift_row, scale_row):
    center = jnp.mean(values, axis=-1, keepdims=True)
    spread = jnp.mean(jnp.square(values - center), axis=-1, keepdims=True)
    normed = (values - center) * lax.rsqrt(spread + norm_eps)
    return (normed * (1.0 + scale_row) + shift_row).astype(BF16)


def gelu(v):
    return 0.5 * v * (1.0 + jnp.tanh(0.7978845608028654 * (v + 0.044715 * v * v * v)))


def middle_body(mixed, hidden, mods, out_w, mark, updated, mlp_in):
    attended = mixed[...].astype(F32).T.astype(BF16)
    projected = jnp.dot(attended, out_w[...], preferred_element_type=F32)
    now = hidden[...].astype(F32) + mods[2:3] * projected
    updated[...] = now
    mlp_in[...] = layer_norm(now, mods[3:4], mods[4:5])


def middle(mixed, hidden, mods, out_w, mark):
    rows, width = hidden.shape
    inputs = (mixed, hidden, mods, out_w, mark)
    return pl.pallas_call(
        middle_body,
        out_shape=(
            pltpu.HBM((rows, width), F32),
            jax.ShapeDtypeStruct((rows, width), BF16),
        ),
        grid=(1,),
        in_specs=[whole(x) for x in inputs],
        out_specs=(pl.BlockSpec((rows, width), lambda i: (0, 0)),) * 2,
        compiler_params=pltpu.CompilerParams(vmem_limit_bytes=14 << 20),
        cost_estimate=pl.CostEstimate(flops=1000, bytes_accessed=1000, transcendentals=0),
        name="middle",
    )(*inputs)


def first_body(chip_ref, own_x, peer_x, *refs):
    weights, out = refs[:-1], refs[-1]
    both = jnp.concatenate([own_x[...], peer_x[...]], axis=0)
    cols = out.shape[1]
    stacked = jnp.concatenate([weight[...] for weight in weights], axis=0)
    parts = lax.dot_general(stacked, both, (((1,), (1,)), ((), ())), preferred_element_type=F32)
    for k in range(len(weights)):
        out[place_of(chip_ref[0], k)] = gelu(parts[k * cols : (k + 1) * cols]).astype(BF16)


def half_of(x, cols, index):
    position = index if x.shape[0] > cols else 0
    return pl.BlockSpec((cols, x.shape[1]), lambda i: (position, 0))


def mlp_first(chip, own_x, peer_x, weights, cols):
    rows = own_x.shape[0]
    count = len(weights)
    shape = (count, cols, 2 * rows)
    return pl.pallas_call(
        first_body,
        out_shape=jax.ShapeDtypeStruct(shape, BF16),
        grid=(1,),
        in_specs=[pl.BlockSpec(memory_space=pltpu.SMEM), whole(own_x), whole(peer_x)]
        + [half_of(x, cols, 0) for x in weights],
        out_specs=pl.BlockSpec(shape, lambda i: (0, 0, 0)),
        compiler_params=pltpu.CompilerParams(vmem_limit_bytes=28 << 20),
        cost_estimate=pl.CostEstimate(flops=1000, bytes_accessed=1000, transcendentals=0),
        name="mlp_first",
    )(chip, own_x, peer_x, *weights)


def second_body(chip_ref, core_ref, own_act, peer_act, *refs):
    weights, (far_low, far_high) = refs[:-5], refs[-5:-3]
    (own_out, peer_out), act = refs[-3:-1], refs[-1]
    count, cols, tokens = own_act.shape
    mid = tokens // 2
    core = core_ref[0]
    for c in range(count):
        mine = pl.ds(pl.multiple_of((2 * c + core) * cols, cols), cols)
        act[mine, :] = own_act[c]
        other = pl.ds(pl.multiple_of((2 * c + 1 - core) * cols, cols), cols)
        act[other, :mid] = peer_act[c, :, mid:]
        act[other, mid:] = peer_act[c, :, :mid]
    width = weights[0].shape[1]
    half = cols // 2
    low = jnp.concatenate([weight[:half] for weight in weights] + [far_low[...]], axis=0)
    parts = jnp.dot(low, act[:width], preferred_element_type=F32)
    high = jnp.concatenate([weight[half:] for weight in weights] + [far_high[...]], axis=0)
    parts += jnp.dot(high, act[width:], preferred_element_type=F32)
    for k in range(count):
        place = place_of(chip_ref[0], k)
        own_out[place] = parts[k * half : (k + 1) * half, :mid]
        peer_out[place] = parts[k * half : (k + 1) * half, mid:]


def mlp_second(chip, core, own_act, peer_act, weights, far):
    count, cols, tokens = own_act.shape
    shape = (count, cols // 2, tokens // 2)
    return pl.pallas_call(
        second_body,
        out_shape=(pltpu.HBM(shape, F32), jax.ShapeDtypeStruct(shape, F32)),
        grid=(1,),
        in_specs=[pl.BlockSpec(memory_space=pltpu.SMEM)] * 2
        + [whole(own_act), whole(peer_act)]
        + [half_of(x, cols, 1) for x in weights]
        + [whole(x) for x in far],
        out_specs=(pl.BlockSpec(shape, lambda i: (0, 0, 0)),) * 2,
        scratch_shapes=[pltpu.VMEM((2 * count * cols, tokens), BF16)],
        compiler_params=pltpu.CompilerParams(vmem_limit_bytes=28 << 20),
        cost_estimate=pl.CostEstimate(flops=1000, bytes_accessed=1000, transcendentals=0),
        name="mlp_second",
    )(chip, core, own_act, peer_act, *weights, *far)


def last_body(
    core_ref, live_ref, gap_ref, own_part, peer_part, updated, mods, finals, final_t, latent,
    velocity, next_latent, scaled, top, bottom, mlp_t,
):
    count, half, _ = own_part.shape
    for source, parity in ((own_part, core_ref[0]), (peer_part, 1 - core_ref[0])):
        for c in range(count):
            start = pl.multiple_of((2 * c + parity) * half, half)
            mlp_t[pl.ds(start, half), :] = source[c]
    refined = updated[...] + mods[5:6] * mlp_t[...].T
    final_in = layer_norm(refined, finals[0:1], finals[1:2])
    predicted = lax.dot_general(
        final_in, final_t[...], (((1,), (1,)), ((), ())), preferred_element_type=F32
    )
    live = jnp.full(predicted.shape, live_ref[0], jnp.int32) != 0
    moved = latent[...] + gap_ref[0] * predicted
    inner = (moved / vae_scale + vae_offset).astype(F32)
    velocity[...] = jnp.where(live, predicted, 0.0)
    next_latent[...] = jnp.where(live, moved, 0.0)
    inner = jnp.where(live, inner, 0.0).astype(BF16)
    scaled[...] = inner
    lanes = inner.shape[1] // 2
    top[...] = inner[:W_P, :lanes]
    bottom[...] = inner[inner.shape[0] - W_P :, lanes:]


def last(core, live, gap, own_part, peer_part, updated, mods, finals, final_t, latent):
    rows, width = updated.shape
    cols = final_t.shape[0]
    smem = pl.BlockSpec(memory_space=pltpu.SMEM)
    updated, final_t, own_part = (
        pltpu.with_memory_space_constraint(x, pltpu.HBM) for x in (updated, final_t, own_part)
    )
    inputs = (own_part, peer_part, updated, mods, finals, final_t, latent)
    shapes = ((rows, cols), (rows, cols), (rows, cols), (W_P, cols // 2), (W_P, cols // 2))
    return pl.pallas_call(
        last_body,
        out_shape=(
            jax.ShapeDtypeStruct((rows, cols), F32),
            jax.ShapeDtypeStruct((rows, cols), F32),
            jax.ShapeDtypeStruct((rows, cols), BF16),
            jax.ShapeDtypeStruct((W_P, cols // 2), BF16),
            jax.ShapeDtypeStruct((W_P, cols // 2), BF16),
        ),
        grid=(1,),
        in_specs=[smem] * 3 + [whole(x) for x in inputs],
        out_specs=tuple(pl.BlockSpec(x, lambda i: (0, 0)) for x in shapes),
        scratch_shapes=[pltpu.VMEM((width, rows), F32)],
        compiler_params=pltpu.CompilerParams(vmem_limit_bytes=12 << 20),
        cost_estimate=pl.CostEstimate(flops=1000, bytes_accessed=1000, transcendentals=0),
        name="last",
    )(core, live, gap, *inputs)


def conv_body(live_ref, scaled, before, after, weights, bias, out):
    lanes = before.shape[1]
    lines = [before[...]]
    for r in range(scaled.shape[0] // W_P):
        rows = scaled[r * W_P : (r + 1) * W_P]
        lines += [rows[:, :lanes], rows[:, lanes:]]
    lines.append(after[...])
    grid = jnp.concatenate([line.astype(F32) for line in lines], axis=1).astype(BF16)
    pixels = 2 * W_P
    pixel = lax.broadcasted_iota(jnp.int32, (pixels, W_P), 0)
    patch = lax.broadcasted_iota(jnp.int32, (pixels, W_P), 1)
    half, odd = pixel // 2, pixel % 2
    shifted = []
    for parity, offset in ((0, -1), (0, 0), (1, 0), (1, 1)):
        pick = jnp.logical_and(odd == parity, patch == half + offset)
        pick = jnp.where(pick, 1.0, 0.0).astype(BF16)
        shifted.append(jnp.dot(pick, grid, preferred_element_type=F32).astype(BF16))
    live = live_ref[0] != 0
    for line in range(out.shape[0]):
        total = jnp.zeros((pixels, out.shape[2]), F32)
        for k in range(4):
            window = shifted[k][:, line * lanes : (line + 3) * lanes]
            total += jnp.dot(window, weights[k], preferred_element_type=F32)
        total = jnp.where(live, total + bias[...], 0.0)
        out[line] = total.astype(BF16)


def convolve(live, scaled, before, after, weights, bias):
    lines = 2 * scaled.shape[0] // W_P
    shape = (lines, 2 * W_P, weights.shape[2])
    inputs = (scaled, before, after, weights, bias)
    return pl.pallas_call(
        conv_body,
        out_shape=jax.ShapeDtypeStruct(shape, BF16),
        grid=(1,),
        in_specs=[pl.BlockSpec(memory_space=pltpu.SMEM)] + [whole(x) for x in inputs],
        out_specs=pl.BlockSpec(shape, lambda i: (0, 0, 0)),
        compiler_params=pltpu.CompilerParams(vmem_limit_bytes=12 << 20),
        cost_estimate=pl.CostEstimate(flops=1000, bytes_accessed=1000, transcendentals=0),
        name="convolve",
    )(live, *inputs)


def conv_weights(conv_weight):
    taps = conv_weight.reshape(3, 3, CH, -1)
    none = jnp.zeros_like(taps[:, 0])
    pairs = ((none, taps[:, 0]), (taps[:, 1], taps[:, 2]), (taps[:, 0], taps[:, 1]), (taps[:, 2], none))
    return jnp.stack([jnp.stack(pair, axis=1).reshape(6 * CH, -1) for pair in pairs])


def per_device(
    hidden,
    text_hidden,
    latent,
    image_mod,
    text_mod,
    final_mod,
    counts,
    step_index,
    qkv_weight,
    text_weight,
    out_weight,
    mlp_in_weight,
    mlp_out_weight,
    final_weight,
    conv_weight,
    conv_bias,
):
    tok_rows, width = hidden.shape[1:]
    width_attn = HEADS * HEAD
    blocks = lax.axis_size("blk")
    blk, img = lax.axis_index("blk"), lax.axis_index("img")
    chip, core = img // 2, img % 2
    mods = image_mod[0]
    chip, core = chip[None], core[None]

    qkv_t = qkv_weight.T
    mlp_mine = jnp.concatenate(
        [mlp_in_weight.T, mlp_out_weight[:width].T, mlp_out_weight[width:].T], axis=0
    )
    gain, qkv_side = lax.optimization_barrier((1.0 + mods[1], qkv_t))
    image_in = modulate(hidden[0], mods[0], gain)
    mlp_mine, image_in = lax.optimization_barrier((mlp_mine, image_in))
    qkv_near = ring_first(qkv_t, qkv_side)
    qkv_next = ring_second(*qkv_near)
    far = jnp.concatenate(qkv_next[:2], axis=0)
    side_left, side_right, mlp_mine = lax.optimization_barrier((*qkv_next[2:], mlp_mine))
    qkv_far = far, swap(far, "img", 2)
    qkv_pieces = [qkv_t, *qkv_near, qkv_far[0], *qkv_next[2:], qkv_far[1]]
    mlp_near = ring_first(mlp_mine, mlp_mine)

    peer_in = swap(image_in, "img", 1)
    ready, peer_in = lax.optimization_barrier((marker(qkv_far[1]), peer_in))
    mine, theirs = project_qkv(chip, ready, image_in, peer_in, qkv_pieces)
    other = swap(theirs, "img", 1)
    heads = place_heads(core, mine, other, blocks)
    head = jnp.minimum(blk, HEADS - 1)
    right, head = lax.optimization_barrier((mlp_near[1], head))
    mlp_near = (mlp_near[0], right, mlp_near[2])
    parts = lax.all_to_all(heads, "blk", 0, 0, tiled=True)
    text_rows = tok_rows * pl.cdiv(text_hidden.shape[1], tok_rows)
    text_kv = text_keys(head[None], text_hidden[0], text_mod[0], text_weight, text_rows)

    mlp_next = ring_second(*mlp_near)
    mark = marker(*mlp_near)
    parts, mark, text_kv = lax.optimization_barrier((parts, mark, text_kv))
    mixed = attend(counts, parts, text_kv, mark)
    mixed, low, high = lax.optimization_barrier((mixed, mlp_next[0], mlp_next[1]))
    peer_low = swap(low, "img", 2)
    quarter = mlp_next[2].shape[0] // 4
    far = (
        ring(mlp_next[2][2 * quarter : 3 * quarter], "img", 4),
        ring(mlp_next[3][3 * quarter :], "img", -4),
    )
    mixed = lax.all_to_all(mixed, "blk", 0, 0, tiled=True)[:HEADS].reshape(width_attn, tok_rows)
    near_pieces, next_pieces = [mlp_mine, *mlp_near], list(mlp_next[2:])

    latent_p = latent[0].reshape(-1, 2, W_P, 2 * CH).transpose(0, 2, 1, 3)
    latent_p = latent_p.reshape(tok_rows, 4 * CH)
    conv_w = conv_weights(conv_weight)
    live = (blk * tok_rows < counts).astype(jnp.int32)
    step_value = step_index.astype(F32)
    gap = plan(step_value + 1.0) - plan(step_value)
    mixed, latent_p, conv_w = lax.optimization_barrier((mixed, latent_p, conv_w))
    updated, mlp_in = middle(mixed, hidden[0], mods, out_weight, marker(peer_low, *next_pieces, *far))
    mlp_cols = mlp_in_weight.shape[1]
    peer_mlp = swap(mlp_in, "img", 1)
    first_pieces = near_pieces + [low] + next_pieces + [peer_low]
    act = mlp_first(chip, mlp_in, peer_mlp, first_pieces, mlp_cols)
    peer_act = swap(act, "img", 1)
    own_part, sent_part = mlp_second(
        chip, core, act, peer_act, near_pieces + [high] + next_pieces, far
    )
    peer_part = swap(sent_part, "img", 1)
    velocity, next_lat, scaled, top, bottom = last(
        core, live, gap, own_part, peer_part, updated, mods, final_mod[0], final_weight.T, latent_p
    )
    size = blocks
    before = lax.ppermute(bottom, "blk", [(i, i + 1) for i in range(size - 1)])
    after = lax.ppermute(top, "blk", [(i + 1, i) for i in range(size - 1)])
    feature = convolve(live, scaled, before, after, conv_w, conv_bias[None])

    def by_rows(x):
        return x.reshape(-1, W_P, 2, 2 * CH).transpose(0, 2, 1, 3).reshape(latent[0].shape)

    return (by_rows(velocity)[None], by_rows(next_lat)[None], feature[None])


def solution(mesh):
    placed = (
        P("img", "blk", None),
        P("img", None, None),
        P("img", "blk", None),
        P("img", None, None),
        P("img", None, None),
        P("img", None, None),
        P("img"),
        P("img"),
        P(None, "img"),
        P(),
        P(),
        P(None, "img"),
        P(None, "img"),
        P(),
        P(),
        P(),
    )
    return jax.shard_map(
        per_device,
        mesh=mesh,
        in_specs=placed,
        out_specs=(P("img", "blk", None), P("img", "blk", None), P("img", "blk", None, None)),
        check_vma=False,
    )
```
